32 devices in a mesh: term: 8 (over z, core), doc: 4 (over y, x).
Axes of the slice: x: 2, y: 2, z: 4, core: 2. Of those that a mesh axis runs over, the one named last changes fastest.
Arguments:
- tile_values: bfloat16 [384, 512, 128], P('term', 'doc'), may hold values from 0.001 to 1, as said below
- tile_rows: int32 [8, 192], P('term', 'doc'), may hold values from 0 to 15, as said below
- tile_cols: int32 [8, 192], P('term', 'doc'), may hold values from 0 to 15, as said below
- tile_count: int32 [8, 4], P('term', 'doc'), may hold values from 16 to 48, as said below
- start_block: bfloat16 [8192, 256], P('doc'), may hold values from -6 to 6
Outputs:
- row_scale: float32 [16384], P('term')
- col_scale: float32 [8192], P('doc')
- left_basis: bfloat16 [16384, 256], P('term')
- right_basis: bfloat16 [8192, 256], P('doc')
The draws below stay inside these ranges and needn't reach their ends.
Inputs may be any that keep to these rules, and one draw needn't show every extreme that they name: `tile_values`: entries are positive. `tile_rows`: within one block pair the occupied (row, column) pairs are distinct, and every tile row and tile column of every block pair holds an occupied tile. `tile_cols`: paired with tile_rows slot by slot. `tile_count`: some block pair has all 48 slots occupied.
All inputs are finite; a program needn't handle non-finite values.
Results may differ from the reference program's by a relative error of at most 0.006.
The reference program's roundings to bfloat16 on the way count: a program that leaves them out, or rounds other values in their place, can miss the bound.
Values may be sent and summed in bfloat16 or wider, within the bound.
A program may use at most 64 MiB of HBM per device.

```python
import jax
import jax.numpy as jnp
from jax import lax

TILE = 128
K = 256
PASSES = 2
RB = 16
CB = 16
CAP = 48
DOCS = 8192
N_TERM = 8
N_DOC = 4


def draw_tile_values(key, part):
    base = jax.random.fold_in(key, 41)
    entries = jax.random.uniform(base, (N_TERM, CAP, N_DOC, TILE, TILE), jnp.float32, 0.05, 1.0)
    level = jax.random.uniform(jax.random.fold_in(base, 3), (N_TERM, N_DOC), jnp.float32, jnp.log(0.03), 0.0)
    factor = jnp.exp(level)
    scaled = entries * factor[:, None, :, None, None]
    return scaled.reshape(N_TERM * CAP, N_DOC * TILE, TILE).astype(jnp.bfloat16)


def tile_places(key):
    base = jax.random.fold_in(key, 17)
    positions = RB * CB
    scores = jax.random.randint(base, (N_TERM, N_DOC, positions), 0, 1 << 20, dtype=jnp.int32)
    cell = jnp.arange(positions, dtype=jnp.int32)
    row_of = cell // CB
    col_of = cell % CB
    forced = row_of == col_of % RB
    ranked = jnp.where(forced[None, None, :], col_of[None, None, :] - CB, scores * positions + cell[None, None, :])
    order = jnp.argsort(ranked, axis=-1, stable=True)[:, :, :CAP].astype(jnp.int32)
    return (order // CB, order % CB)


def draw_tile_rows(key, part):
    row_part, col_part = tile_places(key)
    return row_part.reshape(N_TERM, N_DOC * CAP)


def draw_tile_cols(key, part):
    row_part, col_part = tile_places(key)
    return col_part.reshape(N_TERM, N_DOC * CAP)


def draw_tile_count(key, part):
    base = jax.random.fold_in(key, 29)
    spread = CAP - CB
    level = jax.random.randint(base, (N_TERM * N_DOC,), 0, spread + 1, dtype=jnp.int32)
    filled = CB + level * level // spread * level // spread
    chosen = jax.random.randint(jax.random.fold_in(base, 1), (), 0, N_TERM * N_DOC, dtype=jnp.int32)
    filled = jnp.where(jnp.arange(N_TERM * N_DOC, dtype=jnp.int32) == chosen, CAP, filled)
    return filled.reshape(N_TERM, N_DOC).astype(jnp.int32)


def block_levels(stream_key, shape, pieces, least, top_value):
    factor_of, own = 1.0, jax.random.fold_in(stream_key, 6)
    for position, parts in pieces:
        draws = jnp.exp(jax.random.uniform(jax.random.fold_in(own, position), (parts,), jnp.float32, least / len(pieces), top_value / len(pieces)))
        factor_of = factor_of * jnp.repeat(draws, shape[position] // parts).reshape([-1 if axis == position else 1 for axis in range(len(shape))])
    return factor_of


def scatter_about(rng, extent, scale, bound, shards=(), kind=jnp.bfloat16):
    loudness = block_levels(rng, extent, shards, -0.22, 0.18) if shards else 1.0
    array = jax.random.normal(rng, extent, jnp.float32) * scale * loudness
    return jnp.minimum(jnp.maximum(array, -bound), bound).astype(kind)


def setup_inputs(seed: int = 0) -> dict:
    arg_keys = jax.random.split(jax.random.key(seed), 6)
    tile_values = draw_tile_values(jax.random.fold_in(arg_keys[5], 71), 0)
    tile_rows = draw_tile_rows(jax.random.fold_in(arg_keys[5], 71), 0)
    tile_cols = draw_tile_cols(jax.random.fold_in(arg_keys[5], 71), 0)
    tile_count = draw_tile_count(jax.random.fold_in(arg_keys[5], 71), 0)
    start_block = scatter_about(arg_keys[4], (DOCS, K), 1.0, 6.0, ((0, 4),))
    return dict(tile_values=tile_values, tile_rows=tile_rows, tile_cols=tile_cols, tile_count=tile_count, start_block=start_block)


PRECISE = lax.Precision.HIGHEST

def factor_inverse(gram):
    lower = jnp.linalg.cholesky(gram)
    identity = jnp.eye(gram.shape[0], dtype=gram.dtype)
    return jax.scipy.linalg.solve_triangular(lower, identity, lower=True).T

def apply_matrix(values, row_ids, col_ids, counts, source, forward):
    width = source.shape[-1]
    if forward:
        out_blocks = RB
    else:
        out_blocks = CB

    def outer_block(outer):

        def inner_step(running, inner):
            if forward:
                term_at, doc_at = (outer, inner)
            else:
                term_at, doc_at = (inner, outer)
            tiles_here = values[term_at, :, doc_at].astype(jnp.float32)
            live_mask = (jnp.arange(CAP, dtype=jnp.int32) < counts[term_at, doc_at]).astype(jnp.float32)
            if forward:
                picked = source[doc_at][col_ids[term_at, doc_at]].astype(jnp.float32)
                product = jnp.einsum('sab,sbk->sak', tiles_here, picked, precision=PRECISE)
                target = row_ids[term_at, doc_at]
            else:
                picked = source[term_at][row_ids[term_at, doc_at]].astype(jnp.float32)
                product = jnp.einsum('sab,sak->sbk', tiles_here, picked, precision=PRECISE)
                target = col_ids[term_at, doc_at]
            product = product * live_mask[:, None, None]
            return (running + jax.ops.segment_sum(product, target, num_segments=out_blocks), None)
        initial = jnp.zeros((out_blocks, TILE, width), jnp.float32)
        inner_total = N_DOC if forward else N_TERM
        return lax.scan(inner_step, initial, jnp.arange(inner_total, dtype=jnp.int32))[0]
    outer_total = N_TERM if forward else N_DOC
    return lax.map(outer_block, jnp.arange(outer_total, dtype=jnp.int32))

def reference(tile_values, tile_rows, tile_cols, tile_count, start_block):
    values = tile_values.reshape(N_TERM, CAP, N_DOC, TILE, TILE)
    row_ids = tile_rows.reshape(N_TERM, N_DOC, CAP).astype(jnp.int32)
    col_ids = tile_cols.reshape(N_TERM, N_DOC, CAP).astype(jnp.int32)
    counts = tile_count.astype(jnp.int32)
    terms_total = N_TERM * RB * TILE
    docs_total = N_DOC * CB * TILE
    col_scale = jnp.ones((N_DOC, CB, TILE, 1), jnp.float32)
    row_scale = jnp.ones((N_TERM, RB, TILE, 1), jnp.float32)
    for sweep_index in range(PASSES):
        row_scale = 1.0 / apply_matrix(values, row_ids, col_ids, counts, col_scale, True)
        col_scale = 1.0 / apply_matrix(values, row_ids, col_ids, counts, row_scale, False)
    row_weight = row_scale * apply_matrix(values, row_ids, col_ids, counts, col_scale, True)
    row_flat = row_scale.reshape(-1, 1)
    col_flat = col_scale.reshape(-1, 1)
    weight_flat = row_weight.reshape(-1)
    start = start_block.astype(jnp.float32)
    start_mean = jnp.sum(start, axis=0)
    scaled_start = (col_flat * start).astype(jnp.bfloat16)
    left_raw = apply_matrix(values, row_ids, col_ids, counts, scaled_start.reshape(N_DOC, CB, TILE, K), True).reshape(-1, K)
    left_block = row_flat * left_raw - weight_flat[:, None] * start_mean[None, :] / docs_total
    left_inverse = factor_inverse(jnp.dot(left_block.T, left_block, precision=PRECISE) / terms_total)
    left_float = jnp.dot(left_block, left_inverse, precision=PRECISE)
    left_basis = left_float.astype(jnp.bfloat16)
    lean = jnp.dot(weight_flat, left_float, precision=PRECISE)
    scaled_left = (row_flat * left_basis.astype(jnp.float32)).astype(jnp.bfloat16)
    right_raw = apply_matrix(values, row_ids, col_ids, counts, scaled_left.reshape(N_TERM, RB, TILE, K), False).reshape(-1, K)
    right_block = col_flat * right_raw - lean[None, :] / docs_total
    right_inverse = factor_inverse(jnp.dot(right_block.T, right_block, precision=PRECISE) / docs_total)
    right_basis = jnp.dot(right_block, right_inverse, precision=PRECISE).astype(jnp.bfloat16)
    return (row_scale.reshape(-1), col_scale.reshape(-1), left_basis, right_basis)
```

```python
import functools

import jax
import jax.numpy as jnp
from jax import lax
from jax.experimental import pallas as pl
from jax.experimental.pallas import tpu as pltpu
from jax.sharding import PartitionSpec as P

TILE = 128
RB = 16
CB = 16


PRECISE = lax.Precision.HIGHEST
MESH = pl.DeviceIdType.MESH
VMEM = pl.BlockSpec(memory_space=pltpu.VMEM)
SMEM = pl.BlockSpec(memory_space=pltpu.SMEM)


BLOCK = 64
GROUP = 8


def block_inverse(block, low, high):
    rows = lax.broadcasted_iota(jnp.int32, block.shape, 0)
    pivots = jnp.ones_like(block)
    for base in range(0, BLOCK, GROUP):
        factors = []
        for at in range(base, base + GROUP):
            column = jnp.broadcast_to(block[:, low + at : low + at + 1], block.shape)
            for past, factor in enumerate(factors):
                column = column - factor * column[base + past : base + past + 1, :]
            pivots = jnp.where(rows == at, column, pivots)
            ratio = column * (1.0 / column[at : at + 1, :])
            factors.append(jnp.where(rows > at, ratio, 0.0))
        for at, factor in enumerate(factors):
            block = block - factor * block[base + at : base + at + 1, :]
    lanes = lax.broadcasted_iota(jnp.int32, block.shape, 1)
    inside = (lanes >= high) & (lanes < high + BLOCK)
    return jnp.where(inside, block * lax.rsqrt(pivots), 0.0)


def inverse_kernel(gram_ref, o_ref, work):
    width = gram_ref.shape[0]
    work[:, :width] = gram_ref[...]
    rows = lax.broadcasted_iota(jnp.int32, (width, width), 0)
    lanes = lax.broadcasted_iota(jnp.int32, (width, width), 1)
    work[:, width:] = jnp.where(rows == lanes, 1.0, 0.0)
    for index in range(width // BLOCK):
        start = index * BLOCK
        near = start // TILE * TILE
        low = start - near
        high = TILE - BLOCK - low
        block = work[start : start + BLOCK, near : near + TILE]
        rows = lax.broadcasted_iota(jnp.int32, block.shape, 0)
        lanes = lax.broadcasted_iota(jnp.int32, block.shape, 1)
        inside = (lanes >= low) & (lanes < low + BLOCK)
        block = jnp.where(inside, block, jnp.where(lanes - high == rows, 1.0, 0.0))
        inverse = block_inverse(block, low, high)
        panel = work[start : start + BLOCK, :]
        solved = jnp.dot(
            inverse,
            jnp.concatenate([panel, panel], axis=0),
            precision=PRECISE,
            preferred_element_type=jnp.float32,
        )
        o_ref[start : start + BLOCK, :] = solved[:, width:]
        if start + BLOCK < width:
            update = lax.dot_general(
                solved[:, :width],
                solved,
                (((0,), (0,)), ((), ())),
                precision=PRECISE,
                preferred_element_type=jnp.float32,
            )
            work[start + BLOCK :, :] = work[start + BLOCK :, :] - update[start + BLOCK :, :]


def factor_inverse(gram):
    width = gram.shape[0]
    return pl.pallas_call(
        inverse_kernel,
        out_shape=jax.ShapeDtypeStruct(gram.shape, gram.dtype),
        in_specs=[VMEM],
        out_specs=VMEM,
        scratch_shapes=[pltpu.VMEM((width, 2 * width), jnp.float32)],
        compiler_params=pltpu.CompilerParams(vmem_limit_bytes=16 << 20),
        name="inverse",
    )(gram).T


def params(identifier):
    return pltpu.CompilerParams(
        collective_id=identifier, has_side_effects=True, vmem_limit_bytes=32 << 20
    )


def greet(axes):
    barrier = pltpu.get_barrier_semaphore()
    total = 0
    for axis in axes:
        n = lax.axis_size(axis)
        me = lax.axis_index(axis)
        for step in range(1, n):
            pl.semaphore_signal(
                barrier, inc=1, device_id={axis: lax.rem(me + step, n)}, device_id_type=MESH
            )
        total += n - 1
    pl.semaphore_wait(barrier, total)


def remote(source, target, send_sem, recv_sem, axis, peer):
    return pltpu.make_async_remote_copy(
        src_ref=source,
        dst_ref=target,
        send_sem=send_sem,
        recv_sem=recv_sem,
        device_id={axis: peer},
        device_id_type=MESH,
    )


def scatter_sum_kernel(axis, x_ref, o_ref, held, send_sem, recv_sem):
    n = lax.axis_size(axis)
    me = lax.axis_index(axis)
    greet((axis,))
    copies = []
    for step in range(1, n):
        peer = lax.rem(me + step, n)
        copy = remote(
            x_ref.at[peer], held.at[step], send_sem.at[step], recv_sem.at[step], axis, peer
        )
        copy.start()
        copies.append(copy)
    o_ref[...] = x_ref[me]
    for step, copy in enumerate(copies):
        copy.wait()
        o_ref[...] += held[step + 1]


def scatter_sum(x, axis, identifier):
    n = lax.axis_size(axis)
    return pl.pallas_call(
        functools.partial(scatter_sum_kernel, axis),
        out_shape=jax.ShapeDtypeStruct(x.shape[1:], x.dtype),
        in_specs=[VMEM],
        out_specs=VMEM,
        scratch_shapes=[
            pltpu.VMEM(x.shape, x.dtype),
            pltpu.SemaphoreType.DMA((n,)),
            pltpu.SemaphoreType.DMA((n,)),
        ],
        compiler_params=params(identifier),
        name="scatter_sum",
    )(x)


def gather_kernel(axis, x_ref, o_ref, send_sem, recv_sem):
    n = lax.axis_size(axis)
    me = lax.axis_index(axis)
    greet((axis,))
    copies = []
    for step in range(1, n):
        copy = remote(
            x_ref, o_ref.at[me], send_sem.at[step], recv_sem.at[step], axis, lax.rem(me + step, n)
        )
        copy.start()
        copies.append(copy)
    o_ref[me] = x_ref[...]
    for copy in copies:
        copy.wait()


def gather(x, axis, identifier):
    n = lax.axis_size(axis)
    return pl.pallas_call(
        functools.partial(gather_kernel, axis),
        out_shape=jax.ShapeDtypeStruct((n,) + x.shape, x.dtype),
        in_specs=[VMEM],
        out_specs=VMEM,
        scratch_shapes=[
            pltpu.SemaphoreType.DMA((n,)),
            pltpu.SemaphoreType.DMA((n,)),
        ],
        compiler_params=params(identifier),
        name="gather",
    )(x)


def paired():
    n, me = lax.axis_size("term"), lax.axis_index("term")
    return n // 2, me // 2, lax.rem(me, 2)


def greet_paired(with_doc):
    nz, z, c = paired()
    barrier = pltpu.get_barrier_semaphore()
    targets = [("term", 2 * z + 1 - c)]
    targets += [("term", 2 * lax.rem(z + step, nz) + c) for step in range(1, nz)]
    if with_doc:
        m, my = lax.axis_size("doc"), lax.axis_index("doc")
        targets += [("doc", lax.rem(my + step, m)) for step in range(1, m)]
    for axis, peer in targets:
        pl.semaphore_signal(barrier, inc=1, device_id={axis: peer}, device_id_type=MESH)
    pl.semaphore_wait(barrier, len(targets))


def scatter_paired(x_ref, near, mid, far, total_ref, near_send, near_recv, far_send, far_recv):
    nz, z, c = paired()
    order = list(range(1, nz)) + [0]
    near_copies = {}
    for step in order:
        near_copies[step] = remote(
            x_ref.at[lax.rem(z + step, nz), 1 - c],
            near.at[step],
            near_send.at[step],
            near_recv.at[step],
            "term",
            2 * z + 1 - c,
        )
        near_copies[step].start()
    far_copies = []
    for step in range(1, nz):
        near_copies[step].wait()
        there = lax.rem(z + step, nz)
        mid[step] = x_ref[there, c] + near[step]
        copy = remote(
            mid.at[step], far.at[step], far_send.at[step], far_recv.at[step], "term", 2 * there + c
        )
        copy.start()
        far_copies.append(copy)
    near_copies[0].wait()
    total_ref[...] = x_ref[z, c] + near[0]
    for step, copy in enumerate(far_copies):
        copy.wait()
        total_ref[...] += far[step + 1]


def gather_paired(x_ref, o_ref, near_send, near_recv, far_send, far_recv):
    nz, z, c = paired()
    sibling = 2 * z + 1 - c
    far_copies = []
    for step in range(1, nz):
        copy = remote(
            x_ref,
            o_ref.at[z, c],
            far_send.at[step],
            far_recv.at[step],
            "term",
            2 * lax.rem(z + step, nz) + c,
        )
        copy.start()
        far_copies.append(copy)
    copy = remote(x_ref, o_ref.at[z, c], near_send.at[0], near_recv.at[0], "term", sibling)
    copy.start()
    near_copies = [copy]
    o_ref[z, c] = x_ref[...]
    for step in range(1, nz):
        far_copies[step - 1].wait()
        here = o_ref.at[lax.rem(z - step + nz, nz), c]
        copy = remote(here, here, near_send.at[step], near_recv.at[step], "term", sibling)
        copy.start()
        near_copies.append(copy)
    for copy in near_copies:
        copy.wait()


def semaphores(*sizes):
    return [pltpu.SemaphoreType.DMA((size,)) for size in sizes]


def scatter_term_kernel(x_ref, o_ref, near, mid, far, *sems):
    greet_paired(False)
    scatter_paired(x_ref, near, mid, far, o_ref, *sems)


def scatter_term(x, identifier):
    nz = x.shape[0]
    share = x.shape[2:]
    return pl.pallas_call(
        scatter_term_kernel,
        out_shape=jax.ShapeDtypeStruct(share, x.dtype),
        in_specs=[VMEM],
        out_specs=VMEM,
        scratch_shapes=[pltpu.VMEM((nz,) + share, x.dtype)] * 3 + semaphores(nz, nz, nz, nz),
        compiler_params=params(identifier),
        name="scatter_term",
    )(x)


def gather_term_kernel(x_ref, o_ref, *sems):
    greet_paired(False)
    gather_paired(x_ref, o_ref, *sems)


def gather_term(x, identifier):
    nz = lax.axis_size("term") // 2
    return pl.pallas_call(
        gather_term_kernel,
        out_shape=jax.ShapeDtypeStruct((nz, 2) + x.shape, x.dtype),
        in_specs=[VMEM],
        out_specs=VMEM,
        scratch_shapes=semaphores(nz, nz, nz, nz),
        compiler_params=params(identifier),
        name="gather_term",
    )(x)


def gram_sum_kernel(x_ref, o_ref, near, mid, far, second, part, done, *sems):
    m, my = lax.axis_size("doc"), lax.axis_index("doc")
    send_b, recv_b = sems[4:6]
    greet_paired(True)
    scatter_paired(x_ref, near, mid, far, part, *sems[:4])
    copies = []
    for step in range(1, m):
        copy = remote(
            part, second.at[step], send_b.at[step], recv_b.at[step], "doc", lax.rem(my + step, m)
        )
        copy.start()
        copies.append(copy)
    second[0] = part[...]
    for copy in copies:
        copy.wait()
    total = second[my]
    for source in range(1, m):
        total = total + second[lax.rem(my - source + m, m)]
    done[...] = total
    gather_paired(done, o_ref, *sems[6:])


def gram_sum(x, identifier):
    nz, m = x.shape[0], lax.axis_size("doc")
    share = x.shape[2:]
    return pl.pallas_call(
        gram_sum_kernel,
        out_shape=jax.ShapeDtypeStruct(x.shape, x.dtype),
        in_specs=[VMEM],
        out_specs=VMEM,
        scratch_shapes=[pltpu.VMEM((nz,) + share, x.dtype)] * 3
        + [
            pltpu.VMEM((m,) + share, x.dtype),
            pltpu.VMEM(share, x.dtype),
            pltpu.VMEM(share, x.dtype),
        ]
        + semaphores(nz, nz, nz, nz, m, m, nz, nz, nz, nz),
        compiler_params=params(identifier),
        name="gram_sum",
    )(x)


def split3(value):
    high = value.astype(jnp.bfloat16)
    rest = value - high.astype(jnp.float32)
    middle = rest.astype(jnp.bfloat16)
    return high, middle, (rest - middle.astype(jnp.float32)).astype(jnp.bfloat16)


def spread(value, parts):
    high, middle, low = (part.astype(jnp.float32) for part in split3(value))
    blocks, depth, lanes = parts.shape
    rows = lax.broadcasted_iota(jnp.int32, (depth, lanes), 0)
    for block in range(blocks):
        at = slice(block, block + 1)
        picked = jnp.where(rows == 0, high[at], jnp.where(rows == 1, middle[at], low[at]))
        parts[block] = jnp.where(rows < 3, picked, 0.0).astype(jnp.bfloat16)


def tile_sums(tiles, source_ids, parts, sums, target, forward):
    slots = sums.shape[0]
    for slot in range(slots):
        product = lax.dot_general(
            parts[source_ids[slot]],
            tiles[slot],
            (((1,), (1 if forward else 0,)), ((), ())),
            preferred_element_type=jnp.float32,
        )
        sums[slot : slot + 1, :] = product[0:1] + product[1:2] + product[2:3]
    stacked = jnp.concatenate(split3(sums[...]), axis=0)
    return jnp.dot(target, stacked, preferred_element_type=jnp.float32)


def start_exchange(held, axis, send_sem, recv_sem):
    n, me = lax.axis_size(axis), lax.axis_index(axis)
    copies = []
    for step in range(1, n):
        copy = remote(
            held.at[0], held.at[step], send_sem.at[step], recv_sem.at[step], axis, lax.rem(me + step, n)
        )
        copy.start()
        copies.append(copy)
    return copies


def finish_exchange(copies, held, axis):
    n, me = lax.axis_size(axis), lax.axis_index(axis)
    for copy in copies:
        copy.wait()
    total = held[me]
    for source in range(1, n):
        total = total + held[lax.rem(me - source + n, n)]
    return total


def scale_kernel(
    ids,
    live,
    tiles_hbm,
    start_ref,
    row_ref,
    col_ref,
    weight_ref,
    mean_ref,
    dense_ref,
    turned_ref,
    tiles,
    flipped,
    parts,
    sums,
    held_a,
    held_b,
    held_c,
    held_d,
    held_e,
    load_sem,
    *sems,
):
    slots = tiles_hbm.shape[0]
    load = pltpu.make_async_copy(tiles_hbm, tiles.at[pl.ds(0, slots)], load_sem)
    load.start()
    greet(("term", "doc"))
    tiles[slots] = jnp.zeros(tiles.shape[1:], tiles.dtype)
    flipped[slots] = jnp.zeros(tiles.shape[1:], tiles.dtype)
    blocks = row_ref.shape[0]
    places = lax.broadcasted_iota(jnp.int32, (blocks, live.shape[1]), 0)
    to_rows = jnp.where(places == live[0:1, :], 1.0, 0.0).astype(jnp.bfloat16)
    to_cols = jnp.where(places == live[1:2, :], 1.0, 0.0).astype(jnp.bfloat16)
    row_ids, col_ids = ids.at[pl.ds(0, slots)], ids.at[pl.ds(slots, slots)]

    def build(out_ref, source, turn):
        def place_row(outer, carry):
            at = pl.multiple_of(outer * TILE, TILE)
            for inner in range(blocks):
                place = inner * blocks + outer if turn else outer * blocks + inner
                tile = source[ids[2 * slots + place]]
                out_ref[pl.ds(at, TILE), inner * TILE : (inner + 1) * TILE] = tile
            return carry

        lax.fori_loop(0, blocks, place_row, 0)

    def flip(slot, carry):
        flipped[slot] = tiles[slot].T
        return carry

    spread(jnp.ones(row_ref.shape, jnp.float32), parts)
    mean = jnp.sum(start_ref[...].astype(jnp.float32), axis=0, keepdims=True)
    load.wait()
    held_a[0, :blocks, :] = tile_sums(tiles, col_ids, parts, sums, to_rows, True)
    extra = held_a.shape[1] - blocks
    pieces = [mean[:, at : at + TILE] for at in range(0, mean.shape[1], TILE)]
    pieces.append(jnp.zeros((extra - len(pieces), TILE), jnp.float32))
    held_a[0, blocks:, :] = jnp.concatenate(pieces, axis=0)
    copies = start_exchange(held_a, "doc", *sems[0:2])
    build(dense_ref, tiles, False)
    joined = finish_exchange(copies, held_a, "doc")
    mean_ref[...] = joined[blocks:, :]
    spread(1.0 / joined[:blocks], parts)

    held_b[0] = tile_sums(tiles, row_ids, parts, sums, to_cols, False)
    copies = start_exchange(held_b, "term", *sems[2:4])
    lax.fori_loop(0, slots, flip, 0)
    spread(1.0 / finish_exchange(copies, held_b, "term"), parts)

    held_c[0] = tile_sums(tiles, col_ids, parts, sums, to_rows, True)
    copies = start_exchange(held_c, "doc", *sems[4:6])
    build(turned_ref, flipped, True)
    row_scale = 1.0 / finish_exchange(copies, held_c, "doc")
    row_ref[...] = row_scale
    spread(row_scale, parts)

    held_d[0] = tile_sums(tiles, row_ids, parts, sums, to_cols, False)
    copies = start_exchange(held_d, "term", *sems[6:8])
    col_scale = 1.0 / finish_exchange(copies, held_d, "term")
    col_ref[...] = col_scale
    spread(col_scale, parts)

    held_e[0] = tile_sums(tiles, col_ids, parts, sums, to_rows, True)
    copies = start_exchange(held_e, "doc", *sems[8:10])
    weight_ref[...] = row_scale * finish_exchange(copies, held_e, "doc")


def scale_stage(tile_values, tile_rows, tile_cols, tile_count, start_block, identifier):
    slots = tile_values.shape[0]
    m, n = lax.axis_size("doc"), lax.axis_size("term")
    slot = jnp.arange(slots, dtype=jnp.int32)
    used = slot < tile_count[0, 0]
    rows, cols = tile_rows[0], tile_cols[0]
    cell = jnp.arange(RB * CB, dtype=jnp.int32)
    found = ((rows * CB + cols)[None, :] == cell[:, None]) & used[None, :]
    lookup = slots + jnp.sum(jnp.where(found, slot[None, :] - slots, 0), axis=1)
    ids = jnp.concatenate([rows, cols, lookup])
    live = jnp.stack([jnp.where(used, rows, RB), jnp.where(used, cols, CB)])
    live = jnp.concatenate([live, live, live], axis=1)
    vector = jax.ShapeDtypeStruct((RB, TILE), jnp.float32)
    extra = -(-start_block.shape[1] // (8 * TILE)) * 8
    square = jax.ShapeDtypeStruct((RB * TILE, CB * TILE), tile_values.dtype)
    held = pltpu.VMEM((m, RB, TILE), jnp.float32)
    return pl.pallas_call(
        scale_kernel,
        out_shape=[
            vector,
            vector,
            vector,
            jax.ShapeDtypeStruct((extra, TILE), jnp.float32),
            square,
            square,
        ],
        in_specs=[SMEM, VMEM, pl.BlockSpec(memory_space=pl.ANY), VMEM],
        out_specs=[VMEM] * 6,
        scratch_shapes=[
            pltpu.VMEM((slots + 1, TILE, TILE), tile_values.dtype),
            pltpu.VMEM((slots + 1, TILE, TILE), tile_values.dtype),
            pltpu.VMEM((RB, 16, TILE), jnp.bfloat16),
            pltpu.VMEM((slots, TILE), jnp.float32),
            pltpu.VMEM((m, RB + extra, TILE), jnp.float32),
            pltpu.VMEM((n, RB, TILE), jnp.float32),
            held,
            pltpu.VMEM((n, RB, TILE), jnp.float32),
            held,
            pltpu.SemaphoreType.DMA(()),
        ]
        + semaphores(m, m, n, n, m, m, n, n, m, m),
        compiler_params=params(identifier),
        name="scale",
    )(ids, live, tile_values, start_block)


def total_gram(block, extra, scale, identifier):
    n = lax.axis_size("term")
    width = block.shape[1]
    gram = jnp.dot(block.T, block, precision=PRECISE) / scale
    rows = [gram]
    if extra is not None:
        rows += [extra[None, :], jnp.zeros((8 * n - 1, width), jnp.float32)]
    stacked = jnp.concatenate(rows, axis=0) if extra is not None else gram
    summed = gram_sum(stacked.reshape(n // 2, 2, -1, width), identifier).reshape(stacked.shape)
    return summed[:width], (summed[width] if extra is not None else None)


def per_device(tile_values, tile_rows, tile_cols, tile_count, start_block):
    terms_total = RB * TILE * lax.axis_size("term")
    docs_total = CB * TILE * lax.axis_size("doc")
    width = start_block.shape[1]
    rows_out, cols_out, weights, means, matrix, turned = scale_stage(
        tile_values, tile_rows, tile_cols, tile_count, start_block, 0
    )
    row_flat, col_flat, weight_flat = (x.reshape(-1) for x in (rows_out, cols_out, weights))
    start_mean = means[: width // TILE].reshape(-1)
    scaled_start = (col_flat[:, None] * start_block.astype(jnp.float32)).astype(jnp.bfloat16)
    left_part = jnp.dot(matrix, scaled_start, preferred_element_type=jnp.float32)
    doc_size = lax.axis_size("doc")
    left_share = RB * TILE // doc_size
    left_offset = lax.axis_index("doc") * left_share
    left_raw = scatter_sum(left_part.reshape(doc_size, left_share, width), "doc", 17)
    row_rows = lax.dynamic_slice_in_dim(row_flat, left_offset, left_share)
    row_weight = lax.dynamic_slice_in_dim(weight_flat, left_offset, left_share)
    left_block = (
        row_rows[:, None] * left_raw - row_weight[:, None] * start_mean[None, :] / docs_total
    )
    weighted = jnp.sum(row_weight[:, None] * left_block, axis=0)
    left_gram, weighted = total_gram(left_block, weighted, terms_total, 18)
    left_inverse = factor_inverse(left_gram)
    share_float = jnp.dot(left_block, left_inverse, precision=PRECISE)
    lean = jnp.dot(weighted, left_inverse, precision=PRECISE)
    left_basis = gather(share_float.astype(jnp.bfloat16), "doc", 19).reshape(RB * TILE, width)
    scaled_left = (row_flat[:, None] * left_basis.astype(jnp.float32)).astype(jnp.bfloat16)
    right_part = jnp.dot(turned, scaled_left, preferred_element_type=jnp.float32)
    term_size = lax.axis_size("term")
    right_share = CB * TILE // term_size
    right_offset = lax.axis_index("term") * right_share
    right_raw = scatter_term(right_part.reshape(term_size // 2, 2, right_share, width), 20)
    col_rows = lax.dynamic_slice_in_dim(col_flat, right_offset, right_share)
    right_block = col_rows[:, None] * right_raw - lean[None, :] / docs_total
    right_gram, _ = total_gram(right_block, None, docs_total, 21)
    right_inverse = factor_inverse(right_gram)
    right_piece = jnp.dot(right_block, right_inverse, precision=PRECISE).astype(jnp.bfloat16)
    right_basis = gather_term(right_piece, 22).reshape(CB * TILE, width)
    return (row_flat, col_flat, left_basis, right_basis)


def solution(mesh):
    placed = (
        P("term", "doc", None),
        P("term", "doc"),
        P("term", "doc"),
        P("term", "doc"),
        P("doc", None),
    )
    return jax.shard_map(
        per_device,
        mesh=mesh,
        in_specs=placed,
        out_specs=(P("term"), P("doc"), P("term", None), P("doc", None)),
        check_vma=False,
    )
```

```python
import math

import jax
import jax.numpy as jnp
from jax import lax
from jax.experimental import pallas as pl
from jax.experimental.pallas import tpu as pltpu
from jax.sharding import PartitionSpec as P

TILE = 128
RB = 16
CB = 16


PRECISE = lax.Precision.HIGHEST
MESH = pl.DeviceIdType.MESH
VMEM = pl.BlockSpec(memory_space=pltpu.VMEM)
SMEM = pl.BlockSpec(memory_space=pltpu.SMEM)


BLOCK = 64
GROUP = 8


def block_inverse(block, low, high):
    rows = lax.broadcasted_iota(jnp.int32, block.shape, 0)
    pivots = jnp.ones_like(block)
    for base in range(0, BLOCK, GROUP):
        factors = []
        for at in range(base, base + GROUP):
            column = jnp.broadcast_to(block[:, low + at : low + at + 1], block.shape)
            for past, factor in enumerate(factors):
                column = column - factor * column[base + past : base + past + 1, :]
            pivots = jnp.where(rows == at, column, pivots)
            ratio = column * (1.0 / column[at : at + 1, :])
            factors.append(jnp.where(rows > at, ratio, 0.0))
        for at, factor in enumerate(factors):
            block = block - factor * block[base + at : base + at + 1, :]
    lanes = lax.broadcasted_iota(jnp.int32, block.shape, 1)
    inside = (lanes >= high) & (lanes < high + BLOCK)
    return jnp.where(inside, block * lax.rsqrt(pivots), 0.0)


def inverse_kernel(gram_ref, o_ref, work):
    width = gram_ref.shape[0]
    work[:, :width] = gram_ref[...]
    rows = lax.broadcasted_iota(jnp.int32, (width, width), 0)
    lanes = lax.broadcasted_iota(jnp.int32, (width, width), 1)
    work[:, width:] = jnp.where(rows == lanes, 1.0, 0.0)
    for index in range(width // BLOCK):
        start = index * BLOCK
        near = start // TILE * TILE
        low = start - near
        high = TILE - BLOCK - low
        block = work[start : start + BLOCK, near : near + TILE]
        rows = lax.broadcasted_iota(jnp.int32, block.shape, 0)
        lanes = lax.broadcasted_iota(jnp.int32, block.shape, 1)
        inside = (lanes >= low) & (lanes < low + BLOCK)
        block = jnp.where(inside, block, jnp.where(lanes - high == rows, 1.0, 0.0))
        inverse = block_inverse(block, low, high)
        panel = work[start : start + BLOCK, :]
        solved = jnp.dot(
            inverse,
            jnp.concatenate([panel, panel], axis=0),
            precision=PRECISE,
            preferred_element_type=jnp.float32,
        )
        o_ref[start : start + BLOCK, :] = solved[:, width:]
        if start + BLOCK < width:
            update = lax.dot_general(
                solved[:, :width],
                solved,
                (((0,), (0,)), ((), ())),
                precision=PRECISE,
                preferred_element_type=jnp.float32,
            )
            work[start + BLOCK :, :] = work[start + BLOCK :, :] - update[start + BLOCK :, :]


def params(identifier):
    return pltpu.CompilerParams(
        collective_id=identifier, has_side_effects=True, vmem_limit_bytes=32 << 20
    )


def greet(axes):
    barrier = pltpu.get_barrier_semaphore()
    total = 0
    for axis in axes:
        n = lax.axis_size(axis)
        me = lax.axis_index(axis)
        for step in range(1, n):
            pl.semaphore_signal(
                barrier, inc=1, device_id={axis: lax.rem(me + step, n)}, device_id_type=MESH
            )
        total += n - 1
    pl.semaphore_wait(barrier, total)


def remote(source, target, send_sem, recv_sem, axis, peer):
    return pltpu.make_async_remote_copy(
        src_ref=source,
        dst_ref=target,
        send_sem=send_sem,
        recv_sem=recv_sem,
        device_id={axis: peer},
        device_id_type=MESH,
    )


def paired():
    n, me = lax.axis_size("term"), lax.axis_index("term")
    return n // 2, me // 2, lax.rem(me, 2)


def semaphores(*sizes):
    return [pltpu.SemaphoreType.DMA((size,)) for size in sizes]


def split3(value):
    high = value.astype(jnp.bfloat16)
    rest = value - high.astype(jnp.float32)
    middle = rest.astype(jnp.bfloat16)
    return high, middle, (rest - middle.astype(jnp.float32)).astype(jnp.bfloat16)


def spread(value, parts):
    high, middle, low = (part.astype(jnp.float32) for part in split3(value))
    blocks, depth, lanes = parts.shape
    rows = lax.broadcasted_iota(jnp.int32, (depth, lanes), 0)
    for block in range(blocks):
        at = slice(block, block + 1)
        picked = jnp.where(rows == 0, high[at], jnp.where(rows == 1, middle[at], low[at]))
        parts[block] = jnp.where(rows < 3, picked, 0.0).astype(jnp.bfloat16)


def tile_sums(tiles, source_ids, parts, sums, target, forward):
    slots = sums.shape[0]
    for slot in range(slots):
        product = lax.dot_general(
            parts[source_ids[slot]],
            tiles[slot],
            (((1,), (1 if forward else 0,)), ((), ())),
            preferred_element_type=jnp.float32,
        )
        sums[slot : slot + 1, :] = product[0:1] + product[1:2] + product[2:3]
    stacked = jnp.concatenate(split3(sums[...]), axis=0)
    return jnp.dot(target, stacked, preferred_element_type=jnp.float32)


def start_exchange(held, axis, send_sem, recv_sem):
    n, me = lax.axis_size(axis), lax.axis_index(axis)
    copies = []
    for step in range(1, n):
        copy = remote(
            held.at[0], held.at[step], send_sem.at[step], recv_sem.at[step], axis, lax.rem(me + step, n)
        )
        copy.start()
        copies.append(copy)
    return copies


def finish_exchange(copies, held, axis):
    n, me = lax.axis_size(axis), lax.axis_index(axis)
    for copy in copies:
        copy.wait()
    total = held[me]
    for source in range(1, n):
        total = total + held[lax.rem(me - source + n, n)]
    return total


def scale_kernel(
    ids,
    live,
    tiles_hbm,
    start_ref,
    row_ref,
    col_ref,
    weight_ref,
    mean_ref,
    dense_ref,
    turned_ref,
    tiles,
    flipped,
    parts,
    sums,
    held_a,
    held_b,
    held_c,
    held_d,
    held_e,
    load_sem,
    *sems,
):
    slots = tiles_hbm.shape[0]
    load = pltpu.make_async_copy(tiles_hbm, tiles.at[pl.ds(0, slots)], load_sem)
    load.start()
    greet(("term", "doc"))
    tiles[slots] = jnp.zeros(tiles.shape[1:], tiles.dtype)
    flipped[slots] = jnp.zeros(tiles.shape[1:], tiles.dtype)
    blocks = row_ref.shape[0]
    places = lax.broadcasted_iota(jnp.int32, (blocks, live.shape[1]), 0)
    to_rows = jnp.where(places == live[0:1, :], 1.0, 0.0).astype(jnp.bfloat16)
    to_cols = jnp.where(places == live[1:2, :], 1.0, 0.0).astype(jnp.bfloat16)
    row_ids, col_ids = ids.at[pl.ds(0, slots)], ids.at[pl.ds(slots, slots)]

    def build(out_ref, source, turn):
        def place_row(outer, carry):
            at = pl.multiple_of(outer * TILE, TILE)
            for inner in range(blocks):
                place = inner * blocks + outer if turn else outer * blocks + inner
                tile = source[ids[2 * slots + place]]
                out_ref[pl.ds(at, TILE), inner * TILE : (inner + 1) * TILE] = tile
            return carry

        lax.fori_loop(0, blocks, place_row, 0)

    def flip(slot, carry):
        flipped[slot] = tiles[slot].T
        return carry

    spread(jnp.ones(row_ref.shape, jnp.float32), parts)
    mean = jnp.sum(start_ref[...].astype(jnp.float32), axis=0, keepdims=True)
    load.wait()
    held_a[0, :blocks, :] = tile_sums(tiles, col_ids, parts, sums, to_rows, True)
    extra = held_a.shape[1] - blocks
    pieces = [mean[:, at : at + TILE] for at in range(0, mean.shape[1], TILE)]
    pieces.append(jnp.zeros((extra - len(pieces), TILE), jnp.float32))
    held_a[0, blocks:, :] = jnp.concatenate(pieces, axis=0)
    copies = start_exchange(held_a, "doc", *sems[0:2])
    build(dense_ref, tiles, False)
    joined = finish_exchange(copies, held_a, "doc")
    mean_ref[...] = joined[blocks:, :]
    spread(1.0 / joined[:blocks], parts)

    held_b[0] = tile_sums(tiles, row_ids, parts, sums, to_cols, False)
    copies = start_exchange(held_b, "term", *sems[2:4])
    lax.fori_loop(0, slots, flip, 0)
    spread(1.0 / finish_exchange(copies, held_b, "term"), parts)

    held_c[0] = tile_sums(tiles, col_ids, parts, sums, to_rows, True)
    copies = start_exchange(held_c, "doc", *sems[4:6])
    build(turned_ref, flipped, True)
    row_scale = 1.0 / finish_exchange(copies, held_c, "doc")
    row_ref[...] = row_scale
    spread(row_scale, parts)

    held_d[0] = tile_sums(tiles, row_ids, parts, sums, to_cols, False)
    copies = start_exchange(held_d, "term", *sems[6:8])
    col_scale = 1.0 / finish_exchange(copies, held_d, "term")
    col_ref[...] = col_scale
    spread(col_scale, parts)

    held_e[0] = tile_sums(tiles, col_ids, parts, sums, to_rows, True)
    copies = start_exchange(held_e, "doc", *sems[8:10])
    weight_ref[...] = row_scale * finish_exchange(copies, held_e, "doc")


def scale_stage(tile_values, tile_rows, tile_cols, tile_count, start_block, identifier):
    slots = tile_values.shape[0]
    m, n = lax.axis_size("doc"), lax.axis_size("term")
    slot = jnp.arange(slots, dtype=jnp.int32)
    used = slot < tile_count[0, 0]
    rows, cols = tile_rows[0], tile_cols[0]
    cell = jnp.arange(RB * CB, dtype=jnp.int32)
    found = ((rows * CB + cols)[None, :] == cell[:, None]) & used[None, :]
    lookup = slots + jnp.sum(jnp.where(found, slot[None, :] - slots, 0), axis=1)
    ids = jnp.concatenate([rows, cols, lookup])
    live = jnp.stack([jnp.where(used, rows, RB), jnp.where(used, cols, CB)])
    live = jnp.concatenate([live, live, live], axis=1)
    vector = jax.ShapeDtypeStruct((RB, TILE), jnp.float32)
    extra = -(-start_block.shape[1] // (8 * TILE)) * 8
    square = jax.ShapeDtypeStruct((RB * TILE, CB * TILE), tile_values.dtype)
    held = pltpu.VMEM((m, RB, TILE), jnp.float32)
    return pl.pallas_call(
        scale_kernel,
        out_shape=[
            vector,
            vector,
            vector,
            jax.ShapeDtypeStruct((extra, TILE), jnp.float32),
            square,
            square,
        ],
        in_specs=[SMEM, VMEM, pl.BlockSpec(memory_space=pl.ANY), VMEM],
        out_specs=[VMEM] * 6,
        scratch_shapes=[
            pltpu.VMEM((slots + 1, TILE, TILE), tile_values.dtype),
            pltpu.VMEM((slots + 1, TILE, TILE), tile_values.dtype),
            pltpu.VMEM((RB, 16, TILE), jnp.bfloat16),
            pltpu.VMEM((slots, TILE), jnp.float32),
            pltpu.VMEM((m, RB + extra, TILE), jnp.float32),
            pltpu.VMEM((n, RB, TILE), jnp.float32),
            held,
            pltpu.VMEM((n, RB, TILE), jnp.float32),
            held,
            pltpu.SemaphoreType.DMA(()),
        ]
        + semaphores(m, m, n, n, m, m, n, n, m, m),
        compiler_params=params(identifier),
        name="scale",
    )(ids, live, tile_values, start_block)


CODES = 32760.0
OCTAVE = 256.0 / math.log(2.0)


def encode(value):
    rows, lanes = value.shape
    groups = value.reshape(rows // 8, 8, lanes)
    top = jnp.maximum(jnp.max(jnp.abs(groups), axis=0), 1e-30)
    level = jnp.ceil(jnp.log(top) * OCTAVE)
    codes = jnp.round(groups * (jnp.exp(level * (-1.0 / OCTAVE)) * CODES))
    whole = jnp.concatenate([codes.reshape(rows, lanes), level, level], axis=0)
    return whole.astype(jnp.int32).astype(jnp.int16)


def decode(block):
    rows, lanes = block.shape[0] - 16, block.shape[1]
    value = block.astype(jnp.int32).astype(jnp.float32)
    scale = jnp.exp(value[rows : rows + 8] * (1.0 / OCTAVE)) * (1.0 / CODES)
    return (value[:rows].reshape(rows // 8, 8, lanes) * scale[None]).reshape(rows, lanes)


def grid_of(n):
    nx = int(math.isqrt(n))
    while n % nx:
        nx -= 1
    return nx, n // nx


def turn_out(vector_ref, block, lanes):
    row = jnp.broadcast_to(vector_ref[pl.ds(block, 1), :], (TILE, TILE))
    column = row.T
    return jnp.concatenate([column] * (lanes // TILE), axis=1)


def precise(a, b, dims):
    return lax.dot_general(
        a, b, (dims, ((), ())), precision=PRECISE, preferred_element_type=jnp.float32
    )


def gram_steps(x_ref, o_ref, near, mid, far, second, part, done, *sems):
    nz, z, c = paired()
    m, my = lax.axis_size("doc"), lax.axis_index("doc")
    rows = part.shape[0]
    sibling = 2 * z + 1 - c

    def share(ref, there, core):
        return ref.at[pl.ds(pl.multiple_of((2 * there + core) * rows, 8), rows)]

    near_copies, far_copies = {}, []
    for step in list(range(1, nz)) + [0]:
        there = lax.rem(z + step, nz)
        near_copies[step] = remote(
            share(x_ref, there, 1 - c), near.at[step], sems[0].at[step], sems[1].at[step], "term", sibling
        )
        near_copies[step].start()
    yield
    for step in range(1, nz):
        near_copies[step].wait()
        there = lax.rem(z + step, nz)
        mid[step] = share(x_ref, there, c)[...] + near[step]
        copy = remote(
            mid.at[step], far.at[step], sems[2].at[step], sems[3].at[step], "term", 2 * there + c
        )
        copy.start()
        far_copies.append(copy)
    near_copies[0].wait()
    part[...] = share(x_ref, z, c)[...] + near[0]
    yield
    for step, copy in enumerate(far_copies):
        copy.wait()
        part[...] += far[step + 1]
    copies = []
    for step in range(1, m):
        copy = remote(
            part, second.at[step], sems[4].at[step], sems[5].at[step], "doc", lax.rem(my + step, m)
        )
        copy.start()
        copies.append(copy)
    second[0] = part[...]
    yield
    for copy in copies:
        copy.wait()
    total = second[my]
    for source in range(1, m):
        total = total + second[lax.rem(my - source + m, m)]
    done[...] = total
    far_copies = []
    here = share(o_ref, z, c)
    for step in range(1, nz):
        copy = remote(
            done, here, sems[6].at[step], sems[7].at[step], "term", 2 * lax.rem(z + step, nz) + c
        )
        copy.start()
        far_copies.append(copy)
    copy = remote(done, here, sems[8].at[0], sems[9].at[0], "term", sibling)
    copy.start()
    near_copies = [copy]
    here[...] = total
    yield
    for step in range(1, nz):
        far_copies[step - 1].wait()
        there = share(o_ref, lax.rem(z - step + nz, nz), c)
        copy = remote(there, there, sems[8].at[step], sems[9].at[step], "term", sibling)
        copy.start()
        near_copies.append(copy)
    for copy in near_copies:
        copy.wait()


def gram_scratch(width):
    nz, m = lax.axis_size("term") // 2, lax.axis_size("doc")
    rows = width // (2 * nz)
    spread_over = pltpu.VMEM((nz, rows, width), jnp.float32)
    alone = pltpu.VMEM((rows, width), jnp.float32)
    whole = pltpu.VMEM((width, width), jnp.float32)
    return [whole, whole] + [spread_over] * 3 + [pltpu.VMEM((m, rows, width), jnp.float32), alone, alone] + semaphores(
        nz, nz, nz, nz, m, m, nz, nz, nz, nz
    )


GRAM_REFS = 18


def basis_kernel(
    matrix,
    turned,
    start_ref,
    row_ref,
    col_ref,
    weight_ref,
    mean_ref,
    left_out,
    right_out,
    row_turn,
    col_turn,
    scaled,
    partial,
    send_a,
    recv_a,
    send_b,
    recv_b,
    gathered,
    factor,
    near_send,
    near_recv,
    far_send,
    far_recv,
    right_parts,
    inverse_ref,
    work,
    *rest,
):
    left_gram, right_gram = rest[:GRAM_REFS], rest[GRAM_REFS : 2 * GRAM_REFS]
    sems = rest[2 * GRAM_REFS :]
    n, m = lax.axis_size("term"), lax.axis_size("doc")
    nz, z, c = paired()
    doc = lax.axis_index("doc")
    nx, ny = grid_of(m)
    x, y = lax.rem(doc, nx), doc // nx
    terms, width = left_out.shape
    docs = right_out.shape[0]
    share, piece = terms // m, docs // n
    docs_total = docs * m

    greet(("term", "doc"))

    def axes(flow):
        return (x, nx, y, ny) if flow == 0 else (y, ny, x, nx)

    def device(flow, first, second):
        return second * nx + first if flow == 0 else first * nx + second

    def lanes(flow):
        return slice(flow * TILE, (flow + 1) * TILE)

    def prepare(block, carry):
        at = pl.ds(pl.multiple_of(block * TILE, TILE), TILE)
        column = turn_out(col_ref, block, width)
        col_turn[at, :] = column[:, :TILE]
        scaled[at, :] = (column * start_ref[at, :].astype(jnp.float32)).astype(jnp.bfloat16)
        row_turn[at, :] = turn_out(row_ref, block, TILE)
        return carry

    lax.fori_loop(0, docs // TILE, prepare, 0)

    steps = [(dx, dy) for dx in range(nx) for dy in range(ny)]
    steps.sort(key=lambda s: -((s[0] > 0) + (s[1] > 0)))
    copies_a, copies_b = {}, {}
    for dx, dy in steps:
        target = lax.rem(y + dy, ny) * nx + lax.rem(x + dx, nx)
        at = pl.ds(pl.multiple_of(target * share, share), share)
        product = jnp.dot(matrix[at, :], scaled[...], preferred_element_type=jnp.float32)
        column = row_turn[at, :]
        product = product * jnp.concatenate([column] * (width // TILE), axis=1)
        partial[dy * nx + dx] = product
        for flow in range(2):
            a, n1, b, n2 = axes(flow)
            s1, s2 = (dx, dy) if flow == 0 else (dy, dx)
            if s1 == 0:
                continue
            slot = s1 * n2 + s2
            send_a[flow, slot] = encode(product[:, lanes(flow)])
            copies_a[flow, s1, s2] = remote(
                send_a.at[flow, slot],
                recv_a.at[flow, slot],
                sems[0].at[flow, slot],
                sems[1].at[flow, slot],
                "doc",
                device(flow, lax.rem(a + s1, n1), b),
            )
            copies_a[flow, s1, s2].start()

    def own(flow, s2):
        dx, dy = (0, s2) if flow == 0 else (s2, 0)
        return partial[dy * nx + dx, :, lanes(flow)]

    def landed(flow, s2):
        a, n1, b, n2 = axes(flow)
        total = own(flow, s2)
        for s1 in range(1, n1):
            copies_a[flow, s1, s2].wait()
            total = total + decode(recv_a[flow, s1 * n2 + s2])
        return total

    for flow in range(2):
        a, n1, b, n2 = axes(flow)
        for s2 in range(1, n2):
            send_b[flow, s2] = encode(landed(flow, s2))
            copies_b[flow, s2] = remote(
                send_b.at[flow, s2],
                recv_b.at[flow, s2],
                sems[2].at[flow, s2],
                sems[3].at[flow, s2],
                "doc",
                device(flow, a, lax.rem(b + s2, n2)),
            )
            copies_b[flow, s2].start()

    blocks_of_share = share // TILE
    weight = jnp.concatenate(
        [turn_out(weight_ref, doc * blocks_of_share + k, TILE) for k in range(blocks_of_share)], axis=0
    )
    copies_c, copies_d = {}, {}
    left = []
    for flow in range(2):
        a, n1, b, n2 = axes(flow)
        total = landed(flow, 0)
        for s2 in range(1, n2):
            copies_b[flow, s2].wait()
            total = total + decode(recv_b[flow, s2])
        total = total - weight * (mean_ref[flow : flow + 1, :] * (1.0 / docs_total))
        left.append(total)
        gathered[flow, doc] = encode(total)
        for s1 in range(1, n1):
            copies_c[flow, s1] = remote(
                gathered.at[flow, doc],
                gathered.at[flow, doc],
                sems[4].at[flow, s1],
                sems[5].at[flow, s1],
                "doc",
                device(flow, lax.rem(a + s1, n1), b),
            )
            copies_c[flow, s1].start()

    left_share = jnp.concatenate(left, axis=1)
    gram_in, gram_out = left_gram[:2]
    gram_in[...] = precise(left_share, left_share, ((0,), (0,))) * (1.0 / (terms * n))
    for k in range(width // TILE):
        weighted = jnp.sum(weight * left[k], axis=0, keepdims=True)
        gram_in[width - width // TILE + k : width - width // TILE + k + 1, :TILE] = weighted
    left_steps = gram_steps(*left_gram)
    next(left_steps)

    for flow in range(2):
        a, n1, b, n2 = axes(flow)
        for s1 in range(n1):
            if s1:
                copies_c[flow, s1].wait()
            source = device(flow, lax.rem(a - s1 + n1, n1), b)
            for s2 in range(1, n2):
                copies_d[flow, s1, s2] = remote(
                    gathered.at[flow, source],
                    gathered.at[flow, source],
                    sems[6].at[flow, s1 * n2 + s2],
                    sems[7].at[flow, s1 * n2 + s2],
                    "doc",
                    device(flow, a, lax.rem(b + s2, n2)),
                )
                copies_d[flow, s1, s2].start()
    next(left_steps)
    next(left_steps)
    for copy in copies_d.values():
        copy.wait()

    def unpack(block, carry):
        at = pl.ds(pl.multiple_of(block * share, share), share)
        for flow in range(2):
            value = decode(gathered[flow, block]) * row_turn[at, :]
            high = value.astype(jnp.bfloat16)
            factor[at, lanes(flow)] = high
            low = slice(width + flow * TILE, width + (flow + 1) * TILE)
            factor[at, low] = (value - high.astype(jnp.float32)).astype(jnp.bfloat16)
        return carry

    lax.fori_loop(0, m, unpack, 0)

    def right_product(there, core):
        at = pl.ds(pl.multiple_of((2 * there + core) * piece, piece), piece)
        both = jnp.dot(turned[at, :], factor[...], preferred_element_type=jnp.float32)
        column = col_turn[at, :]
        return (both[:, :width] + both[:, width:]) * jnp.concatenate(
            [column] * (width // TILE), axis=1
        )

    sibling = 2 * z + 1 - c
    near_copies, far_copies = {}, {}
    order = list(range(1, nz)) + [0]
    for step in order:
        near_send[step] = right_product(lax.rem(z + step, nz), 1 - c)
        near_copies[step] = remote(
            near_send.at[step], near_recv.at[step], sems[8].at[step], sems[9].at[step], "term", sibling
        )
        near_copies[step].start()
    next(left_steps)
    for step in order:
        there = lax.rem(z + step, nz)
        product = right_product(there, c)
        near_copies[step].wait()
        product = product + near_recv[step]
        if step == 0:
            own_right = product
            continue
        far_send[step] = encode(product)
        far_copies[step] = remote(
            far_send.at[step], far_recv.at[step], sems[10].at[step], sems[11].at[step], "term", 2 * there + c
        )
        far_copies[step].start()
    near_send[0] = own_right
    for _ in left_steps:
        pass
    inverse_kernel(gram_out, inverse_ref, work)
    whiten = inverse_ref[...]

    def finish_left(block, carry):
        at = pl.ds(pl.multiple_of(block * share, share), share)
        value = jnp.concatenate([decode(gathered[flow, block]) for flow in range(2)], axis=1)
        left_out[at, :] = precise(value, inverse_ref[...], ((1,), (1,))).astype(jnp.bfloat16)
        return carry

    lax.fori_loop(0, m, finish_left, 0)
    pieces = width // TILE
    weighted = jnp.concatenate(
        [gram_out[width - pieces + k : width - pieces + k + 1, :TILE] for k in range(pieces)], axis=1
    )
    lean = precise(jnp.broadcast_to(weighted, (8, width)), whiten, ((1,), (1,)))[0:1]
    total = near_send[0]
    for step in range(1, nz):
        far_copies[step].wait()
        total = total + decode(far_recv[step])
    block = precise(total, inverse_ref[...], ((1,), (1,))) - lean * (1.0 / docs_total)

    me = 2 * z + c
    right_parts[me] = encode(block)
    gram_in, gram_out = right_gram[:2]
    gram_in[...] = precise(block, block, ((0,), (0,))) * (1.0 / docs_total)
    for _ in gram_steps(*right_gram):
        pass
    far_copies = []
    for step in range(1, nz):
        copy = remote(
            right_parts.at[me],
            right_parts.at[me],
            sems[12].at[step],
            sems[13].at[step],
            "term",
            2 * lax.rem(z + step, nz) + c,
        )
        copy.start()
        far_copies.append(copy)
    copy = remote(
        right_parts.at[me], right_parts.at[me], sems[14].at[0], sems[15].at[0], "term", sibling
    )
    copy.start()
    near_copies = [copy]
    inverse_kernel(gram_out, inverse_ref, work)

    def finish_right(t):
        at = pl.ds(pl.multiple_of(t * piece, piece), piece)
        right_out[at, :] = precise(
            decode(right_parts[t]), inverse_ref[...], ((1,), (1,))
        ).astype(jnp.bfloat16)

    finish_right(me)
    for step in range(1, nz):
        far_copies[step - 1].wait()
        t = 2 * lax.rem(z - step + nz, nz) + c
        copy = remote(
            right_parts.at[t], right_parts.at[t], sems[14].at[step], sems[15].at[step], "term", sibling
        )
        copy.start()
        near_copies.append(copy)
        finish_right(t)
    for step, copy in enumerate(near_copies):
        copy.wait()
        finish_right(2 * lax.rem(z - step + nz, nz) + 1 - c)


def basis_stage(matrix, turned, start_block, row, col, weight, mean, identifier):
    n, m = lax.axis_size("term"), lax.axis_size("doc")
    nz = n // 2
    terms, docs, width = matrix.shape[0], turned.shape[0], start_block.shape[1]
    share, piece = terms // m, docs // n
    wide = max(grid_of(m))
    int16, f32, bf16 = jnp.int16, jnp.float32, jnp.bfloat16
    coded = pltpu.VMEM((2, m, share + 16, TILE), int16)
    coded_b = pltpu.VMEM((2, wide, share + 16, TILE), int16)
    far = pltpu.VMEM((nz, piece + 16, width), int16)
    near = pltpu.VMEM((nz, piece, width), f32)
    pairs = [pltpu.SemaphoreType.DMA((2, size)) for size in (m, m, wide, wide, wide, wide, m, m)]
    return pl.pallas_call(
        basis_kernel,
        out_shape=[
            jax.ShapeDtypeStruct((terms, width), bf16),
            jax.ShapeDtypeStruct((docs, width), bf16),
        ],
        in_specs=[VMEM] * 7,
        out_specs=[VMEM] * 2,
        scratch_shapes=[
            pltpu.VMEM((terms, TILE), f32),
            pltpu.VMEM((docs, TILE), f32),
            pltpu.VMEM((docs, width), bf16),
            pltpu.VMEM((m, share, width), f32),
            coded,
            coded,
            coded_b,
            coded_b,
            coded,
            pltpu.VMEM((terms, 2 * width), bf16),
            near,
            near,
            far,
            far,
            pltpu.VMEM((n, piece + 16, width), int16),
            pltpu.VMEM((width, width), f32),
            pltpu.VMEM((width, 2 * width), f32),
        ]
        + gram_scratch(width)
        + gram_scratch(width)
        + pairs
        + semaphores(*[nz] * 8),
        compiler_params=pltpu.CompilerParams(
            collective_id=identifier, has_side_effects=True, vmem_limit_bytes=58 << 20
        ),
        name="basis",
    )(matrix, turned, start_block, row, col, weight, mean)


def per_device(tile_values, tile_rows, tile_cols, tile_count, start_block):
    rows_out, cols_out, weights, means, matrix, turned = scale_stage(
        tile_values, tile_rows, tile_cols, tile_count, start_block, 0
    )
    left_basis, right_basis = basis_stage(
        matrix, turned, start_block, rows_out, cols_out, weights, means, 1
    )
    return (rows_out.reshape(-1), cols_out.reshape(-1), left_basis, right_basis)


def solution(mesh):
    placed = (
        P("term", "doc", None),
        P("term", "doc"),
        P("term", "doc"),
        P("term", "doc"),
        P("doc", None),
    )
    return jax.shard_map(
        per_device,
        mesh=mesh,
        in_specs=placed,
        out_specs=(P("term"), P("doc"), P("term", None), P("doc", None)),
        check_vma=False,
    )
```

```python
import math

import jax
import jax.numpy as jnp
from jax import lax
from jax.experimental import pallas as pl
from jax.experimental.pallas import tpu as pltpu
from jax.sharding import PartitionSpec as P

TILE = 128
RB = 16
CB = 16


PRECISE = lax.Precision.HIGHEST
MESH = pl.DeviceIdType.MESH
VMEM = pl.BlockSpec(memory_space=pltpu.VMEM)
SMEM = pl.BlockSpec(memory_space=pltpu.SMEM)


BLOCK = 64
GROUP = 8


def block_inverse(block, low, high):
    rows = lax.broadcasted_iota(jnp.int32, block.shape, 0)
    pivots = jnp.ones_like(block)
    for base in range(0, BLOCK, GROUP):
        factors = []
        for at in range(base, base + GROUP):
            column = jnp.broadcast_to(block[:, low + at : low + at + 1], block.shape)
            for past, factor in enumerate(factors):
                column = column - factor * column[base + past : base + past + 1, :]
            pivots = jnp.where(rows == at, column, pivots)
            ratio = column * (1.0 / column[at : at + 1, :])
            factors.append(jnp.where(rows > at, ratio, 0.0))
        for at, factor in enumerate(factors):
            block = block - factor * block[base + at : base + at + 1, :]
    lanes = lax.broadcasted_iota(jnp.int32, block.shape, 1)
    inside = (lanes >= high) & (lanes < high + BLOCK)
    return jnp.where(inside, block * lax.rsqrt(pivots), 0.0)


def inverse_kernel(gram_ref, o_ref, work):
    width = gram_ref.shape[0]
    work[:, :width] = gram_ref[...]
    rows = lax.broadcasted_iota(jnp.int32, (width, width), 0)
    lanes = lax.broadcasted_iota(jnp.int32, (width, width), 1)
    work[:, width:] = jnp.where(rows == lanes, 1.0, 0.0)
    for index in range(width // BLOCK):
        start = index * BLOCK
        near = start // TILE * TILE
        low = start - near
        high = TILE - BLOCK - low
        block = work[start : start + BLOCK, near : near + TILE]
        rows = lax.broadcasted_iota(jnp.int32, block.shape, 0)
        lanes = lax.broadcasted_iota(jnp.int32, block.shape, 1)
        inside = (lanes >= low) & (lanes < low + BLOCK)
        block = jnp.where(inside, block, jnp.where(lanes - high == rows, 1.0, 0.0))
        inverse = block_inverse(block, low, high)
        panel = work[start : start + BLOCK, :]
        solved = jnp.dot(
            inverse,
            jnp.concatenate([panel, panel], axis=0),
            precision=PRECISE,
            preferred_element_type=jnp.float32,
        )
        o_ref[start : start + BLOCK, :] = solved[:, width:]
        if start + BLOCK < width:
            update = lax.dot_general(
                solved[:, :width],
                solved,
                (((0,), (0,)), ((), ())),
                precision=PRECISE,
                preferred_element_type=jnp.float32,
            )
            work[start + BLOCK :, :] = work[start + BLOCK :, :] - update[start + BLOCK :, :]


def greet(axes):
    barrier = pltpu.get_barrier_semaphore()
    total = 0
    for axis in axes:
        n = lax.axis_size(axis)
        me = lax.axis_index(axis)
        for step in range(1, n):
            pl.semaphore_signal(
                barrier, inc=1, device_id={axis: lax.rem(me + step, n)}, device_id_type=MESH
            )
        total += n - 1
    pl.semaphore_wait(barrier, total)


def remote(source, target, send_sem, recv_sem, axis, peer):
    return pltpu.make_async_remote_copy(
        src_ref=source,
        dst_ref=target,
        send_sem=send_sem,
        recv_sem=recv_sem,
        device_id={axis: peer},
        device_id_type=MESH,
    )


def paired():
    n, me = lax.axis_size("term"), lax.axis_index("term")
    return n // 2, me // 2, lax.rem(me, 2)


def semaphores(*sizes):
    return [pltpu.SemaphoreType.DMA((size,)) for size in sizes]


def split3(value):
    high = value.astype(jnp.bfloat16)
    rest = value - high.astype(jnp.float32)
    middle = rest.astype(jnp.bfloat16)
    return high, middle, (rest - middle.astype(jnp.float32)).astype(jnp.bfloat16)


def spread(value, parts):
    high, middle, low = (part.astype(jnp.float32) for part in split3(value))
    blocks, depth, lanes = parts.shape
    rows = lax.broadcasted_iota(jnp.int32, (depth, lanes), 0)
    for block in range(blocks):
        at = slice(block, block + 1)
        picked = jnp.where(rows == 0, high[at], jnp.where(rows == 1, middle[at], low[at]))
        parts[block] = jnp.where(rows < 3, picked, 0.0).astype(jnp.bfloat16)


def tile_sums(tiles, source_ids, parts, sums, target, forward):
    slots = sums.shape[0]
    for slot in range(slots):
        product = lax.dot_general(
            parts[source_ids[slot]],
            tiles[slot],
            (((1,), (1 if forward else 0,)), ((), ())),
            preferred_element_type=jnp.float32,
        )
        sums[slot : slot + 1, :] = product[0:1] + product[1:2] + product[2:3]
    stacked = jnp.concatenate(split3(sums[...]), axis=0)
    return jnp.dot(target, stacked, preferred_element_type=jnp.float32)


def start_exchange(held, axis, send_sem, recv_sem):
    n, me = lax.axis_size(axis), lax.axis_index(axis)
    copies = []
    for step in range(1, n):
        copy = remote(
            held.at[0], held.at[step], send_sem.at[step], recv_sem.at[step], axis, lax.rem(me + step, n)
        )
        copy.start()
        copies.append(copy)
    return copies


def finish_exchange(copies, held, axis):
    n, me = lax.axis_size(axis), lax.axis_index(axis)
    for copy in copies:
        copy.wait()
    total = held[me]
    for source in range(1, n):
        total = total + held[lax.rem(me - source + n, n)]
    return total


def scale_phase(
    ids_hbm,
    live,
    tiles_hbm,
    start_hbm,
    row_ref,
    col_ref,
    weight_ref,
    mean_ref,
    start_ref,
    dense_ref,
    turned_ref,
    ids,
    tiles,
    flipped,
    parts,
    sums,
    held_a,
    held_b,
    held_c,
    held_d,
    held_e,
    load_sem,
    *sems,
):
    slots = tiles_hbm.shape[0]
    loads = [
        pltpu.make_async_copy(ids_hbm, ids, load_sem.at[0]),
        pltpu.make_async_copy(start_hbm, start_ref, load_sem.at[1]),
        pltpu.make_async_copy(tiles_hbm, tiles.at[pl.ds(0, slots)], load_sem.at[2]),
    ]
    for load in loads:
        load.start()
    greet(("term", "doc"))
    tiles[slots] = jnp.zeros(tiles.shape[1:], tiles.dtype)
    flipped[slots] = jnp.zeros(tiles.shape[1:], tiles.dtype)
    blocks = row_ref.shape[0]
    places = lax.broadcasted_iota(jnp.int32, (blocks, live.shape[1]), 0)
    to_rows = jnp.where(places == live[0:1, :], 1.0, 0.0).astype(jnp.bfloat16)
    to_cols = jnp.where(places == live[1:2, :], 1.0, 0.0).astype(jnp.bfloat16)
    row_ids, col_ids = ids.at[pl.ds(0, slots)], ids.at[pl.ds(slots, slots)]

    def build(out_ref, source, turn):
        def place_row(outer, carry):
            at = pl.multiple_of(outer * TILE, TILE)
            for inner in range(blocks):
                place = inner * blocks + outer if turn else outer * blocks + inner
                tile = source[ids[2 * slots + place]]
                out_ref[pl.ds(at, TILE), inner * TILE : (inner + 1) * TILE] = tile
            return carry

        lax.fori_loop(0, blocks, place_row, 0)

    def flip(slot, carry):
        flipped[slot] = tiles[slot].T
        return carry

    spread(jnp.ones(row_ref.shape, jnp.float32), parts)
    loads[0].wait()
    loads[1].wait()
    mean = jnp.sum(start_ref[...].astype(jnp.float32), axis=0, keepdims=True)
    loads[2].wait()
    held_a[0, :blocks, :] = tile_sums(tiles, col_ids, parts, sums, to_rows, True)
    extra = held_a.shape[1] - blocks
    pieces = [mean[:, at : at + TILE] for at in range(0, mean.shape[1], TILE)]
    pieces.append(jnp.zeros((extra - len(pieces), TILE), jnp.float32))
    held_a[0, blocks:, :] = jnp.concatenate(pieces, axis=0)
    copies = start_exchange(held_a, "doc", *sems[0:2])
    build(dense_ref, tiles, False)
    joined = finish_exchange(copies, held_a, "doc")
    mean_ref[...] = joined[blocks:, :]
    spread(1.0 / joined[:blocks], parts)

    held_b[0] = tile_sums(tiles, row_ids, parts, sums, to_cols, False)
    copies = start_exchange(held_b, "term", *sems[2:4])
    lax.fori_loop(0, slots, flip, 0)
    total = finish_exchange(copies, held_b, "term")
    spread(1.0 / total, parts)

    held_c[0] = tile_sums(tiles, col_ids, parts, sums, to_rows, True)
    copies = start_exchange(held_c, "doc", *sems[4:6])
    build(turned_ref, flipped, True)
    row_scale = 1.0 / finish_exchange(copies, held_c, "doc")
    row_ref[...] = row_scale
    spread(row_scale, parts)

    held_d[0] = tile_sums(tiles, row_ids, parts, sums, to_cols, False)
    copies = start_exchange(held_d, "term", *sems[6:8])
    col_scale = 1.0 / finish_exchange(copies, held_d, "term")
    col_ref[...] = col_scale
    spread(col_scale, parts)

    held_e[0] = tile_sums(tiles, col_ids, parts, sums, to_rows, True)
    return start_exchange(held_e, "doc", *sems[8:10])


def scale_scratch(terms, docs, width, slots, kind):
    m, n = lax.axis_size("doc"), lax.axis_size("term")
    vector = pltpu.VMEM((RB, TILE), jnp.float32)
    extra = -(-width // (8 * TILE)) * 8
    stack = pltpu.VMEM((slots + 1, TILE, TILE), kind)

    def held(count, more=0):
        return pltpu.VMEM((count, RB + more, TILE), jnp.float32)

    return [
        vector,
        pltpu.VMEM((extra, TILE), jnp.float32),
        pltpu.VMEM((docs, width), kind),
        pltpu.VMEM((terms, docs), kind),
        pltpu.VMEM((docs, terms), kind),
        pltpu.SMEM((2 * slots + RB * CB,), jnp.int32),
        stack,
        stack,
        pltpu.VMEM((RB, 16, TILE), jnp.bfloat16),
        pltpu.VMEM((slots, TILE), jnp.float32),
        held(m, extra),
        held(n),
        held(m),
        held(n),
        held(m),
        pltpu.SemaphoreType.DMA((3,)),
    ] + semaphores(m, m, n, n, m, m, n, n, m, m)


SCALE_REFS = 26


def tables(tile_rows, tile_cols, tile_count):
    slots = tile_rows.shape[1]
    slot = jnp.arange(slots, dtype=jnp.int32)
    used = slot < tile_count[0, 0]
    rows, cols = tile_rows[0], tile_cols[0]
    cell = jnp.arange(RB * CB, dtype=jnp.int32)
    found = ((rows * CB + cols)[None, :] == cell[:, None]) & used[None, :]
    lookup = slots + jnp.sum(jnp.where(found, slot[None, :] - slots, 0), axis=1)
    live = jnp.stack([jnp.where(used, rows, RB), jnp.where(used, cols, CB)])
    return jnp.concatenate([rows, cols, lookup]), jnp.concatenate([live, live, live], axis=1)


CODES = 32760.0
OCTAVE = 256.0 / math.log(2.0)


def encode(value):
    rows, lanes = value.shape
    groups = value.reshape(rows // 8, 8, lanes)
    top = jnp.maximum(jnp.max(jnp.abs(groups), axis=0), 1e-30)
    level = jnp.ceil(jnp.log(top) * OCTAVE)
    codes = jnp.round(groups * (jnp.exp(level * (-1.0 / OCTAVE)) * CODES))
    whole = jnp.concatenate([codes.reshape(rows, lanes), level, level], axis=0)
    return whole.astype(jnp.int32).astype(jnp.int16)


def decode(block):
    rows, lanes = block.shape[0] - 16, block.shape[1]
    value = block.astype(jnp.int32).astype(jnp.float32)
    scale = jnp.exp(value[rows : rows + 8] * (1.0 / OCTAVE)) * (1.0 / CODES)
    return (value[:rows].reshape(rows // 8, 8, lanes) * scale[None]).reshape(rows, lanes)


def grid_of(n):
    nx = int(math.isqrt(n))
    while n % nx:
        nx -= 1
    return nx, n // nx


def turn_out(vector_ref, block, lanes):
    row = jnp.broadcast_to(vector_ref[pl.ds(block, 1), :], (TILE, TILE))
    column = row.T
    return jnp.concatenate([column] * (lanes // TILE), axis=1)


def precise(a, b, dims):
    return lax.dot_general(
        a, b, (dims, ((), ())), precision=PRECISE, preferred_element_type=jnp.float32
    )


def gram_steps(x_ref, o_ref, near, mid, far, second, part, done, *sems):
    nz, z, c = paired()
    m, my = lax.axis_size("doc"), lax.axis_index("doc")
    rows = part.shape[0]
    sibling = 2 * z + 1 - c

    def share(ref, there, core):
        return ref.at[pl.ds(pl.multiple_of((2 * there + core) * rows, 8), rows)]

    near_copies, far_copies = {}, []
    for step in list(range(1, nz)) + [0]:
        there = lax.rem(z + step, nz)
        near_copies[step] = remote(
            share(x_ref, there, 1 - c), near.at[step], sems[0].at[step], sems[1].at[step], "term", sibling
        )
        near_copies[step].start()
    yield
    for step in range(1, nz):
        near_copies[step].wait()
        there = lax.rem(z + step, nz)
        mid[step] = share(x_ref, there, c)[...] + near[step]
        copy = remote(
            mid.at[step], far.at[step], sems[2].at[step], sems[3].at[step], "term", 2 * there + c
        )
        copy.start()
        far_copies.append(copy)
    near_copies[0].wait()
    part[...] = share(x_ref, z, c)[...] + near[0]
    yield
    for step, copy in enumerate(far_copies):
        copy.wait()
        part[...] += far[step + 1]
    copies = []
    for step in range(1, m):
        copy = remote(
            part, second.at[step], sems[4].at[step], sems[5].at[step], "doc", lax.rem(my + step, m)
        )
        copy.start()
        copies.append(copy)
    second[0] = part[...]
    yield
    for copy in copies:
        copy.wait()
    total = second[my]
    for source in range(1, m):
        total = total + second[lax.rem(my - source + m, m)]
    done[...] = total
    far_copies = []
    here = share(o_ref, z, c)
    for step in range(1, nz):
        copy = remote(
            done, here, sems[6].at[step], sems[7].at[step], "term", 2 * lax.rem(z + step, nz) + c
        )
        copy.start()
        far_copies.append(copy)
    copy = remote(done, here, sems[8].at[0], sems[9].at[0], "term", sibling)
    copy.start()
    near_copies = [copy]
    here[...] = total
    yield
    for step in range(1, nz):
        far_copies[step - 1].wait()
        there = share(o_ref, lax.rem(z - step + nz, nz), c)
        copy = remote(there, there, sems[8].at[step], sems[9].at[step], "term", sibling)
        copy.start()
        near_copies.append(copy)
    for copy in near_copies:
        copy.wait()


def gram_scratch(width):
    nz, m = lax.axis_size("term") // 2, lax.axis_size("doc")
    rows = width // (2 * nz)
    spread_over = pltpu.VMEM((nz, rows, width), jnp.float32)
    alone = pltpu.VMEM((rows, width), jnp.float32)
    whole = pltpu.VMEM((width, width), jnp.float32)
    return [whole, whole] + [spread_over] * 3 + [pltpu.VMEM((m, rows, width), jnp.float32), alone, alone] + semaphores(
        nz, nz, nz, nz, m, m, nz, nz, nz, nz
    )


GRAM_REFS = 18


def whole_kernel(
    ids_hbm,
    live,
    tiles_hbm,
    start_hbm,
    row_ref,
    col_ref,
    left_out,
    right_out,
    row_turn,
    col_turn,
    scaled,
    partial,
    send_a,
    recv_a,
    send_b,
    recv_b,
    gathered,
    factor,
    near_send,
    near_recv,
    far_send,
    far_recv,
    right_parts,
    inverse_ref,
    work,
    *rest,
):
    left_gram, right_gram = rest[:GRAM_REFS], rest[GRAM_REFS : 2 * GRAM_REFS]
    scale_refs = rest[2 * GRAM_REFS : 2 * GRAM_REFS + SCALE_REFS]
    weight_ref, mean_ref, start_ref, matrix, turned = scale_refs[:5]
    held_e = scale_refs[14]
    sems = rest[2 * GRAM_REFS + SCALE_REFS :]
    n, m = lax.axis_size("term"), lax.axis_size("doc")
    nz, z, c = paired()
    doc = lax.axis_index("doc")
    nx, ny = grid_of(m)
    x, y = lax.rem(doc, nx), doc // nx
    terms, width = left_out.shape
    docs = right_out.shape[0]
    share, piece = terms // m, docs // n
    docs_total = docs * m

    weight_copies = scale_phase(
        ids_hbm, live, tiles_hbm, start_hbm, row_ref, col_ref, *scale_refs
    )

    def axes(flow):
        return (x, nx, y, ny) if flow == 0 else (y, ny, x, nx)

    def device(flow, first, second):
        return second * nx + first if flow == 0 else first * nx + second

    def lanes(flow):
        return slice(flow * TILE, (flow + 1) * TILE)

    def prepare(block, carry):
        at = pl.ds(pl.multiple_of(block * TILE, TILE), TILE)
        column = turn_out(col_ref, block, width)
        col_turn[at, :] = column[:, :TILE]
        scaled[at, :] = (column * start_ref[at, :].astype(jnp.float32)).astype(jnp.bfloat16)
        row_turn[at, :] = turn_out(row_ref, block, TILE)
        return carry

    lax.fori_loop(0, docs // TILE, prepare, 0)

    steps = [(dx, dy) for dx in range(nx) for dy in range(ny)]
    steps.sort(key=lambda s: -((s[0] > 0) + (s[1] > 0)))
    copies_a, copies_b = {}, {}
    for dx, dy in steps:
        target = lax.rem(y + dy, ny) * nx + lax.rem(x + dx, nx)
        at = pl.ds(pl.multiple_of(target * share, share), share)
        product = jnp.dot(matrix[at, :], scaled[...], preferred_element_type=jnp.float32)
        column = row_turn[at, :]
        product = product * jnp.concatenate([column] * (width // TILE), axis=1)
        partial[dy * nx + dx] = product
        for flow in range(2):
            a, n1, b, n2 = axes(flow)
            s1, s2 = (dx, dy) if flow == 0 else (dy, dx)
            if s1 == 0:
                continue
            slot = s1 * n2 + s2
            send_a[flow, slot] = encode(product[:, lanes(flow)])
            copies_a[flow, s1, s2] = remote(
                send_a.at[flow, slot],
                recv_a.at[flow, slot],
                sems[0].at[flow, slot],
                sems[1].at[flow, slot],
                "doc",
                device(flow, lax.rem(a + s1, n1), b),
            )
            copies_a[flow, s1, s2].start()

    def own(flow, s2):
        dx, dy = (0, s2) if flow == 0 else (s2, 0)
        return partial[dy * nx + dx, :, lanes(flow)]

    def landed(flow, s2):
        a, n1, b, n2 = axes(flow)
        total = own(flow, s2)
        for s1 in range(1, n1):
            copies_a[flow, s1, s2].wait()
            total = total + decode(recv_a[flow, s1 * n2 + s2])
        return total

    for flow in range(2):
        a, n1, b, n2 = axes(flow)
        for s2 in range(1, n2):
            send_b[flow, s2] = encode(landed(flow, s2))
            copies_b[flow, s2] = remote(
                send_b.at[flow, s2],
                recv_b.at[flow, s2],
                sems[2].at[flow, s2],
                sems[3].at[flow, s2],
                "doc",
                device(flow, a, lax.rem(b + s2, n2)),
            )
            copies_b[flow, s2].start()

    weight_ref[...] = row_ref[...] * finish_exchange(weight_copies, held_e, "doc")
    blocks_of_share = share // TILE
    weight = jnp.concatenate(
        [turn_out(weight_ref, doc * blocks_of_share + k, TILE) for k in range(blocks_of_share)], axis=0
    )
    copies_c, copies_d = {}, {}
    left = []
    for flow in range(2):
        a, n1, b, n2 = axes(flow)
        total = landed(flow, 0)
        for s2 in range(1, n2):
            copies_b[flow, s2].wait()
            total = total + decode(recv_b[flow, s2])
        total = total - weight * (mean_ref[flow : flow + 1, :] * (1.0 / docs_total))
        left.append(total)
        gathered[flow, doc] = encode(total)
        for s1 in range(1, n1):
            copies_c[flow, s1] = remote(
                gathered.at[flow, doc],
                gathered.at[flow, doc],
                sems[4].at[flow, s1],
                sems[5].at[flow, s1],
                "doc",
                device(flow, lax.rem(a + s1, n1), b),
            )
            copies_c[flow, s1].start()

    left_share = jnp.concatenate(left, axis=1)
    gram_in, gram_out = left_gram[:2]
    gram_in[...] = precise(left_share, left_share, ((0,), (0,))) * (1.0 / (terms * n))
    for k in range(width // TILE):
        weighted = jnp.sum(weight * left[k], axis=0, keepdims=True)
        gram_in[width - width // TILE + k : width - width // TILE + k + 1, :TILE] = weighted
    left_steps = gram_steps(*left_gram)
    next(left_steps)

    for flow in range(2):
        a, n1, b, n2 = axes(flow)
        for s1 in range(n1):
            if s1:
                copies_c[flow, s1].wait()
            source = device(flow, lax.rem(a - s1 + n1, n1), b)
            for s2 in range(1, n2):
                copies_d[flow, s1, s2] = remote(
                    gathered.at[flow, source],
                    gathered.at[flow, source],
                    sems[6].at[flow, s1 * n2 + s2],
                    sems[7].at[flow, s1 * n2 + s2],
                    "doc",
                    device(flow, a, lax.rem(b + s2, n2)),
                )
                copies_d[flow, s1, s2].start()
    next(left_steps)
    next(left_steps)
    for copy in copies_d.values():
        copy.wait()

    def unpack(block, carry):
        at = pl.ds(pl.multiple_of(block * share, share), share)
        for flow in range(2):
            value = decode(gathered[flow, block]) * row_turn[at, :]
            high = value.astype(jnp.bfloat16)
            factor[at, lanes(flow)] = high
            low = slice(width + flow * TILE, width + (flow + 1) * TILE)
            factor[at, low] = (value - high.astype(jnp.float32)).astype(jnp.bfloat16)
        return carry

    lax.fori_loop(0, m, unpack, 0)

    def right_product(there, core):
        at = pl.ds(pl.multiple_of((2 * there + core) * piece, piece), piece)
        both = jnp.dot(turned[at, :], factor[...], preferred_element_type=jnp.float32)
        column = col_turn[at, :]
        return (both[:, :width] + both[:, width:]) * jnp.concatenate(
            [column] * (width // TILE), axis=1
        )

    sibling = 2 * z + 1 - c
    near_copies, far_copies = {}, {}
    order = list(range(1, nz)) + [0]
    for step in order:
        near_send[step] = right_product(lax.rem(z + step, nz), 1 - c)
        near_copies[step] = remote(
            near_send.at[step], near_recv.at[step], sems[8].at[step], sems[9].at[step], "term", sibling
        )
        near_copies[step].start()
    next(left_steps)
    for step in order:
        there = lax.rem(z + step, nz)
        product = right_product(there, c)
        near_copies[step].wait()
        product = product + near_recv[step]
        if step == 0:
            own_right = product
            continue
        far_send[step] = encode(product)
        far_copies[step] = remote(
            far_send.at[step], far_recv.at[step], sems[10].at[step], sems[11].at[step], "term", 2 * there + c
        )
        far_copies[step].start()
    near_send[0] = own_right
    for _ in left_steps:
        pass
    inverse_kernel(gram_out, inverse_ref, work)
    whiten = inverse_ref[...]

    def finish_left(block, carry):
        at = pl.ds(pl.multiple_of(block * share, share), share)
        value = jnp.concatenate([decode(gathered[flow, block]) for flow in range(2)], axis=1)
        left_out[at, :] = precise(value, inverse_ref[...], ((1,), (1,))).astype(jnp.bfloat16)
        return carry

    lax.fori_loop(0, m, finish_left, 0)
    pieces = width // TILE
    weighted = jnp.concatenate(
        [gram_out[width - pieces + k : width - pieces + k + 1, :TILE] for k in range(pieces)], axis=1
    )
    lean = precise(jnp.broadcast_to(weighted, (8, width)), whiten, ((1,), (1,)))[0:1]
    total = near_send[0]
    for step in range(1, nz):
        far_copies[step].wait()
        total = total + decode(far_recv[step])
    block = precise(total, inverse_ref[...], ((1,), (1,))) - lean * (1.0 / docs_total)

    me = 2 * z + c
    right_parts[me] = encode(block)
    gram_in, gram_out = right_gram[:2]
    gram_in[...] = precise(block, block, ((0,), (0,))) * (1.0 / docs_total)
    for _ in gram_steps(*right_gram):
        pass
    far_copies = []
    for step in range(1, nz):
        copy = remote(
            right_parts.at[me],
            right_parts.at[me],
            sems[12].at[step],
            sems[13].at[step],
            "term",
            2 * lax.rem(z + step, nz) + c,
        )
        copy.start()
        far_copies.append(copy)
    copy = remote(
        right_parts.at[me], right_parts.at[me], sems[14].at[0], sems[15].at[0], "term", sibling
    )
    copy.start()
    near_copies = [copy]
    inverse_kernel(gram_out, inverse_ref, work)

    def finish_right(t):
        at = pl.ds(pl.multiple_of(t * piece, piece), piece)
        right_out[at, :] = precise(
            decode(right_parts[t]), inverse_ref[...], ((1,), (1,))
        ).astype(jnp.bfloat16)

    finish_right(me)
    for step in range(1, nz):
        far_copies[step - 1].wait()
        t = 2 * lax.rem(z - step + nz, nz) + c
        copy = remote(
            right_parts.at[t], right_parts.at[t], sems[14].at[step], sems[15].at[step], "term", sibling
        )
        copy.start()
        near_copies.append(copy)
        finish_right(t)
    for step, copy in enumerate(near_copies):
        copy.wait()
        finish_right(2 * lax.rem(z - step + nz, nz) + 1 - c)


def emit_kernel(row_ref, col_ref, left_ref, right_ref, *rest):
    outs, sems = rest[:4], rest[4]
    copies = [
        pltpu.make_async_copy(source, target, sems.at[k])
        for k, (source, target) in enumerate(zip((row_ref, col_ref, left_ref, right_ref), outs))
    ]
    for copy in copies:
        copy.start()
    for copy in copies:
        copy.wait()


def emit(arrays):
    return pl.pallas_call(
        emit_kernel,
        out_shape=[jax.ShapeDtypeStruct(x.shape, x.dtype) for x in arrays],
        in_specs=[VMEM] * 4,
        out_specs=[pl.BlockSpec(memory_space=pl.ANY)] * 4,
        scratch_shapes=[pltpu.SemaphoreType.DMA((4,))],
        name="emit",
    )(*arrays)


def per_device(tile_values, tile_rows, tile_cols, tile_count, start_block):
    n, m = lax.axis_size("term"), lax.axis_size("doc")
    nz = n // 2
    terms, (docs, width) = RB * TILE, start_block.shape
    share, piece = terms // m, docs // n
    wide = max(grid_of(m))
    int16, f32, bf16 = jnp.int16, jnp.float32, jnp.bfloat16
    coded = pltpu.VMEM((2, m, share + 16, TILE), int16)
    coded_b = pltpu.VMEM((2, wide, share + 16, TILE), int16)
    far = pltpu.VMEM((nz, piece + 16, width), int16)
    near = pltpu.VMEM((nz, piece, width), f32)
    pairs = [pltpu.SemaphoreType.DMA((2, size)) for size in (m, m, wide, wide, wide, wide, m, m)]
    vector = jax.ShapeDtypeStruct((RB, TILE), f32)
    hbm = pl.BlockSpec(memory_space=pl.ANY)
    ids, live = tables(tile_rows, tile_cols, tile_count)
    outs = pl.pallas_call(
        whole_kernel,
        out_shape=[
            vector,
            vector,
            jax.ShapeDtypeStruct((terms, width), bf16),
            jax.ShapeDtypeStruct((docs, width), bf16),
        ],
        in_specs=[hbm, VMEM, hbm, hbm],
        out_specs=[VMEM] * 4,
        scratch_shapes=[
            pltpu.VMEM((terms, TILE), f32),
            pltpu.VMEM((docs, TILE), f32),
            pltpu.VMEM((docs, width), bf16),
            pltpu.VMEM((m, share, width), f32),
            coded,
            coded,
            coded_b,
            coded_b,
            coded,
            pltpu.VMEM((terms, 2 * width), bf16),
            near,
            near,
            far,
            far,
            pltpu.VMEM((n, piece + 16, width), int16),
            pltpu.VMEM((width, width), f32),
            pltpu.VMEM((width, 2 * width), f32),
        ]
        + gram_scratch(width)
        + gram_scratch(width)
        + scale_scratch(terms, docs, width, tile_values.shape[0], tile_values.dtype)
        + pairs
        + semaphores(*[nz] * 8),
        compiler_params=pltpu.CompilerParams(
            collective_id=0, has_side_effects=True, vmem_limit_bytes=44 << 20
        ),
        name="whole",
    )(ids, live, tile_values, start_block)
    row, col, left_basis, right_basis = emit(outs)
    return (row.reshape(-1), col.reshape(-1), left_basis, right_basis)


def solution(mesh):
    placed = (
        P("term", "doc", None),
        P("term", "doc"),
        P("term", "doc"),
        P("term", "doc"),
        P("doc", None),
    )
    return jax.shard_map(
        per_device,
        mesh=mesh,
        in_specs=placed,
        out_specs=(P("term"), P("doc"), P("term", None), P("doc", None)),
        check_vma=False,
    )
```

```python
import math

import jax
import jax.numpy as jnp
from jax import lax
from jax.experimental import pallas as pl
from jax.experimental.pallas import tpu as pltpu
from jax.sharding import PartitionSpec as P

TILE = 128
RB = 16
CB = 16


PRECISE = lax.Precision.HIGHEST
MESH = pl.DeviceIdType.MESH
VMEM = pl.BlockSpec(memory_space=pltpu.VMEM)
SMEM = pl.BlockSpec(memory_space=pltpu.SMEM)


BLOCK = 64
GROUP = 8


def block_inverse(block, low, high):
    rows = lax.broadcasted_iota(jnp.int32, block.shape, 0)
    pivots = jnp.ones_like(block)
    for base in range(0, BLOCK, GROUP):
        factors = []
        for at in range(base, base + GROUP):
            column = jnp.broadcast_to(block[:, low + at : low + at + 1], block.shape)
            for past, factor in enumerate(factors):
                column = column - factor * column[base + past : base + past + 1, :]
            pivots = jnp.where(rows == at, column, pivots)
            ratio = column * (1.0 / column[at : at + 1, :])
            factors.append(jnp.where(rows > at, ratio, 0.0))
        for at, factor in enumerate(factors):
            block = block - factor * block[base + at : base + at + 1, :]
    lanes = lax.broadcasted_iota(jnp.int32, block.shape, 1)
    inside = (lanes >= high) & (lanes < high + BLOCK)
    return jnp.where(inside, block * lax.rsqrt(pivots), 0.0)


def inverse_kernel(gram_ref, o_ref, work):
    width = gram_ref.shape[0]
    work[:, :width] = gram_ref[...]
    rows = lax.broadcasted_iota(jnp.int32, (width, width), 0)
    lanes = lax.broadcasted_iota(jnp.int32, (width, width), 1)
    work[:, width:] = jnp.where(rows == lanes, 1.0, 0.0)
    for index in range(width // BLOCK):
        start = index * BLOCK
        near = start // TILE * TILE
        low = start - near
        high = TILE - BLOCK - low
        block = work[start : start + BLOCK, near : near + TILE]
        rows = lax.broadcasted_iota(jnp.int32, block.shape, 0)
        lanes = lax.broadcasted_iota(jnp.int32, block.shape, 1)
        inside = (lanes >= low) & (lanes < low + BLOCK)
        block = jnp.where(inside, block, jnp.where(lanes - high == rows, 1.0, 0.0))
        inverse = block_inverse(block, low, high)
        panel = work[start : start + BLOCK, :]
        solved = jnp.dot(
            inverse,
            jnp.concatenate([panel, panel], axis=0),
            precision=PRECISE,
            preferred_element_type=jnp.float32,
        )
        o_ref[start : start + BLOCK, :] = solved[:, width:]
        if start + BLOCK < width:
            update = lax.dot_general(
                solved[:, :width],
                solved,
                (((0,), (0,)), ((), ())),
                precision=PRECISE,
                preferred_element_type=jnp.float32,
            )
            work[start + BLOCK :, :] = work[start + BLOCK :, :] - update[start + BLOCK :, :]


def greet():
    barrier = pltpu.get_barrier_semaphore()
    n, m = lax.axis_size("term"), lax.axis_size("doc")
    me, doc = lax.axis_index("term"), lax.axis_index("doc")
    peers = [{"term": lax.rem(me + step, n)} for step in range(1, n)]
    for step in range(1, m):
        there = lax.rem(doc + step, m)
        peers += [{"doc": there}, {"doc": there, "term": me + 1 - 2 * lax.rem(me, 2)}]
    for peer in peers:
        pl.semaphore_signal(barrier, inc=1, device_id=peer, device_id_type=MESH)
    pl.semaphore_wait(barrier, len(peers))


def remote(source, target, send_sem, recv_sem, axis, peer):
    return pltpu.make_async_remote_copy(
        src_ref=source,
        dst_ref=target,
        send_sem=send_sem,
        recv_sem=recv_sem,
        device_id=axis if peer is None else {axis: peer},
        device_id_type=MESH,
    )


def paired():
    n, me = lax.axis_size("term"), lax.axis_index("term")
    return n // 2, me // 2, lax.rem(me, 2)


def semaphores(*sizes):
    return [pltpu.SemaphoreType.DMA((size,)) for size in sizes]


def split3(value):
    high = value.astype(jnp.bfloat16)
    rest = value - high.astype(jnp.float32)
    middle = rest.astype(jnp.bfloat16)
    return high, middle, (rest - middle.astype(jnp.float32)).astype(jnp.bfloat16)


def spread(value, parts):
    high, middle, low = (part.astype(jnp.float32) for part in split3(value))
    blocks, depth, lanes = parts.shape
    rows = lax.broadcasted_iota(jnp.int32, (depth, lanes), 0)
    for block in range(blocks):
        at = slice(block, block + 1)
        picked = jnp.where(rows == 0, high[at], jnp.where(rows == 1, middle[at], low[at]))
        parts[block] = jnp.where(rows < 3, picked, 0.0).astype(jnp.bfloat16)


def tile_sums(tiles, source_ids, parts, sums, target, forward):
    slots = sums.shape[0]
    for slot in range(slots):
        product = lax.dot_general(
            parts[source_ids[slot]],
            tiles[slot],
            (((1,), (1 if forward else 0,)), ((), ())),
            preferred_element_type=jnp.float32,
        )
        sums[slot : slot + 1, :] = product[0:1] + product[1:2] + product[2:3]
    stacked = jnp.concatenate(split3(sums[...]), axis=0)
    return jnp.dot(target, stacked, preferred_element_type=jnp.float32)


def start_exchange(held, axis, send_sem, recv_sem):
    n, me = lax.axis_size(axis), lax.axis_index(axis)
    copies = []
    for step in range(1, n):
        copy = remote(
            held.at[0], held.at[step], send_sem.at[step], recv_sem.at[step], axis, lax.rem(me + step, n)
        )
        copy.start()
        copies.append(copy)
    return copies


def finish_exchange(copies, held, axis):
    n, me = lax.axis_size(axis), lax.axis_index(axis)
    for copy in copies:
        copy.wait()
    total = held[me]
    for source in range(1, n):
        total = total + held[lax.rem(me - source + n, n)]
    return total


def scale_phase(
    meanwhile,
    ids_hbm,
    live,
    tiles_hbm,
    start_hbm,
    row_ref,
    col_ref,
    weight_ref,
    mean_ref,
    start_ref,
    dense_ref,
    turned_ref,
    ids,
    tiles,
    flipped,
    parts,
    sums,
    held_a,
    held_b,
    held_c,
    held_d,
    held_e,
    load_sem,
    *sems,
):
    slots = tiles_hbm.shape[0]
    loads = [
        pltpu.make_async_copy(ids_hbm, ids, load_sem.at[0]),
        pltpu.make_async_copy(start_hbm, start_ref, load_sem.at[1]),
        pltpu.make_async_copy(tiles_hbm, tiles.at[pl.ds(0, slots)], load_sem.at[2]),
    ]
    for load in loads:
        load.start()
    greet()
    tiles[slots] = jnp.zeros(tiles.shape[1:], tiles.dtype)
    flipped[slots] = jnp.zeros(tiles.shape[1:], tiles.dtype)
    blocks = row_ref.shape[0]
    places = lax.broadcasted_iota(jnp.int32, (blocks, live.shape[1]), 0)
    to_rows = jnp.where(places == live[0:1, :], 1.0, 0.0).astype(jnp.bfloat16)
    to_cols = jnp.where(places == live[1:2, :], 1.0, 0.0).astype(jnp.bfloat16)
    row_ids, col_ids = ids.at[pl.ds(0, slots)], ids.at[pl.ds(slots, slots)]

    def build(out_ref, source, turn):
        def place_row(outer, carry):
            at = pl.multiple_of(outer * TILE, TILE)
            for inner in range(blocks):
                place = inner * blocks + outer if turn else outer * blocks + inner
                tile = source[ids[2 * slots + place]]
                out_ref[pl.ds(at, TILE), inner * TILE : (inner + 1) * TILE] = tile
            return carry

        lax.fori_loop(0, blocks, place_row, 0)

    def flip(slot, carry):
        flipped[slot] = tiles[slot].T
        return carry

    spread(jnp.ones(row_ref.shape, jnp.float32), parts)
    loads[0].wait()
    loads[1].wait()
    mean = jnp.sum(start_ref[...].astype(jnp.float32), axis=0, keepdims=True)
    loads[2].wait()
    held_a[0, :blocks, :] = tile_sums(tiles, col_ids, parts, sums, to_rows, True)
    extra = held_a.shape[1] - blocks
    pieces = [mean[:, at : at + TILE] for at in range(0, mean.shape[1], TILE)]
    pieces.append(jnp.zeros((extra - len(pieces), TILE), jnp.float32))
    held_a[0, blocks:, :] = jnp.concatenate(pieces, axis=0)
    copies = start_exchange(held_a, "doc", *sems[0:2])
    build(dense_ref, tiles, False)
    joined = finish_exchange(copies, held_a, "doc")
    mean_ref[...] = joined[blocks:, :]
    spread(1.0 / joined[:blocks], parts)

    held_b[0] = tile_sums(tiles, row_ids, parts, sums, to_cols, False)
    copies = start_exchange(held_b, "term", *sems[2:4])
    lax.fori_loop(0, slots, flip, 0)
    total = finish_exchange(copies, held_b, "term")
    spread(1.0 / total, parts)

    held_c[0] = tile_sums(tiles, col_ids, parts, sums, to_rows, True)
    copies = start_exchange(held_c, "doc", *sems[4:6])
    build(turned_ref, flipped, True)
    row_scale = 1.0 / finish_exchange(copies, held_c, "doc")
    row_ref[...] = row_scale
    spread(row_scale, parts)

    held_d[0] = tile_sums(tiles, row_ids, parts, sums, to_cols, False)
    copies = start_exchange(held_d, "term", *sems[6:8])
    meanwhile()
    col_ref[...] = 1.0 / finish_exchange(copies, held_d, "term")

    def weigh():
        spread(col_ref[...], parts)
        held_e[0] = tile_sums(tiles, col_ids, parts, sums, to_rows, True)
        return start_exchange(held_e, "doc", *sems[8:10])

    return weigh


def scale_scratch(terms, docs, width, slots, kind):
    m, n = lax.axis_size("doc"), lax.axis_size("term")
    vector = pltpu.VMEM((RB, TILE), jnp.float32)
    extra = -(-width // (8 * TILE)) * 8
    stack = pltpu.VMEM((slots + 1, TILE, TILE), kind)

    def held(count, more=0):
        return pltpu.VMEM((count, RB + more, TILE), jnp.float32)

    return [
        vector,
        pltpu.VMEM((extra, TILE), jnp.float32),
        pltpu.VMEM((docs, width), kind),
        pltpu.VMEM((terms, docs), kind),
        pltpu.VMEM((docs, terms), kind),
        pltpu.SMEM((2 * slots + RB * CB,), jnp.int32),
        stack,
        stack,
        pltpu.VMEM((RB, 16, TILE), jnp.bfloat16),
        pltpu.VMEM((slots, TILE), jnp.float32),
        held(m, extra),
        held(n),
        held(m),
        held(n),
        held(m),
        pltpu.SemaphoreType.DMA((3,)),
    ] + semaphores(m, m, n, n, m, m, n, n, m, m)


SCALE_REFS = 26


def tables(tile_rows, tile_cols, tile_count):
    slots = tile_rows.shape[1]
    slot = jnp.arange(slots, dtype=jnp.int32)
    used = slot < tile_count[0, 0]
    rows, cols = tile_rows[0], tile_cols[0]
    cell = jnp.arange(RB * CB, dtype=jnp.int32)
    found = ((rows * CB + cols)[None, :] == cell[:, None]) & used[None, :]
    lookup = slots + jnp.sum(jnp.where(found, slot[None, :] - slots, 0), axis=1)
    live = jnp.stack([jnp.where(used, rows, RB), jnp.where(used, cols, CB)])
    return jnp.concatenate([rows, cols, lookup]), jnp.concatenate([live, live, live], axis=1)


CODES = 32760.0
OCTAVE = 256.0 / math.log(2.0)


def encode(value):
    rows, lanes = value.shape
    groups = value.reshape(rows // 8, 8, lanes)
    top = jnp.maximum(jnp.max(jnp.abs(groups), axis=0), 1e-30)
    level = jnp.ceil(jnp.log(top) * OCTAVE)
    codes = jnp.round(groups * (jnp.exp(level * (-1.0 / OCTAVE)) * CODES))
    whole = jnp.concatenate([codes.reshape(rows, lanes), level, level], axis=0)
    return whole.astype(jnp.int32).astype(jnp.int16)


def decode(block):
    rows, lanes = block.shape[0] - 16, block.shape[1]
    value = block.astype(jnp.int32).astype(jnp.float32)
    scale = jnp.exp(value[rows : rows + 8] * (1.0 / OCTAVE)) * (1.0 / CODES)
    return (value[:rows].reshape(rows // 8, 8, lanes) * scale[None]).reshape(rows, lanes)


def grid_of(n):
    nx = int(math.isqrt(n))
    while n % nx:
        nx -= 1
    return nx, n // nx


def turn_out(vector_ref, block, lanes):
    row = jnp.broadcast_to(vector_ref[pl.ds(block, 1), :], (TILE, TILE))
    column = row.T
    return jnp.concatenate([column] * (lanes // TILE), axis=1)


def precise(a, b, dims):
    return lax.dot_general(
        a, b, (dims, ((), ())), precision=PRECISE, preferred_element_type=jnp.float32
    )


def pack_gram(gram, extras, packed):
    groups, rows = packed.shape[0], packed.shape[1] - 8
    row = lax.broadcasted_iota(jnp.int32, (TILE, TILE), 0)
    lane = lax.broadcasted_iota(jnp.int32, (TILE, TILE), 1)
    last = gram[TILE:, TILE:]
    packed_rows = [jnp.where(row <= lane, gram[:TILE, :TILE], last), gram[:TILE, TILE:]]
    packed_rows = jnp.concatenate(packed_rows, axis=0)
    diagonal = jnp.sum(jnp.where(row == lane, last, 0.0), axis=0, keepdims=True)
    extras = [diagonal] + extras
    extras.append(jnp.zeros((8 - len(extras), TILE), jnp.float32))
    for group in range(groups):
        packed[group, :rows, :] = packed_rows[group * rows : (group + 1) * rows]
        packed[group, rows:, :] = (
            jnp.concatenate(extras, axis=0) if group == 0 else jnp.zeros((8, TILE), jnp.float32)
        )


def unpack_gram(packed, gram):
    rows = packed.shape[1] - 8
    row = lax.broadcasted_iota(jnp.int32, (TILE, TILE), 0)
    lane = lax.broadcasted_iota(jnp.int32, (TILE, TILE), 1)
    half = packed.shape[0] // 2
    both = jnp.concatenate([packed[g, :rows, :] for g in range(half)], axis=0)
    cross = jnp.concatenate([packed[half + g, :rows, :] for g in range(half)], axis=0)
    other = both.T
    gram[:TILE, :TILE] = jnp.where(row <= lane, both, other)
    gram[:TILE, TILE:] = cross
    gram[TILE:, :TILE] = jnp.zeros((TILE, TILE), jnp.float32)
    diagonal = jnp.broadcast_to(packed[0, rows : rows + 1, :], (TILE, TILE))
    last = jnp.where(row > lane, both, jnp.where(row == lane, diagonal, other))
    gram[TILE:, TILE:] = last


def gram_steps(x_ref, o_ref, landing, held, *sems):
    nz, z, c = paired()
    m, my = lax.axis_size("doc"), lax.axis_index("doc")
    steps = [(step, flip) for step in range(m) for flip in range(2) if step or flip]

    def peer(step, flip):
        there = lax.rem(my + step, m)
        core = 1 - c if flip else c
        return 2 * there + core, {"doc": there, "term": 2 * z + core}

    def exchange(source, target, send_sem, recv_sem):
        copies = []
        for step, flip in steps:
            group, place = peer(step, flip)
            slot = 2 * step + flip
            copy = remote(
                source(group), target(slot), send_sem.at[slot], recv_sem.at[slot], place, None
            )
            copy.start()
            copies.append(copy)
        return copies

    mine = 2 * my + c
    copies = exchange(lambda g: x_ref.at[g], lambda k: landing.at[k], *sems[0:2])
    yield
    total = x_ref[mine]
    for (step, flip), copy in zip(steps, copies):
        copy.wait()
        total = total + landing[2 * step + flip]
    held[0] = total
    copies = []
    for step in range(1, nz):
        copy = remote(
            held.at[0], held.at[step], sems[2].at[step], sems[3].at[step], "term", 2 * lax.rem(z + step, nz) + c
        )
        copy.start()
        copies.append(copy)
    yield
    for copy in copies:
        copy.wait()
    total = held[z]
    for source in range(1, nz):
        total = total + held[lax.rem(z - source + nz, nz)]
    o_ref[mine] = total
    copies = exchange(lambda g: o_ref.at[mine], lambda k: o_ref.at[mine], *sems[4:6])
    yield
    for copy in copies:
        copy.wait()


def gram_scratch():
    nz, m = lax.axis_size("term") // 2, lax.axis_size("doc")
    rows = TILE // m + 8
    packed = pltpu.VMEM((2 * m, rows, TILE), jnp.float32)
    return [packed, packed, packed, pltpu.VMEM((nz, rows, TILE), jnp.float32)] + semaphores(
        2 * m, 2 * m, nz, nz, 2 * m, 2 * m
    )


GRAM_REFS = 10


def whole_kernel(
    ids_hbm,
    live,
    tiles_hbm,
    start_hbm,
    row_ref,
    col_ref,
    left_out,
    right_out,
    row_turn,
    col_turn,
    scaled,
    partial,
    send_a,
    recv_a,
    send_b,
    recv_b,
    gathered,
    factor,
    near_send,
    near_recv,
    far_send,
    far_recv,
    right_parts,
    inverse_ref,
    halves,
    gram,
    work,
    *rest,
):
    left_gram, right_gram = rest[:GRAM_REFS], rest[GRAM_REFS : 2 * GRAM_REFS]
    scale_refs = rest[2 * GRAM_REFS : 2 * GRAM_REFS + SCALE_REFS]
    weight_ref, mean_ref, start_ref, matrix, turned = scale_refs[:5]
    held_e = scale_refs[14]
    sems = rest[2 * GRAM_REFS + SCALE_REFS :]
    n, m = lax.axis_size("term"), lax.axis_size("doc")
    nz, z, c = paired()
    doc = lax.axis_index("doc")
    nx, ny = grid_of(m)
    x, y = lax.rem(doc, nx), doc // nx
    terms, width = left_out.shape
    docs = right_out.shape[0]
    share, piece = terms // m, docs // n
    docs_total = docs * m

    def turn_rows():
        def turn(block, carry):
            at = pl.ds(pl.multiple_of(block * TILE, TILE), TILE)
            row_turn[at, :] = turn_out(row_ref, block, TILE)
            return carry

        lax.fori_loop(0, terms // TILE, turn, 0)

    weigh = scale_phase(
        turn_rows, ids_hbm, live, tiles_hbm, start_hbm, row_ref, col_ref, *scale_refs
    )

    def axes(flow):
        return (x, nx, y, ny) if flow == 0 else (y, ny, x, nx)

    def device(flow, first, second):
        return second * nx + first if flow == 0 else first * nx + second

    def lanes(flow):
        return slice(flow * TILE, (flow + 1) * TILE)

    def prepare(block, carry):
        at = pl.ds(pl.multiple_of(block * TILE, TILE), TILE)
        column = turn_out(col_ref, block, width)
        col_turn[at, :] = column[:, :TILE]
        scaled[at, :] = (column * start_ref[at, :].astype(jnp.float32)).astype(jnp.bfloat16)
        return carry

    lax.fori_loop(0, docs // TILE, prepare, 0)

    steps = [(dx, dy) for dx in range(nx) for dy in range(ny)]
    steps.sort(key=lambda s: -((s[0] > 0) + (s[1] > 0)))
    copies_a, copies_b = {}, {}
    for dx, dy in steps:
        target = lax.rem(y + dy, ny) * nx + lax.rem(x + dx, nx)
        at = pl.ds(pl.multiple_of(target * share, share), share)
        product = jnp.dot(matrix[at, :], scaled[...], preferred_element_type=jnp.float32)
        column = row_turn[at, :]
        product = product * jnp.concatenate([column] * (width // TILE), axis=1)
        partial[dy * nx + dx] = product
        for flow in range(2):
            a, n1, b, n2 = axes(flow)
            s1, s2 = (dx, dy) if flow == 0 else (dy, dx)
            if s1 == 0:
                continue
            slot = s1 * n2 + s2
            send_a[flow, slot] = encode(product[:, lanes(flow)])
            copies_a[flow, s1, s2] = remote(
                send_a.at[flow, slot],
                recv_a.at[flow, slot],
                sems[0].at[flow, slot],
                sems[1].at[flow, slot],
                "doc",
                device(flow, lax.rem(a + s1, n1), b),
            )
            copies_a[flow, s1, s2].start()

    weight_copies = weigh()

    def own(flow, s2):
        dx, dy = (0, s2) if flow == 0 else (s2, 0)
        return partial[dy * nx + dx, :, lanes(flow)]

    def landed(flow, s2):
        a, n1, b, n2 = axes(flow)
        total = own(flow, s2)
        for s1 in range(1, n1):
            copies_a[flow, s1, s2].wait()
            total = total + decode(recv_a[flow, s1 * n2 + s2])
        return total

    for flow in range(2):
        a, n1, b, n2 = axes(flow)
        for s2 in range(1, n2):
            send_b[flow, s2] = encode(landed(flow, s2))
            copies_b[flow, s2] = remote(
                send_b.at[flow, s2],
                recv_b.at[flow, s2],
                sems[2].at[flow, s2],
                sems[3].at[flow, s2],
                "doc",
                device(flow, a, lax.rem(b + s2, n2)),
            )
            copies_b[flow, s2].start()

    weight_ref[...] = row_ref[...] * finish_exchange(weight_copies, held_e, "doc")
    blocks_of_share = share // TILE
    weight = jnp.concatenate(
        [turn_out(weight_ref, doc * blocks_of_share + k, TILE) for k in range(blocks_of_share)], axis=0
    )
    copies_c, copies_d = {}, {}
    left = []
    for flow in range(2):
        a, n1, b, n2 = axes(flow)
        total = landed(flow, 0)
        for s2 in range(1, n2):
            copies_b[flow, s2].wait()
            total = total + decode(recv_b[flow, s2])
        total = total - weight * (mean_ref[flow : flow + 1, :] * (1.0 / docs_total))
        left.append(total)
        gathered[flow, doc] = encode(total)
        for s1 in range(1, n1):
            copies_c[flow, s1] = remote(
                gathered.at[flow, doc],
                gathered.at[flow, doc],
                sems[4].at[flow, s1],
                sems[5].at[flow, s1],
                "doc",
                device(flow, lax.rem(a + s1, n1), b),
            )
            copies_c[flow, s1].start()

    left_share = jnp.concatenate(left, axis=1)
    pack_gram(
        precise(left_share, left_share, ((0,), (0,))) * (1.0 / (terms * n)),
        [jnp.sum(weight * part, axis=0, keepdims=True) for part in left],
        left_gram[0],
    )
    left_steps = gram_steps(*left_gram)
    next(left_steps)

    def unpack(flow, block):
        at = pl.ds(pl.multiple_of(block * share, share), share)
        value = decode(gathered[flow, block]) * row_turn[at, :]
        factor[at, lanes(flow)] = value.astype(jnp.bfloat16)

    for flow in range(2):
        unpack(flow, doc)
    for flow in range(2):
        a, n1, b, n2 = axes(flow)
        for s1 in range(n1):
            if s1:
                copies_c[flow, s1].wait()
            source = device(flow, lax.rem(a - s1 + n1, n1), b)
            for s2 in range(1, n2):
                copies_d[flow, s1, s2] = remote(
                    gathered.at[flow, source],
                    gathered.at[flow, source],
                    sems[6].at[flow, s1 * n2 + s2],
                    sems[7].at[flow, s1 * n2 + s2],
                    "doc",
                    device(flow, a, lax.rem(b + s2, n2)),
                )
                copies_d[flow, s1, s2].start()
    for flow in range(2):
        a, n1, b, n2 = axes(flow)
        for s1 in range(1, n1):
            unpack(flow, device(flow, lax.rem(a - s1 + n1, n1), b))
    next(left_steps)
    for flow in range(2):
        a, n1, b, n2 = axes(flow)
        for s1 in range(n1):
            for s2 in range(1, n2):
                copies_d[flow, s1, s2].wait()
                unpack(
                    flow,
                    device(flow, lax.rem(a - s1 + n1, n1), lax.rem(b - s2 + n2, n2)),
                )
    wide = 2 * piece

    def right_product(chunk, core):
        at = pl.ds(pl.multiple_of(core * (docs // 2) + chunk * wide, wide), wide)
        product = jnp.dot(turned[at, :], factor[...], preferred_element_type=jnp.float32)
        return product * jnp.concatenate([col_turn[at, :]] * (width // TILE), axis=1)

    sibling = 2 * z + 1 - c
    chunks = [lax.rem(z // 2 + 1 + j, nz // 2) for j in range(nz // 2)]
    near_copies = []
    for j, chunk in enumerate(chunks):
        near_send[j] = right_product(chunk, 1 - c)
        copy = remote(near_send.at[j], near_recv.at[j], sems[8].at[j], sems[9].at[j], "term", sibling)
        copy.start()
        near_copies.append(copy)

    def far_copy(step):
        there = lax.rem(z + step, nz)
        return remote(
            far_send.at[step], far_recv.at[step], sems[10].at[step], sems[11].at[step], "term", 2 * there + c
        )

    for j, chunk in enumerate(chunks):
        product = right_product(chunk, c)
        near_copies[j].wait()
        near_recv[j] = near_recv[j] + product
        last = j + 1 == len(chunks)
        for k in range(2):
            if last and k:
                continue
            inner = 1 - lax.rem(z, 2) if last else k
            step = lax.rem(2 * chunk + inner - z + nz, nz)
            at = pl.ds(pl.multiple_of(inner * piece, piece), piece)
            far_send[step] = encode(near_recv[j, at, :])
            far_copy(step).start()
        if j == 0:
            next(left_steps)
    for _ in left_steps:
        pass
    unpack_gram(left_gram[1], gram)
    inverse_kernel(gram, inverse_ref, work)

    def split_inverse():
        whiten = inverse_ref[...].T
        high = whiten.astype(jnp.bfloat16)
        halves[0] = high
        halves[1] = (whiten - high.astype(jnp.float32)).astype(jnp.bfloat16)

    def whitened(value):
        high = value.astype(jnp.bfloat16)
        low = (value - high.astype(jnp.float32)).astype(jnp.bfloat16)
        parts = [(high, 0), (low, 0), (high, 1)]
        total = [jnp.dot(v, halves[k], preferred_element_type=jnp.float32) for v, k in parts]
        return total[0] + (total[1] + total[2])

    def finish_left(block):
        at = pl.ds(pl.multiple_of(block * share, share), share)
        value = jnp.concatenate([decode(gathered[flow, block]) for flow in range(2)], axis=1)
        left_out[at, :] = whitened(value).astype(jnp.bfloat16)

    extra = left_gram[1].shape[1] - 8
    weighted = jnp.concatenate(
        [left_gram[1][0, extra + 1 + k : extra + 2 + k, :] for k in range(width // TILE)], axis=1
    )
    lean = precise(jnp.broadcast_to(weighted, (8, width)), inverse_ref[...], ((1,), (1,)))[0:1]
    split_inverse()
    own_rows = pl.ds(pl.multiple_of(lax.rem(z, 2) * piece, piece), piece)
    total = near_recv[len(chunks) - 1, own_rows, :]
    for step in range(1, nz):
        far_copy(step).wait()
        total = total + decode(far_recv[step])
    block = precise(total, inverse_ref[...], ((1,), (1,))) - lean * (1.0 / docs_total)

    me = c * nz + z
    pack_gram(
        precise(block, block, ((0,), (0,))) * (1.0 / docs_total), [], right_gram[0]
    )
    right_steps = gram_steps(*right_gram)
    next(right_steps)
    right_parts[me] = encode(block)
    for k in range(m // 4):
        finish_left(k)
    next(right_steps)
    for k in range(m // 4, 3 * m // 4):
        finish_left(k)
    next(right_steps)
    far_copies = []
    for step in range(1, nz):
        copy = remote(
            right_parts.at[me],
            right_parts.at[me],
            sems[12].at[step],
            sems[13].at[step],
            "term",
            2 * lax.rem(z + step, nz) + c,
        )
        copy.start()
        far_copies.append(copy)
    copy = remote(
        right_parts.at[me], right_parts.at[me], sems[14].at[0], sems[15].at[0], "term", sibling
    )
    copy.start()
    near_copies = [copy]
    for k in range(3 * m // 4, m):
        finish_left(k)
    for _ in right_steps:
        pass
    unpack_gram(right_gram[1], gram)
    inverse_kernel(gram, inverse_ref, work)
    split_inverse()

    def finish_right(t):
        at = pl.ds(pl.multiple_of(t * piece, piece), piece)
        right_out[at, :] = whitened(decode(right_parts[t])).astype(jnp.bfloat16)

    for step in range(1, nz):
        far_copies[step - 1].wait()
        t = c * nz + lax.rem(z - step + nz, nz)
        copy = remote(
            right_parts.at[t], right_parts.at[t], sems[14].at[step], sems[15].at[step], "term", sibling
        )
        copy.start()
        near_copies.append(copy)
    for step in range(nz):
        finish_right(c * nz + lax.rem(z - step + nz, nz))
    for step, copy in enumerate(near_copies):
        copy.wait()
        finish_right((1 - c) * nz + lax.rem(z - step + nz, nz))


def emit_kernel(row_ref, col_ref, left_ref, right_ref, *rest):
    outs, sems = rest[:4], rest[4]
    copies = [
        pltpu.make_async_copy(source, target, sems.at[k])
        for k, (source, target) in enumerate(zip((row_ref, col_ref, left_ref, right_ref), outs))
    ]
    for copy in copies:
        copy.start()
    for copy in copies:
        copy.wait()


def emit(arrays):
    return pl.pallas_call(
        emit_kernel,
        out_shape=[jax.ShapeDtypeStruct(x.shape, x.dtype) for x in arrays],
        in_specs=[VMEM] * 4,
        out_specs=[pl.BlockSpec(memory_space=pl.ANY)] * 4,
        scratch_shapes=[pltpu.SemaphoreType.DMA((4,))],
        compiler_params=pltpu.CompilerParams(vmem_limit_bytes=4 << 20),
        name="emit",
    )(*arrays)


def per_device(tile_values, tile_rows, tile_cols, tile_count, start_block):
    n, m = lax.axis_size("term"), lax.axis_size("doc")
    nz = n // 2
    terms, (docs, width) = RB * TILE, start_block.shape
    share, piece = terms // m, docs // n
    wide = max(grid_of(m))
    int16, f32, bf16 = jnp.int16, jnp.float32, jnp.bfloat16
    coded = pltpu.VMEM((2, m, share + 16, TILE), int16)
    coded_b = pltpu.VMEM((2, wide, share + 16, TILE), int16)
    far = pltpu.VMEM((nz, piece + 16, width), int16)
    near = pltpu.VMEM((nz // 2, 2 * piece, width), f32)
    pairs = [pltpu.SemaphoreType.DMA((2, size)) for size in (m, m, wide, wide, wide, wide, m, m)]
    vector = jax.ShapeDtypeStruct((RB, TILE), f32)
    hbm = pl.BlockSpec(memory_space=pl.ANY)
    ids, live = tables(tile_rows, tile_cols, tile_count)
    outs = pl.pallas_call(
        whole_kernel,
        out_shape=[
            vector,
            vector,
            jax.ShapeDtypeStruct((terms, width), bf16),
            jax.ShapeDtypeStruct((docs, width), bf16),
        ],
        in_specs=[hbm, VMEM, hbm, hbm],
        out_specs=[VMEM] * 4,
        scratch_shapes=[
            pltpu.VMEM((terms, TILE), f32),
            pltpu.VMEM((docs, TILE), f32),
            pltpu.VMEM((docs, width), bf16),
            pltpu.VMEM((m, share, width), f32),
            coded,
            coded,
            coded_b,
            coded_b,
            coded,
            pltpu.VMEM((terms, width), bf16),
            near,
            near,
            far,
            far,
            pltpu.VMEM((n, piece + 16, width), int16),
            pltpu.VMEM((width, width), f32),
            pltpu.VMEM((2, width, width), bf16),
            pltpu.VMEM((width, width), f32),
            pltpu.VMEM((width, 2 * width), f32),
        ]
        + gram_scratch()
        + gram_scratch()
        + scale_scratch(terms, docs, width, tile_values.shape[0], tile_values.dtype)
        + pairs
        + semaphores(*[nz] * 8),
        compiler_params=pltpu.CompilerParams(
            collective_id=0, has_side_effects=True, vmem_limit_bytes=44 << 20
        ),
        name="whole",
    )(ids, live, tile_values, start_block)
    row, col, left_basis, right_basis = emit(outs)
    return (row.reshape(-1), col.reshape(-1), left_basis, right_basis)


def solution(mesh):
    placed = (
        P("term", "doc", None),
        P("term", "doc"),
        P("term", "doc"),
        P("term", "doc"),
        P("doc", None),
    )
    return jax.shard_map(
        per_device,
        mesh=mesh,
        in_specs=placed,
        out_specs=(P("term"), P("doc"), P("term", None), P("doc", None)),
        check_vma=False,
    )
```

```python
import math

import jax
import jax.numpy as jnp
from jax import lax
from jax.experimental import pallas as pl
from jax.experimental.pallas import tpu as pltpu
from jax.sharding import PartitionSpec as P

TILE = 128
RB = 16
CB = 16


PRECISE = lax.Precision.HIGHEST
MESH = pl.DeviceIdType.MESH
VMEM = pl.BlockSpec(memory_space=pltpu.VMEM)
SMEM = pl.BlockSpec(memory_space=pltpu.SMEM)


BLOCK = 64
GROUP = 8


def block_inverse(block, low, high):
    rows = lax.broadcasted_iota(jnp.int32, block.shape, 0)
    pivots = jnp.ones_like(block)
    for base in range(0, BLOCK, GROUP):
        factors = []
        for at in range(base, base + GROUP):
            column = jnp.broadcast_to(block[:, low + at : low + at + 1], block.shape)
            for past, factor in enumerate(factors):
                column = column - factor * column[base + past : base + past + 1, :]
            pivots = jnp.where(rows == at, column, pivots)
            ratio = column * (1.0 / column[at : at + 1, :])
            factors.append(jnp.where(rows > at, ratio, 0.0))
        for at, factor in enumerate(factors):
            block = block - factor * block[base + at : base + at + 1, :]
    lanes = lax.broadcasted_iota(jnp.int32, block.shape, 1)
    inside = (lanes >= high) & (lanes < high + BLOCK)
    return jnp.where(inside, block * lax.rsqrt(pivots), 0.0)


def inverse_kernel(gram_ref, o_ref, work):
    width = gram_ref.shape[0]
    work[:, :width] = gram_ref[...]
    rows = lax.broadcasted_iota(jnp.int32, (width, width), 0)
    lanes = lax.broadcasted_iota(jnp.int32, (width, width), 1)
    work[:, width:] = jnp.where(rows == lanes, 1.0, 0.0)
    for index in range(width // BLOCK):
        start = index * BLOCK
        near = start // TILE * TILE
        low = start - near
        high = TILE - BLOCK - low
        block = work[start : start + BLOCK, near : near + TILE]
        rows = lax.broadcasted_iota(jnp.int32, block.shape, 0)
        lanes = lax.broadcasted_iota(jnp.int32, block.shape, 1)
        inside = (lanes >= low) & (lanes < low + BLOCK)
        block = jnp.where(inside, block, jnp.where(lanes - high == rows, 1.0, 0.0))
        inverse = block_inverse(block, low, high)
        panel = work[start : start + BLOCK, :]
        solved = jnp.dot(
            inverse,
            jnp.concatenate([panel, panel], axis=0),
            precision=PRECISE,
            preferred_element_type=jnp.float32,
        )
        o_ref[start : start + BLOCK, :] = solved[:, width:]
        if start + BLOCK < width:
            update = lax.dot_general(
                solved[:, :width],
                solved,
                (((0,), (0,)), ((), ())),
                precision=PRECISE,
                preferred_element_type=jnp.float32,
            )
            work[start + BLOCK :, :] = work[start + BLOCK :, :] - update[start + BLOCK :, :]


def greet():
    barrier = pltpu.get_barrier_semaphore()
    n, m = lax.axis_size("term"), lax.axis_size("doc")
    me, doc = lax.axis_index("term"), lax.axis_index("doc")
    peers = [{"term": lax.rem(me + step, n)} for step in range(1, n)]
    for step in range(1, m):
        there = lax.rem(doc + step, m)
        peers += [{"doc": there}, {"doc": there, "term": me + 1 - 2 * lax.rem(me, 2)}]
    for peer in peers:
        pl.semaphore_signal(barrier, inc=1, device_id=peer, device_id_type=MESH)
    pl.semaphore_wait(barrier, len(peers))


def remote(source, target, send_sem, recv_sem, axis, peer):
    return pltpu.make_async_remote_copy(
        src_ref=source,
        dst_ref=target,
        send_sem=send_sem,
        recv_sem=recv_sem,
        device_id=axis if peer is None else {axis: peer},
        device_id_type=MESH,
    )


def paired():
    n, me = lax.axis_size("term"), lax.axis_index("term")
    return n // 2, me // 2, lax.rem(me, 2)


def semaphores(*sizes):
    return [pltpu.SemaphoreType.DMA((size,)) for size in sizes]


def split3(value):
    high = value.astype(jnp.bfloat16)
    rest = value - high.astype(jnp.float32)
    middle = rest.astype(jnp.bfloat16)
    return high, middle, (rest - middle.astype(jnp.float32)).astype(jnp.bfloat16)


def spread(value, parts):
    high, middle, low = (part.astype(jnp.float32) for part in split3(value))
    blocks, depth, lanes = parts.shape
    rows = lax.broadcasted_iota(jnp.int32, (depth, lanes), 0)
    for block in range(blocks):
        at = slice(block, block + 1)
        picked = jnp.where(rows == 0, high[at], jnp.where(rows == 1, middle[at], low[at]))
        parts[block] = jnp.where(rows < 3, picked, 0.0).astype(jnp.bfloat16)


def tile_sums(tiles, source_ids, parts, sums, target, forward):
    slots = sums.shape[0]
    for slot in range(slots):
        product = lax.dot_general(
            parts[source_ids[0, slot]],
            tiles[slot],
            (((1,), (1 if forward else 0,)), ((), ())),
            preferred_element_type=jnp.float32,
        )
        sums[slot : slot + 1, :] = product[0:1] + product[1:2] + product[2:3]
    stacked = jnp.concatenate(split3(sums[...]), axis=0)
    return jnp.dot(target, stacked, preferred_element_type=jnp.float32)


def start_exchange(held, axis, send_sem, recv_sem):
    n, me = lax.axis_size(axis), lax.axis_index(axis)
    copies = []
    for step in range(1, n):
        copy = remote(
            held.at[0], held.at[step], send_sem.at[step], recv_sem.at[step], axis, lax.rem(me + step, n)
        )
        copy.start()
        copies.append(copy)
    return copies


def finish_exchange(copies, held, axis):
    n, me = lax.axis_size(axis), lax.axis_index(axis)
    for copy in copies:
        copy.wait()
    total = held[me]
    for source in range(1, n):
        total = total + held[lax.rem(me - source + n, n)]
    return total


def scale_phase(
    meanwhile,
    count,
    rows_hbm,
    cols_hbm,
    tiles_hbm,
    start_hbm,
    row_ref,
    col_ref,
    weight_ref,
    mean_ref,
    start_ref,
    dense_ref,
    turned_ref,
    row_ids,
    col_ids,
    lanes,
    places,
    lookup,
    tiles,
    flipped,
    parts,
    sums,
    held_a,
    held_b,
    held_c,
    held_d,
    held_e,
    load_sem,
    *sems,
):
    slots = tiles_hbm.shape[0]
    sources = [rows_hbm, cols_hbm, rows_hbm, cols_hbm, start_hbm, tiles_hbm]
    targets = [row_ids, col_ids, lanes.at[0], lanes.at[1], start_ref, tiles.at[pl.ds(0, slots)]]
    loads = [
        pltpu.make_async_copy(source, target, load_sem.at[k])
        for k, (source, target) in enumerate(zip(sources, targets))
    ]
    for load in loads:
        load.start()
    tiles[slots] = jnp.zeros(tiles.shape[1:], tiles.dtype)
    flipped[slots] = jnp.zeros(tiles.shape[1:], tiles.dtype)
    blocks = row_ref.shape[0]
    spread(jnp.ones(row_ref.shape, jnp.float32), parts)
    for load in loads[:4]:
        load.wait()
    used = count[0, 0]
    place = lax.broadcasted_iota(jnp.int32, (blocks, slots), 0)
    live = lax.broadcasted_iota(jnp.int32, (blocks, slots), 1) < used
    to_rows, to_cols = (
        jnp.concatenate([jnp.where(live & (place == lanes[k]), 1.0, 0.0)] * 3, axis=1).astype(jnp.bfloat16)
        for k in range(2)
    )
    row = lax.broadcasted_iota(jnp.int32, places.shape, 0)
    col = lax.broadcasted_iota(jnp.int32, places.shape, 1)
    table = jnp.full(places.shape, slots, jnp.int32)
    for slot in range(slots):
        found = (row == row_ids[0, slot]) & (col == jnp.where(slot < used, col_ids[0, slot], -1))
        table = jnp.where(found, slot, table)
    places[...] = table
    keep = pltpu.make_async_copy(places, lookup, load_sem.at[7])
    keep.start()
    greet()

    def build(out_ref, source, turn):
        def place_row(outer, carry):
            at = pl.multiple_of(outer * TILE, TILE)
            for inner in range(blocks):
                slot = lookup[inner, outer] if turn else lookup[outer, inner]
                tile = source[slot]
                out_ref[pl.ds(at, TILE), inner * TILE : (inner + 1) * TILE] = tile
            return carry

        lax.fori_loop(0, blocks, place_row, 0)

    def flip(slot, carry):
        flipped[slot] = tiles[slot].T
        return carry

    loads[4].wait()
    mean = jnp.sum(start_ref[...].astype(jnp.float32), axis=0, keepdims=True)
    keep.wait()
    loads[5].wait()
    held_a[0, :blocks, :] = tile_sums(tiles, col_ids, parts, sums, to_rows, True)
    extra = held_a.shape[1] - blocks
    pieces = [mean[:, at : at + TILE] for at in range(0, mean.shape[1], TILE)]
    pieces.append(jnp.zeros((extra - len(pieces), TILE), jnp.float32))
    held_a[0, blocks:, :] = jnp.concatenate(pieces, axis=0)
    copies = start_exchange(held_a, "doc", *sems[0:2])
    build(dense_ref, tiles, False)
    joined = finish_exchange(copies, held_a, "doc")
    mean_ref[...] = joined[blocks:, :]
    spread(1.0 / joined[:blocks], parts)

    held_b[0] = tile_sums(tiles, row_ids, parts, sums, to_cols, False)
    copies = start_exchange(held_b, "term", *sems[2:4])
    lax.fori_loop(0, slots, flip, 0)
    total = finish_exchange(copies, held_b, "term")
    spread(1.0 / total, parts)

    held_c[0] = tile_sums(flipped, col_ids, parts, sums, to_rows, False)
    copies = start_exchange(held_c, "doc", *sems[4:6])
    build(turned_ref, flipped, True)
    row_scale = 1.0 / finish_exchange(copies, held_c, "doc")
    row_ref[...] = row_scale
    spread(row_scale, parts)

    held_d[0] = tile_sums(tiles, row_ids, parts, sums, to_cols, False)
    copies = start_exchange(held_d, "term", *sems[6:8])
    meanwhile()
    col_ref[...] = 1.0 / finish_exchange(copies, held_d, "term")

    def weigh():
        spread(col_ref[...], parts)
        held_e[0] = tile_sums(flipped, col_ids, parts, sums, to_rows, False)
        return start_exchange(held_e, "doc", *sems[8:10])

    return weigh


def scale_scratch(terms, docs, width, slots, kind):
    m, n = lax.axis_size("doc"), lax.axis_size("term")
    vector = pltpu.VMEM((RB, TILE), jnp.float32)
    extra = -(-width // (8 * TILE)) * 8
    stack = pltpu.VMEM((slots + 1, TILE, TILE), kind)

    def held(count, more=0):
        return pltpu.VMEM((count, RB + more, TILE), jnp.float32)

    return [
        vector,
        pltpu.VMEM((extra, TILE), jnp.float32),
        pltpu.VMEM((docs, width), kind),
        pltpu.VMEM((terms, docs), kind),
        pltpu.VMEM((docs, terms), kind),
        pltpu.SMEM((1, slots), jnp.int32),
        pltpu.SMEM((1, slots), jnp.int32),
        pltpu.VMEM((2, 1, slots), jnp.int32),
        pltpu.VMEM((RB, TILE), jnp.int32),
        pltpu.SMEM((RB, TILE), jnp.int32),
        stack,
        stack,
        pltpu.VMEM((RB, 16, TILE), jnp.bfloat16),
        pltpu.VMEM((slots, TILE), jnp.float32),
        held(m, extra),
        held(n),
        held(m),
        held(n),
        held(m),
        pltpu.SemaphoreType.DMA((8,)),
    ] + semaphores(m, m, n, n, m, m, n, n, m, m)


SCALE_REFS = 30


CODES = 32760.0
OCTAVE = 256.0 / math.log(2.0)


def encode(value):
    rows, lanes = value.shape
    groups = value.reshape(rows // 8, 8, lanes)
    top = jnp.maximum(jnp.max(jnp.abs(groups), axis=0), 1e-30)
    level = jnp.ceil(jnp.log(top) * OCTAVE)
    codes = jnp.round(groups * (jnp.exp(level * (-1.0 / OCTAVE)) * CODES))
    whole = jnp.concatenate([codes.reshape(rows, lanes), level, level], axis=0)
    return whole.astype(jnp.int32).astype(jnp.int16)


def decode(block):
    rows, lanes = block.shape[0] - 16, block.shape[1]
    value = block.astype(jnp.int32).astype(jnp.float32)
    scale = jnp.exp(value[rows : rows + 8] * (1.0 / OCTAVE)) * (1.0 / CODES)
    return (value[:rows].reshape(rows // 8, 8, lanes) * scale[None]).reshape(rows, lanes)


def grid_of(n):
    nx = int(math.isqrt(n))
    while n % nx:
        nx -= 1
    return nx, n // nx


def turn_out(vector_ref, block, lanes):
    row = jnp.broadcast_to(vector_ref[pl.ds(block, 1), :], (TILE, TILE))
    column = row.T
    return jnp.concatenate([column] * (lanes // TILE), axis=1)


def precise(a, b, dims):
    return lax.dot_general(
        a, b, (dims, ((), ())), precision=PRECISE, preferred_element_type=jnp.float32
    )


def pack_gram(gram, extras, packed):
    groups, rows = packed.shape[0], packed.shape[1] - 8
    row = lax.broadcasted_iota(jnp.int32, (TILE, TILE), 0)
    lane = lax.broadcasted_iota(jnp.int32, (TILE, TILE), 1)
    last = gram[TILE:, TILE:]
    packed_rows = [jnp.where(row <= lane, gram[:TILE, :TILE], last), gram[:TILE, TILE:]]
    packed_rows = jnp.concatenate(packed_rows, axis=0)
    diagonal = jnp.sum(jnp.where(row == lane, last, 0.0), axis=0, keepdims=True)
    extras = [diagonal] + extras
    extras.append(jnp.zeros((8 - len(extras), TILE), jnp.float32))
    for group in range(groups):
        packed[group, :rows, :] = packed_rows[group * rows : (group + 1) * rows]
        packed[group, rows:, :] = (
            jnp.concatenate(extras, axis=0) if group == 0 else jnp.zeros((8, TILE), jnp.float32)
        )


def unpack_gram(packed, gram):
    rows = packed.shape[1] - 8
    row = lax.broadcasted_iota(jnp.int32, (TILE, TILE), 0)
    lane = lax.broadcasted_iota(jnp.int32, (TILE, TILE), 1)
    half = packed.shape[0] // 2
    both = jnp.concatenate([packed[g, :rows, :] for g in range(half)], axis=0)
    cross = jnp.concatenate([packed[half + g, :rows, :] for g in range(half)], axis=0)
    other = both.T
    gram[:TILE, :TILE] = jnp.where(row <= lane, both, other)
    gram[:TILE, TILE:] = cross
    gram[TILE:, :TILE] = jnp.zeros((TILE, TILE), jnp.float32)
    diagonal = jnp.broadcast_to(packed[0, rows : rows + 1, :], (TILE, TILE))
    last = jnp.where(row > lane, both, jnp.where(row == lane, diagonal, other))
    gram[TILE:, TILE:] = last


def gram_steps(x_ref, o_ref, landing, held, *sems):
    nz, z, c = paired()
    m, my = lax.axis_size("doc"), lax.axis_index("doc")
    steps = [(step, flip) for step in range(m) for flip in range(2) if step or flip]

    def peer(step, flip):
        there = lax.rem(my + step, m)
        core = 1 - c if flip else c
        return 2 * there + core, {"doc": there, "term": 2 * z + core}

    def exchange(source, target, send_sem, recv_sem):
        copies = []
        for step, flip in steps:
            group, place = peer(step, flip)
            slot = 2 * step + flip
            copy = remote(
                source(group), target(slot), send_sem.at[slot], recv_sem.at[slot], place, None
            )
            copy.start()
            copies.append(copy)
        return copies

    mine = 2 * my + c
    copies = exchange(lambda g: x_ref.at[g], lambda k: landing.at[k], *sems[0:2])
    yield
    total = x_ref[mine]
    for (step, flip), copy in zip(steps, copies):
        copy.wait()
        total = total + landing[2 * step + flip]
    held[0] = total
    copies = []
    for step in range(1, nz):
        copy = remote(
            held.at[0], held.at[step], sems[2].at[step], sems[3].at[step], "term", 2 * lax.rem(z + step, nz) + c
        )
        copy.start()
        copies.append(copy)
    yield
    for copy in copies:
        copy.wait()
    total = held[z]
    for source in range(1, nz):
        total = total + held[lax.rem(z - source + nz, nz)]
    o_ref[mine] = total
    copies = exchange(lambda g: o_ref.at[mine], lambda k: o_ref.at[mine], *sems[4:6])
    yield
    for copy in copies:
        copy.wait()


def gram_scratch():
    nz, m = lax.axis_size("term") // 2, lax.axis_size("doc")
    rows = TILE // m + 8
    packed = pltpu.VMEM((2 * m, rows, TILE), jnp.float32)
    return [packed, packed, packed, pltpu.VMEM((nz, rows, TILE), jnp.float32)] + semaphores(
        2 * m, 2 * m, nz, nz, 2 * m, 2 * m
    )


GRAM_REFS = 10


def whole_kernel(
    count,
    rows_hbm,
    cols_hbm,
    tiles_hbm,
    start_hbm,
    row_ref,
    col_ref,
    left_out,
    right_out,
    row_turn,
    col_turn,
    scaled,
    partial,
    send_a,
    recv_a,
    send_b,
    recv_b,
    gathered,
    factor,
    near_send,
    near_recv,
    far_send,
    far_recv,
    right_parts,
    inverse_ref,
    halves,
    gram,
    work,
    *rest,
):
    left_gram, right_gram = rest[:GRAM_REFS], rest[GRAM_REFS : 2 * GRAM_REFS]
    scale_refs = rest[2 * GRAM_REFS : 2 * GRAM_REFS + SCALE_REFS]
    weight_ref, mean_ref, start_ref, matrix, turned = scale_refs[:5]
    held_e = scale_refs[18]
    sems = rest[2 * GRAM_REFS + SCALE_REFS :]
    n, m = lax.axis_size("term"), lax.axis_size("doc")
    nz, z, c = paired()
    doc = lax.axis_index("doc")
    nx, ny = grid_of(m)
    x, y = lax.rem(doc, nx), doc // nx
    terms, width = left_out.shape
    docs = right_out.shape[0]
    share, piece = terms // m, docs // n
    docs_total = docs * m

    def turn_rows():
        def turn(block, carry):
            at = pl.ds(pl.multiple_of(block * TILE, TILE), TILE)
            row_turn[at, :] = turn_out(row_ref, block, TILE)
            return carry

        lax.fori_loop(0, terms // TILE, turn, 0)

    weigh = scale_phase(
        turn_rows,
        count,
        rows_hbm,
        cols_hbm,
        tiles_hbm,
        start_hbm,
        row_ref,
        col_ref,
        *scale_refs,
    )

    def axes(flow):
        return (x, nx, y, ny) if flow == 0 else (y, ny, x, nx)

    def device(flow, first, second):
        return second * nx + first if flow == 0 else first * nx + second

    def lanes(flow):
        return slice(flow * TILE, (flow + 1) * TILE)

    def prepare(block, carry):
        at = pl.ds(pl.multiple_of(block * TILE, TILE), TILE)
        column = turn_out(col_ref, block, width)
        col_turn[at, :] = column[:, :TILE]
        scaled[at, :] = (column * start_ref[at, :].astype(jnp.float32)).astype(jnp.bfloat16)
        return carry

    lax.fori_loop(0, docs // TILE, prepare, 0)

    steps = [(dx, dy) for dx in range(nx) for dy in range(ny)]
    steps.sort(key=lambda s: -((s[0] > 0) + (s[1] > 0)))
    copies_a, copies_b = {}, {}
    for dx, dy in steps:
        target = lax.rem(y + dy, ny) * nx + lax.rem(x + dx, nx)
        at = pl.ds(pl.multiple_of(target * share, share), share)
        product = jnp.dot(matrix[at, :], scaled[...], preferred_element_type=jnp.float32)
        column = row_turn[at, :]
        product = product * jnp.concatenate([column] * (width // TILE), axis=1)
        partial[dy * nx + dx] = product
        for flow in range(2):
            a, n1, b, n2 = axes(flow)
            s1, s2 = (dx, dy) if flow == 0 else (dy, dx)
            if s1 == 0:
                continue
            slot = s1 * n2 + s2
            send_a[flow, slot] = encode(product[:, lanes(flow)])
            copies_a[flow, s1, s2] = remote(
                send_a.at[flow, slot],
                recv_a.at[flow, slot],
                sems[0].at[flow, slot],
                sems[1].at[flow, slot],
                "doc",
                device(flow, lax.rem(a + s1, n1), b),
            )
            copies_a[flow, s1, s2].start()

    weight_copies = weigh()

    def own(flow, s2):
        dx, dy = (0, s2) if flow == 0 else (s2, 0)
        return partial[dy * nx + dx, :, lanes(flow)]

    def landed(flow, s2):
        a, n1, b, n2 = axes(flow)
        total = own(flow, s2)
        for s1 in range(1, n1):
            copies_a[flow, s1, s2].wait()
            total = total + decode(recv_a[flow, s1 * n2 + s2])
        return total

    for flow in range(2):
        a, n1, b, n2 = axes(flow)
        for s2 in range(1, n2):
            send_b[flow, s2] = encode(landed(flow, s2))
            copies_b[flow, s2] = remote(
                send_b.at[flow, s2],
                recv_b.at[flow, s2],
                sems[2].at[flow, s2],
                sems[3].at[flow, s2],
                "doc",
                device(flow, a, lax.rem(b + s2, n2)),
            )
            copies_b[flow, s2].start()

    weight_ref[...] = row_ref[...] * finish_exchange(weight_copies, held_e, "doc")
    blocks_of_share = share // TILE
    weight = jnp.concatenate(
        [turn_out(weight_ref, doc * blocks_of_share + k, TILE) for k in range(blocks_of_share)], axis=0
    )
    copies_c, copies_d = {}, {}
    left = []
    for flow in range(2):
        a, n1, b, n2 = axes(flow)
        total = landed(flow, 0)
        for s2 in range(1, n2):
            copies_b[flow, s2].wait()
            total = total + decode(recv_b[flow, s2])
        total = total - weight * (mean_ref[flow : flow + 1, :] * (1.0 / docs_total))
        left.append(total)
        gathered[flow, doc] = encode(total)
        for s1 in range(1, n1):
            copies_c[flow, s1] = remote(
                gathered.at[flow, doc],
                gathered.at[flow, doc],
                sems[4].at[flow, s1],
                sems[5].at[flow, s1],
                "doc",
                device(flow, lax.rem(a + s1, n1), b),
            )
            copies_c[flow, s1].start()

    left_share = jnp.concatenate(left, axis=1)
    pack_gram(
        precise(left_share, left_share, ((0,), (0,))) * (1.0 / (terms * n)),
        [jnp.sum(weight * part, axis=0, keepdims=True) for part in left],
        left_gram[0],
    )
    left_steps = gram_steps(*left_gram)
    next(left_steps)

    def unpack(flow, block):
        at = pl.ds(pl.multiple_of(block * share, share), share)
        value = decode(gathered[flow, block]) * row_turn[at, :]
        factor[at, lanes(flow)] = value.astype(jnp.bfloat16)

    for flow in range(2):
        unpack(flow, doc)
    for flow in range(2):
        a, n1, b, n2 = axes(flow)
        for s1 in range(n1):
            if s1:
                copies_c[flow, s1].wait()
            source = device(flow, lax.rem(a - s1 + n1, n1), b)
            for s2 in range(1, n2):
                copies_d[flow, s1, s2] = remote(
                    gathered.at[flow, source],
                    gathered.at[flow, source],
                    sems[6].at[flow, s1 * n2 + s2],
                    sems[7].at[flow, s1 * n2 + s2],
                    "doc",
                    device(flow, a, lax.rem(b + s2, n2)),
                )
                copies_d[flow, s1, s2].start()
    for flow in range(2):
        a, n1, b, n2 = axes(flow)
        for s1 in range(1, n1):
            unpack(flow, device(flow, lax.rem(a - s1 + n1, n1), b))
    next(left_steps)
    for flow in range(2):
        a, n1, b, n2 = axes(flow)
        for s1 in range(n1):
            for s2 in range(1, n2):
                copies_d[flow, s1, s2].wait()
                unpack(
                    flow,
                    device(flow, lax.rem(a - s1 + n1, n1), lax.rem(b - s2 + n2, n2)),
                )
    wide = 2 * piece

    def right_product(chunk, core):
        at = pl.ds(pl.multiple_of(core * (docs // 2) + chunk * wide, wide), wide)
        product = jnp.dot(turned[at, :], factor[...], preferred_element_type=jnp.float32)
        return product * jnp.concatenate([col_turn[at, :]] * (width // TILE), axis=1)

    sibling = 2 * z + 1 - c
    chunks = [lax.rem(z // 2 + 1 + j, nz // 2) for j in range(nz // 2)]
    near_copies = []
    for j, chunk in enumerate(chunks):
        near_send[j] = right_product(chunk, 1 - c)
        copy = remote(near_send.at[j], near_recv.at[j], sems[8].at[j], sems[9].at[j], "term", sibling)
        copy.start()
        near_copies.append(copy)

    def far_copy(step):
        there = lax.rem(z + step, nz)
        return remote(
            far_send.at[step], far_recv.at[step], sems[10].at[step], sems[11].at[step], "term", 2 * there + c
        )

    for j, chunk in enumerate(chunks):
        product = right_product(chunk, c)
        near_copies[j].wait()
        near_recv[j] = near_recv[j] + product
        last = j + 1 == len(chunks)
        for k in range(2):
            if last and k:
                continue
            inner = 1 - lax.rem(z, 2) if last else k
            step = lax.rem(2 * chunk + inner - z + nz, nz)
            at = pl.ds(pl.multiple_of(inner * piece, piece), piece)
            far_send[step] = encode(near_recv[j, at, :])
            far_copy(step).start()
        if j == 0:
            next(left_steps)
    for _ in left_steps:
        pass
    unpack_gram(left_gram[1], gram)
    inverse_kernel(gram, inverse_ref, work)

    def split_inverse():
        whiten = inverse_ref[...].T
        high = whiten.astype(jnp.bfloat16)
        halves[0] = high
        halves[1] = (whiten - high.astype(jnp.float32)).astype(jnp.bfloat16)

    def whitened(value):
        high = value.astype(jnp.bfloat16)
        low = (value - high.astype(jnp.float32)).astype(jnp.bfloat16)
        parts = [(high, 0), (low, 0), (high, 1)]
        total = [jnp.dot(v, halves[k], preferred_element_type=jnp.float32) for v, k in parts]
        return total[0] + (total[1] + total[2])

    def finish_left(block):
        at = pl.ds(pl.multiple_of(block * share, share), share)
        value = jnp.concatenate([decode(gathered[flow, block]) for flow in range(2)], axis=1)
        left_out[at, :] = whitened(value).astype(jnp.bfloat16)

    extra = left_gram[1].shape[1] - 8
    weighted = jnp.concatenate(
        [left_gram[1][0, extra + 1 + k : extra + 2 + k, :] for k in range(width // TILE)], axis=1
    )
    lean = precise(jnp.broadcast_to(weighted, (8, width)), inverse_ref[...], ((1,), (1,)))[0:1]
    split_inverse()
    own_rows = pl.ds(pl.multiple_of(lax.rem(z, 2) * piece, piece), piece)
    total = near_recv[len(chunks) - 1, own_rows, :]
    for step in range(1, nz):
        far_copy(step).wait()
        total = total + decode(far_recv[step])
    block = precise(total, inverse_ref[...], ((1,), (1,))) - lean * (1.0 / docs_total)

    me = c * nz + z
    pack_gram(
        precise(block, block, ((0,), (0,))) * (1.0 / docs_total), [], right_gram[0]
    )
    right_steps = gram_steps(*right_gram)
    next(right_steps)
    right_parts[me] = encode(block)
    for k in range(m // 4):
        finish_left(k)
    next(right_steps)
    for k in range(m // 4, 3 * m // 4):
        finish_left(k)
    next(right_steps)
    far_copies = []
    for step in range(1, nz):
        copy = remote(
            right_parts.at[me],
            right_parts.at[me],
            sems[12].at[step],
            sems[13].at[step],
            "term",
            2 * lax.rem(z + step, nz) + c,
        )
        copy.start()
        far_copies.append(copy)
    copy = remote(
        right_parts.at[me], right_parts.at[me], sems[14].at[0], sems[15].at[0], "term", sibling
    )
    copy.start()
    near_copies = [copy]
    for k in range(3 * m // 4, m):
        finish_left(k)
    for _ in right_steps:
        pass
    unpack_gram(right_gram[1], gram)
    inverse_kernel(gram, inverse_ref, work)
    split_inverse()

    def finish_right(t):
        at = pl.ds(pl.multiple_of(t * piece, piece), piece)
        right_out[at, :] = whitened(decode(right_parts[t])).astype(jnp.bfloat16)

    for step in range(1, nz):
        far_copies[step - 1].wait()
        t = c * nz + lax.rem(z - step + nz, nz)
        copy = remote(
            right_parts.at[t], right_parts.at[t], sems[14].at[step], sems[15].at[step], "term", sibling
        )
        copy.start()
        near_copies.append(copy)
    for step in range(nz):
        finish_right(c * nz + lax.rem(z - step + nz, nz))
    for step, copy in enumerate(near_copies):
        copy.wait()
        finish_right((1 - c) * nz + lax.rem(z - step + nz, nz))


def emit_kernel(row_ref, col_ref, left_ref, right_ref, *rest):
    outs, sems = rest[:4], rest[4]
    copies = [
        pltpu.make_async_copy(source, target, sems.at[k])
        for k, (source, target) in enumerate(zip((row_ref, col_ref, left_ref, right_ref), outs))
    ]
    for copy in copies:
        copy.start()
    for copy in copies:
        copy.wait()


def emit(arrays):
    return pl.pallas_call(
        emit_kernel,
        out_shape=[jax.ShapeDtypeStruct(x.shape, x.dtype) for x in arrays],
        in_specs=[VMEM] * 4,
        out_specs=[pl.BlockSpec(memory_space=pl.ANY)] * 4,
        scratch_shapes=[pltpu.SemaphoreType.DMA((4,))],
        compiler_params=pltpu.CompilerParams(vmem_limit_bytes=4 << 20),
        name="emit",
    )(*arrays)


def per_device(tile_values, tile_rows, tile_cols, tile_count, start_block):
    n, m = lax.axis_size("term"), lax.axis_size("doc")
    nz = n // 2
    terms, (docs, width) = RB * TILE, start_block.shape
    share, piece = terms // m, docs // n
    wide = max(grid_of(m))
    int16, f32, bf16 = jnp.int16, jnp.float32, jnp.bfloat16
    coded = pltpu.VMEM((2, m, share + 16, TILE), int16)
    coded_b = pltpu.VMEM((2, wide, share + 16, TILE), int16)
    far = pltpu.VMEM((nz, piece + 16, width), int16)
    near = pltpu.VMEM((nz // 2, 2 * piece, width), f32)
    pairs = [pltpu.SemaphoreType.DMA((2, size)) for size in (m, m, wide, wide, wide, wide, m, m)]
    vector = jax.ShapeDtypeStruct((RB, TILE), f32)
    hbm = pl.BlockSpec(memory_space=pltpu.HBM)
    outs = pl.pallas_call(
        whole_kernel,
        out_shape=[
            vector,
            vector,
            jax.ShapeDtypeStruct((terms, width), bf16),
            jax.ShapeDtypeStruct((docs, width), bf16),
        ],
        in_specs=[SMEM] + [hbm] * 4,
        out_specs=[VMEM] * 4,
        scratch_shapes=[
            pltpu.VMEM((terms, TILE), f32),
            pltpu.VMEM((docs, TILE), f32),
            pltpu.VMEM((docs, width), bf16),
            pltpu.VMEM((m, share, width), f32),
            coded,
            coded,
            coded_b,
            coded_b,
            coded,
            pltpu.VMEM((terms, width), bf16),
            near,
            near,
            far,
            far,
            pltpu.VMEM((n, piece + 16, width), int16),
            pltpu.VMEM((width, width), f32),
            pltpu.VMEM((2, width, width), bf16),
            pltpu.VMEM((width, width), f32),
            pltpu.VMEM((width, 2 * width), f32),
        ]
        + gram_scratch()
        + gram_scratch()
        + scale_scratch(terms, docs, width, tile_values.shape[0], tile_values.dtype)
        + pairs
        + semaphores(*[nz] * 8),
        compiler_params=pltpu.CompilerParams(
            collective_id=0, has_side_effects=True, vmem_limit_bytes=44 << 20
        ),
        name="whole",
    )(
        tile_count,
        *(
            pltpu.with_memory_space_constraint(x, pltpu.HBM)
            for x in (tile_rows, tile_cols, tile_values, start_block)
        ),
    )
    row, col, left_basis, right_basis = emit(outs)
    return (row.reshape(-1), col.reshape(-1), left_basis, right_basis)


def solution(mesh):
    placed = (
        P("term", "doc", None),
        P("term", "doc"),
        P("term", "doc"),
        P("term", "doc"),
        P("doc", None),
    )
    return jax.shard_map(
        per_device,
        mesh=mesh,
        in_specs=placed,
        out_specs=(P("term"), P("doc"), P("term", None), P("doc", None)),
        check_vma=False,
    )
```

```python
import math

import jax
import jax.numpy as jnp
from jax import lax
from jax.experimental import pallas as pl
from jax.experimental.pallas import tpu as pltpu
from jax.sharding import PartitionSpec as P

TILE = 128
RB = 16
CB = 16


PRECISE = lax.Precision.HIGHEST
MESH = pl.DeviceIdType.MESH
VMEM = pl.BlockSpec(memory_space=pltpu.VMEM)
SMEM = pl.BlockSpec(memory_space=pltpu.SMEM)


BLOCK = 64
GROUP = 16


def block_inverse(block, low, high):
    finished = []
    lanes = lax.broadcasted_iota(jnp.int32, (GROUP, block.shape[1]), 1)
    inside = (lanes >= high) & (lanes < high + BLOCK)
    for base in range(0, BLOCK, GROUP):
        rows = lax.broadcasted_iota(jnp.int32, block.shape, 0)
        pivots = jnp.ones((GROUP, block.shape[1]), block.dtype)
        factors = []
        for at in range(GROUP):
            lane = low + base + at
            column = jnp.broadcast_to(block[:, lane : lane + 1], block.shape)
            for past, factor in enumerate(factors):
                column = column - factor * column[past : past + 1, :]
            pivots = jnp.where(rows[:GROUP] == at, column[:GROUP], pivots)
            ratio = column * (1.0 / column[at : at + 1, :])
            factors.append(jnp.where(rows > at, ratio, 0.0))
        for at, factor in enumerate(factors):
            block = block - factor * block[at : at + 1, :]
        finished.append(jnp.where(inside, block[:GROUP] * lax.rsqrt(pivots), 0.0))
        block = block[GROUP:]
    return jnp.concatenate(finished, axis=0)


def inverse_kernel(gram_ref, o_ref, work):
    width = gram_ref.shape[0]
    work[:, :width] = gram_ref[...]
    rows = lax.broadcasted_iota(jnp.int32, (width, width), 0)
    lanes = lax.broadcasted_iota(jnp.int32, (width, width), 1)
    work[:, width:] = jnp.where(rows == lanes, 1.0, 0.0)
    rows = lax.broadcasted_iota(jnp.int32, (BLOCK, TILE), 0)
    lanes = lax.broadcasted_iota(jnp.int32, (BLOCK, TILE), 1)
    block = gram_ref[:BLOCK, :TILE]
    for index in range(width // BLOCK):
        start = index * BLOCK
        after = start + BLOCK
        near = start // TILE * TILE
        low = start - near
        high = TILE - BLOCK - low
        inside = (lanes >= low) & (lanes < low + BLOCK)
        block = jnp.where(inside, block, jnp.where(lanes - high == rows, 1.0, 0.0))
        inverse = block_inverse(block, low, high)
        inverse = inverse[:, high : high + BLOCK]
        if after < width:
            near = after // TILE * TILE
            low = after - near
            window = precise(inverse, work[start:after, near : near + TILE], ((1,), (0,)))
            block = work[after : after + BLOCK, near : near + TILE] - precise(
                window[:, low : low + BLOCK], window, ((0,), (0,))
            )
        solved = precise(inverse, work[start:after, :], ((1,), (0,)))
        o_ref[start:after, :] = solved[:, width:]
        if after < width:
            update = precise(solved[:, after:width], solved, ((0,), (0,)))
            work[after:, :] = work[after:, :] - update


def greet():
    barrier = pltpu.get_barrier_semaphore()
    n, m = lax.axis_size("term"), lax.axis_size("doc")
    me, doc = lax.axis_index("term"), lax.axis_index("doc")
    peers = [{"term": lax.rem(me + step, n)} for step in range(1, n)]
    for step in range(1, m):
        there = lax.rem(doc + step, m)
        peers += [{"doc": there}, {"doc": there, "term": me + 1 - 2 * lax.rem(me, 2)}]
    for peer in peers:
        pl.semaphore_signal(barrier, inc=1, device_id=peer, device_id_type=MESH)
    pl.semaphore_wait(barrier, len(peers))


def remote(source, target, send_sem, recv_sem, axis, peer):
    return pltpu.make_async_remote_copy(
        src_ref=source,
        dst_ref=target,
        send_sem=send_sem,
        recv_sem=recv_sem,
        device_id=axis if peer is None else {axis: peer},
        device_id_type=MESH,
    )


def paired():
    n, me = lax.axis_size("term"), lax.axis_index("term")
    return n // 2, me // 2, lax.rem(me, 2)


def semaphores(*sizes):
    return [pltpu.SemaphoreType.DMA((size,)) for size in sizes]


def split3(value):
    high = value.astype(jnp.bfloat16)
    rest = value - high.astype(jnp.float32)
    middle = rest.astype(jnp.bfloat16)
    return high, middle, (rest - middle.astype(jnp.float32)).astype(jnp.bfloat16)


def spread(value, parts):
    high, middle, low = (part.astype(jnp.float32) for part in split3(value))
    blocks, depth, lanes = parts.shape
    rows = lax.broadcasted_iota(jnp.int32, (depth, lanes), 0)
    for block in range(blocks):
        at = slice(block, block + 1)
        picked = jnp.where(rows == 0, high[at], jnp.where(rows == 1, middle[at], low[at]))
        parts[block] = jnp.where(rows < 3, picked, 0.0).astype(jnp.bfloat16)


def tile_sums(tiles, source_ids, parts, sums, target, forward):
    slots = sums.shape[0]
    for slot in range(slots):
        product = lax.dot_general(
            parts[source_ids[0, slot]],
            tiles[slot],
            (((1,), (1 if forward else 0,)), ((), ())),
            preferred_element_type=jnp.float32,
        )
        sums[slot : slot + 1, :] = product[0:1] + product[1:2] + product[2:3]
    stacked = jnp.concatenate(split3(sums[...]), axis=0)
    return jnp.dot(target, stacked, preferred_element_type=jnp.float32)


def start_exchange(held, axis, send_sem, recv_sem):
    n, me = lax.axis_size(axis), lax.axis_index(axis)
    copies = []
    for step in range(1, n):
        copy = remote(
            held.at[0], held.at[step], send_sem.at[step], recv_sem.at[step], axis, lax.rem(me + step, n)
        )
        copy.start()
        copies.append(copy)
    return copies


def finish_exchange(copies, held, axis):
    n, me = lax.axis_size(axis), lax.axis_index(axis)
    for copy in copies:
        copy.wait()
    total = held[me]
    for source in range(1, n):
        total = total + held[lax.rem(me - source + n, n)]
    return total


def scale_phase(
    meanwhile,
    count,
    rows_hbm,
    cols_hbm,
    tiles_hbm,
    start_hbm,
    row_ref,
    col_ref,
    weight_ref,
    mean_ref,
    start_ref,
    dense_ref,
    turned_ref,
    row_ids,
    col_ids,
    lanes,
    places,
    lookup,
    tiles,
    flipped,
    parts,
    sums,
    held_a,
    held_b,
    held_c,
    held_d,
    held_e,
    load_sem,
    *sems,
):
    slots = tiles_hbm.shape[0]
    sources = [rows_hbm, cols_hbm, rows_hbm, cols_hbm, start_hbm, tiles_hbm]
    targets = [row_ids, col_ids, lanes.at[0], lanes.at[1], start_ref, tiles.at[pl.ds(0, slots)]]
    loads = [
        pltpu.make_async_copy(source, target, load_sem.at[k])
        for k, (source, target) in enumerate(zip(sources, targets))
    ]
    for load in loads:
        load.start()
    tiles[slots] = jnp.zeros(tiles.shape[1:], tiles.dtype)
    flipped[slots] = jnp.zeros(tiles.shape[1:], tiles.dtype)
    blocks = row_ref.shape[0]
    spread(jnp.ones(row_ref.shape, jnp.float32), parts)
    for load in loads[:4]:
        load.wait()
    used = count[0, 0]
    place = lax.broadcasted_iota(jnp.int32, (blocks, slots), 0)
    live = lax.broadcasted_iota(jnp.int32, (blocks, slots), 1) < used
    to_rows, to_cols = (
        jnp.concatenate([jnp.where(live & (place == lanes[k]), 1.0, 0.0)] * 3, axis=1).astype(jnp.bfloat16)
        for k in range(2)
    )
    row = lax.broadcasted_iota(jnp.int32, places.shape, 0)
    col = lax.broadcasted_iota(jnp.int32, places.shape, 1)
    table = jnp.full(places.shape, slots, jnp.int32)
    for slot in range(slots):
        found = (row == row_ids[0, slot]) & (col == jnp.where(slot < used, col_ids[0, slot], -1))
        table = jnp.where(found, slot, table)
    places[...] = table
    keep = pltpu.make_async_copy(places, lookup, load_sem.at[7])
    keep.start()
    greet()

    def build(out_ref, source, turn):
        def place_row(outer, carry):
            at = pl.multiple_of(outer * TILE, TILE)
            for inner in range(blocks):
                slot = lookup[inner, outer] if turn else lookup[outer, inner]
                tile = source[slot]
                out_ref[pl.ds(at, TILE), inner * TILE : (inner + 1) * TILE] = tile
            return carry

        lax.fori_loop(0, blocks, place_row, 0)

    def flip(slot, carry):
        flipped[slot] = tiles[slot].T
        return carry

    loads[4].wait()
    mean = jnp.sum(start_ref[...].astype(jnp.float32), axis=0, keepdims=True)
    keep.wait()
    loads[5].wait()
    held_a[0, :blocks, :] = tile_sums(tiles, col_ids, parts, sums, to_rows, True)
    extra = held_a.shape[1] - blocks
    pieces = [mean[:, at : at + TILE] for at in range(0, mean.shape[1], TILE)]
    pieces.append(jnp.zeros((extra - len(pieces), TILE), jnp.float32))
    held_a[0, blocks:, :] = jnp.concatenate(pieces, axis=0)
    copies = start_exchange(held_a, "doc", *sems[0:2])
    build(dense_ref, tiles, False)
    joined = finish_exchange(copies, held_a, "doc")
    mean_ref[...] = joined[blocks:, :]
    spread(1.0 / joined[:blocks], parts)

    held_b[0] = tile_sums(tiles, row_ids, parts, sums, to_cols, False)
    copies = start_exchange(held_b, "term", *sems[2:4])
    lax.fori_loop(0, slots, flip, 0)
    total = finish_exchange(copies, held_b, "term")
    spread(1.0 / total, parts)

    held_c[0] = tile_sums(flipped, col_ids, parts, sums, to_rows, False)
    copies = start_exchange(held_c, "doc", *sems[4:6])
    build(turned_ref, flipped, True)
    row_scale = 1.0 / finish_exchange(copies, held_c, "doc")
    row_ref[...] = row_scale
    spread(row_scale, parts)

    held_d[0] = tile_sums(tiles, row_ids, parts, sums, to_cols, False)
    copies = start_exchange(held_d, "term", *sems[6:8])
    meanwhile()
    col_ref[...] = 1.0 / finish_exchange(copies, held_d, "term")

    def weigh():
        spread(col_ref[...], parts)
        held_e[0] = tile_sums(flipped, col_ids, parts, sums, to_rows, False)
        return start_exchange(held_e, "doc", *sems[8:10])

    return weigh


def scale_scratch(terms, docs, width, slots, kind):
    m, n = lax.axis_size("doc"), lax.axis_size("term")
    vector = pltpu.VMEM((RB, TILE), jnp.float32)
    extra = -(-width // (8 * TILE)) * 8
    stack = pltpu.VMEM((slots + 1, TILE, TILE), kind)

    def held(count, more=0):
        return pltpu.VMEM((count, RB + more, TILE), jnp.float32)

    return [
        vector,
        pltpu.VMEM((extra, TILE), jnp.float32),
        pltpu.VMEM((docs, width), kind),
        pltpu.VMEM((terms, docs), kind),
        pltpu.VMEM((docs, terms), kind),
        pltpu.SMEM((1, slots), jnp.int32),
        pltpu.SMEM((1, slots), jnp.int32),
        pltpu.VMEM((2, 1, slots), jnp.int32),
        pltpu.VMEM((RB, TILE), jnp.int32),
        pltpu.SMEM((RB, TILE), jnp.int32),
        stack,
        stack,
        pltpu.VMEM((RB, 16, TILE), jnp.bfloat16),
        pltpu.VMEM((slots, TILE), jnp.float32),
        held(m, extra),
        held(n),
        held(m),
        held(n),
        held(m),
        pltpu.SemaphoreType.DMA((8,)),
    ] + semaphores(m, m, n, n, m, m, n, n, m, m)


SCALE_REFS = 30


CODES = 32760.0
OCTAVE = 256.0 / math.log(2.0)


def encode(value):
    rows, lanes = value.shape
    groups = value.reshape(rows // 8, 8, lanes)
    top = jnp.maximum(jnp.max(jnp.abs(groups), axis=0), 1e-30)
    level = jnp.ceil(jnp.log(top) * OCTAVE)
    codes = jnp.round(groups * (jnp.exp(level * (-1.0 / OCTAVE)) * CODES))
    whole = jnp.concatenate([codes.reshape(rows, lanes), level, level], axis=0)
    return whole.astype(jnp.int32).astype(jnp.int16)


def decode(block):
    rows, lanes = block.shape[0] - 16, block.shape[1]
    value = block.astype(jnp.int32).astype(jnp.float32)
    scale = jnp.exp(value[rows : rows + 8] * (1.0 / OCTAVE)) * (1.0 / CODES)
    return (value[:rows].reshape(rows // 8, 8, lanes) * scale[None]).reshape(rows, lanes)


def grid_of(n):
    nx = int(math.isqrt(n))
    while n % nx:
        nx -= 1
    return nx, n // nx


def turn_out(vector_ref, block, lanes):
    row = jnp.broadcast_to(vector_ref[pl.ds(block, 1), :], (TILE, TILE))
    column = row.T
    return jnp.concatenate([column] * (lanes // TILE), axis=1)


def precise(a, b, dims):
    return lax.dot_general(
        a, b, (dims, ((), ())), precision=PRECISE, preferred_element_type=jnp.float32
    )


def pack_gram(gram, extras, packed):
    groups, rows = packed.shape[0], packed.shape[1] - 8
    row = lax.broadcasted_iota(jnp.int32, (TILE, TILE), 0)
    lane = lax.broadcasted_iota(jnp.int32, (TILE, TILE), 1)
    last = gram[TILE:, TILE:]
    packed_rows = [jnp.where(row <= lane, gram[:TILE, :TILE], last), gram[:TILE, TILE:]]
    packed_rows = jnp.concatenate(packed_rows, axis=0)
    diagonal = jnp.sum(jnp.where(row == lane, last, 0.0), axis=0, keepdims=True)
    extras = [diagonal] + extras
    extras.append(jnp.zeros((8 - len(extras), TILE), jnp.float32))
    for group in range(groups):
        packed[group, :rows, :] = packed_rows[group * rows : (group + 1) * rows]
        packed[group, rows:, :] = (
            jnp.concatenate(extras, axis=0) if group == 0 else jnp.zeros((8, TILE), jnp.float32)
        )


def unpack_gram(packed, gram):
    rows = packed.shape[1] - 8
    row = lax.broadcasted_iota(jnp.int32, (TILE, TILE), 0)
    lane = lax.broadcasted_iota(jnp.int32, (TILE, TILE), 1)
    half = packed.shape[0] // 2
    both = jnp.concatenate([packed[g, :rows, :] for g in range(half)], axis=0)
    cross = jnp.concatenate([packed[half + g, :rows, :] for g in range(half)], axis=0)
    other = both.T
    gram[:TILE, :TILE] = jnp.where(row <= lane, both, other)
    gram[:TILE, TILE:] = cross
    gram[TILE:, :TILE] = jnp.zeros((TILE, TILE), jnp.float32)
    diagonal = jnp.broadcast_to(packed[0, rows : rows + 1, :], (TILE, TILE))
    last = jnp.where(row > lane, both, jnp.where(row == lane, diagonal, other))
    gram[TILE:, TILE:] = last


def gram_steps(x_ref, o_ref, landing, held, *sems):
    nz, z, c = paired()
    m, my = lax.axis_size("doc"), lax.axis_index("doc")
    steps = [(step, flip) for step in range(m) for flip in range(2) if step or flip]

    def peer(step, flip):
        there = lax.rem(my + step, m)
        core = 1 - c if flip else c
        return 2 * there + core, {"doc": there, "term": 2 * z + core}

    def exchange(source, target, send_sem, recv_sem):
        copies = []
        for step, flip in steps:
            group, place = peer(step, flip)
            slot = 2 * step + flip
            copy = remote(
                source(group), target(slot), send_sem.at[slot], recv_sem.at[slot], place, None
            )
            copy.start()
            copies.append(copy)
        return copies

    mine = 2 * my + c
    copies = exchange(lambda g: x_ref.at[g], lambda k: landing.at[k], *sems[0:2])
    yield
    total = x_ref[mine]
    for (step, flip), copy in zip(steps, copies):
        copy.wait()
        total = total + landing[2 * step + flip]
    held[0] = total
    copies = []
    for step in range(1, nz):
        copy = remote(
            held.at[0], held.at[step], sems[2].at[step], sems[3].at[step], "term", 2 * lax.rem(z + step, nz) + c
        )
        copy.start()
        copies.append(copy)
    yield
    for copy in copies:
        copy.wait()
    total = held[z]
    for source in range(1, nz):
        total = total + held[lax.rem(z - source + nz, nz)]
    o_ref[mine] = total
    copies = exchange(lambda g: o_ref.at[mine], lambda k: o_ref.at[mine], *sems[4:6])
    yield
    for copy in copies:
        copy.wait()


def gram_scratch():
    nz, m = lax.axis_size("term") // 2, lax.axis_size("doc")
    rows = TILE // m + 8
    packed = pltpu.VMEM((2 * m, rows, TILE), jnp.float32)
    return [packed, packed, packed, pltpu.VMEM((nz, rows, TILE), jnp.float32)] + semaphores(
        2 * m, 2 * m, nz, nz, 2 * m, 2 * m
    )


GRAM_REFS = 10


def whole_kernel(
    count,
    rows_hbm,
    cols_hbm,
    tiles_hbm,
    start_hbm,
    row_ref,
    col_ref,
    left_out,
    right_out,
    row_turn,
    col_turn,
    scaled,
    partial,
    send_a,
    recv_a,
    send_b,
    recv_b,
    gathered,
    factor,
    right_sum,
    near_send,
    near_recv,
    far_send,
    far_recv,
    right_parts,
    inverse_ref,
    halves,
    gram,
    work,
    *rest,
):
    left_gram, right_gram = rest[:GRAM_REFS], rest[GRAM_REFS : 2 * GRAM_REFS]
    scale_refs = rest[2 * GRAM_REFS : 2 * GRAM_REFS + SCALE_REFS]
    weight_ref, mean_ref, start_ref, matrix, turned = scale_refs[:5]
    held_e = scale_refs[18]
    sems = rest[2 * GRAM_REFS + SCALE_REFS :]
    n, m = lax.axis_size("term"), lax.axis_size("doc")
    nz, z, c = paired()
    doc = lax.axis_index("doc")
    nx, ny = grid_of(m)
    x, y = lax.rem(doc, nx), doc // nx
    terms, width = left_out.shape
    docs = right_out.shape[0]
    share, piece = terms // m, docs // n
    docs_total = docs * m

    def turn_rows():
        def turn(block, carry):
            at = pl.ds(pl.multiple_of(block * TILE, TILE), TILE)
            row_turn[at, :] = turn_out(row_ref, block, TILE)
            return carry

        lax.fori_loop(0, terms // TILE, turn, 0)

    weigh = scale_phase(
        turn_rows,
        count,
        rows_hbm,
        cols_hbm,
        tiles_hbm,
        start_hbm,
        row_ref,
        col_ref,
        *scale_refs,
    )

    def axes(flow):
        return (x, nx, y, ny) if flow == 0 else (y, ny, x, nx)

    def device(flow, first, second):
        return second * nx + first if flow == 0 else first * nx + second

    def lanes(flow):
        return slice(flow * TILE, (flow + 1) * TILE)

    def prepare(block, carry):
        at = pl.ds(pl.multiple_of(block * TILE, TILE), TILE)
        column = turn_out(col_ref, block, width)
        col_turn[at, :] = column[:, :TILE]
        scaled[at, :] = (column * start_ref[at, :].astype(jnp.float32)).astype(jnp.bfloat16)
        return carry

    lax.fori_loop(0, docs // TILE, prepare, 0)

    steps = [(dx, dy) for dx in range(nx) for dy in range(ny)]
    steps.sort(key=lambda s: -((s[0] > 0) + (s[1] > 0)))
    copies_a, copies_b = {}, {}
    for dx, dy in steps:
        target = lax.rem(y + dy, ny) * nx + lax.rem(x + dx, nx)
        at = pl.ds(pl.multiple_of(target * share, share), share)
        product = jnp.dot(matrix[at, :], scaled[...], preferred_element_type=jnp.float32)
        column = row_turn[at, :]
        product = product * jnp.concatenate([column] * (width // TILE), axis=1)
        partial[dy * nx + dx] = product
        for flow in range(2):
            a, n1, b, n2 = axes(flow)
            s1, s2 = (dx, dy) if flow == 0 else (dy, dx)
            if s1 == 0:
                continue
            slot = s1 * n2 + s2
            send_a[flow, slot] = encode(product[:, lanes(flow)])
            copies_a[flow, s1, s2] = remote(
                send_a.at[flow, slot],
                recv_a.at[flow, slot],
                sems[0].at[flow, slot],
                sems[1].at[flow, slot],
                "doc",
                device(flow, lax.rem(a + s1, n1), b),
            )
            copies_a[flow, s1, s2].start()

    weight_copies = weigh()

    def own(flow, s2):
        dx, dy = (0, s2) if flow == 0 else (s2, 0)
        return partial[dy * nx + dx, :, lanes(flow)]

    def landed(flow, s2):
        a, n1, b, n2 = axes(flow)
        total = own(flow, s2)
        for s1 in range(1, n1):
            copies_a[flow, s1, s2].wait()
            total = total + decode(recv_a[flow, s1 * n2 + s2])
        return total

    for flow in range(2):
        a, n1, b, n2 = axes(flow)
        for s2 in range(1, n2):
            send_b[flow, s2] = encode(landed(flow, s2))
            copies_b[flow, s2] = remote(
                send_b.at[flow, s2],
                recv_b.at[flow, s2],
                sems[2].at[flow, s2],
                sems[3].at[flow, s2],
                "doc",
                device(flow, a, lax.rem(b + s2, n2)),
            )
            copies_b[flow, s2].start()

    weight_ref[...] = row_ref[...] * finish_exchange(weight_copies, held_e, "doc")
    blocks_of_share = share // TILE
    weight = jnp.concatenate(
        [turn_out(weight_ref, doc * blocks_of_share + k, TILE) for k in range(blocks_of_share)], axis=0
    )
    copies_c, copies_d = {}, {}
    left = []
    for flow in range(2):
        a, n1, b, n2 = axes(flow)
        total = landed(flow, 0)
        for s2 in range(1, n2):
            copies_b[flow, s2].wait()
            total = total + decode(recv_b[flow, s2])
        total = total - weight * (mean_ref[flow : flow + 1, :] * (1.0 / docs_total))
        left.append(total)
        gathered[flow, doc] = encode(total)
        for s1 in range(1, n1):
            copies_c[flow, s1] = remote(
                gathered.at[flow, doc],
                gathered.at[flow, doc],
                sems[4].at[flow, s1],
                sems[5].at[flow, s1],
                "doc",
                device(flow, lax.rem(a + s1, n1), b),
            )
            copies_c[flow, s1].start()

    left_share = jnp.concatenate(left, axis=1)
    pack_gram(
        precise(left_share, left_share, ((0,), (0,))) * (1.0 / (terms * n)),
        [jnp.sum(weight * part, axis=0, keepdims=True) for part in left],
        left_gram[0],
    )
    left_steps = gram_steps(*left_gram)
    next(left_steps)

    def unpack(flow, block):
        at = pl.ds(pl.multiple_of(block * share, share), share)
        value = decode(gathered[flow, block]) * row_turn[at, :]
        factor[at, lanes(flow)] = value.astype(jnp.bfloat16)

    def multiply(block, first_flow, flows, fresh):
        at = pl.ds(pl.multiple_of(block * share, share), share)
        cols = slice(first_flow * TILE, (first_flow + flows) * TILE)
        tall = docs // 2

        def rows_of(k, carry):
            rows = pl.ds(pl.multiple_of(k * tall, tall), tall)
            product = jnp.dot(
                turned[rows, at], factor[at, cols], preferred_element_type=jnp.float32
            )
            right_sum[rows, cols] = product if fresh else right_sum[rows, cols] + product
            return carry

        lax.fori_loop(0, 2, rows_of, 0)

    def source_of(flow, s1, s2):
        a, n1, b, n2 = axes(flow)
        return device(flow, lax.rem(a - s1 + n1, n1), lax.rem(b - s2 + n2, n2))

    for flow in range(2):
        unpack(flow, doc)
    multiply(doc, 0, 2, True)
    for flow in range(2):
        a, n1, b, n2 = axes(flow)
        for s1 in range(n1):
            if s1:
                copies_c[flow, s1].wait()
            source = source_of(flow, s1, 0)
            for s2 in range(1, n2):
                copies_d[flow, s1, s2] = remote(
                    gathered.at[flow, source],
                    gathered.at[flow, source],
                    sems[6].at[flow, s1 * n2 + s2],
                    sems[7].at[flow, s1 * n2 + s2],
                    "doc",
                    device(flow, a, lax.rem(b + s2, n2)),
                )
                copies_d[flow, s1, s2].start()
    next(left_steps)
    for flow in range(2):
        for s1 in range(1, axes(flow)[1]):
            block = source_of(flow, s1, 0)
            unpack(flow, block)
            multiply(block, flow, 1, False)
    for flow in range(2):
        for s2 in range(1, axes(flow)[3]):
            copies_d[flow, 0, s2].wait()
            block = source_of(flow, 0, s2)
            unpack(flow, block)
            multiply(block, flow, 1, False)
    across = [(dx, dy) for dx in range(1, nx) for dy in range(1, ny)]
    for dx, dy in across:
        block = source_of(0, dx, dy)
        copies_d[0, dx, dy].wait()
        unpack(0, block)
        copies_d[1, dy, dx].wait()
        unpack(1, block)
        if (dx, dy) != across[-1]:
            multiply(block, 0, 2, False)
    next(left_steps)

    wide = 2 * piece
    last_terms = pl.ds(pl.multiple_of(block * share, share), share)

    def right_product(chunk, core):
        at = pl.ds(pl.multiple_of(core * (docs // 2) + chunk * wide, wide), wide)
        product = jnp.dot(
            turned[at, last_terms], factor[last_terms, :], preferred_element_type=jnp.float32
        )
        column = jnp.concatenate([col_turn[at, :]] * (width // TILE), axis=1)
        return (right_sum[at, :] + product) * column

    sibling = 2 * z + 1 - c
    chunks = [lax.rem(z // 2 + 1 + j, nz // 2) for j in range(nz // 2)]
    near_copies = []
    for j, chunk in enumerate(chunks):
        near_send[j] = right_product(chunk, 1 - c)
        copy = remote(near_send.at[j], near_recv.at[j], sems[8].at[j], sems[9].at[j], "term", sibling)
        copy.start()
        near_copies.append(copy)

    def far_copy(step):
        there = lax.rem(z + step, nz)
        return remote(
            far_send.at[step], far_recv.at[step], sems[10].at[step], sems[11].at[step], "term", 2 * there + c
        )

    for j, chunk in enumerate(chunks):
        product = right_product(chunk, c)
        near_copies[j].wait()
        near_recv[j] = near_recv[j] + product
        last = j + 1 == len(chunks)
        for k in range(2):
            if last and k:
                continue
            inner = 1 - lax.rem(z, 2) if last else k
            step = lax.rem(2 * chunk + inner - z + nz, nz)
            at = pl.ds(pl.multiple_of(inner * piece, piece), piece)
            far_send[step] = encode(near_recv[j, at, :])
            far_copy(step).start()
    for _ in left_steps:
        pass
    unpack_gram(left_gram[1], gram)
    inverse_kernel(gram, inverse_ref, work)

    def split_inverse():
        whiten = inverse_ref[...].T
        high = whiten.astype(jnp.bfloat16)
        halves[0] = high
        halves[1] = (whiten - high.astype(jnp.float32)).astype(jnp.bfloat16)

    def whitened(value):
        high = value.astype(jnp.bfloat16)
        low = (value - high.astype(jnp.float32)).astype(jnp.bfloat16)
        parts = [(high, 0), (low, 0), (high, 1)]
        total = [jnp.dot(v, halves[k], preferred_element_type=jnp.float32) for v, k in parts]
        return total[0] + (total[1] + total[2])

    def finish_left(block):
        at = pl.ds(pl.multiple_of(block * share, share), share)
        value = jnp.concatenate([decode(gathered[flow, block]) for flow in range(2)], axis=1)
        left_out[at, :] = whitened(value).astype(jnp.bfloat16)

    extra = left_gram[1].shape[1] - 8
    weighted = jnp.concatenate(
        [left_gram[1][0, extra + 1 + k : extra + 2 + k, :] for k in range(width // TILE)], axis=1
    )
    lean = precise(jnp.broadcast_to(weighted, (8, width)), inverse_ref[...], ((1,), (1,)))[0:1]
    split_inverse()
    own_rows = pl.ds(pl.multiple_of(lax.rem(z, 2) * piece, piece), piece)
    total = near_recv[len(chunks) - 1, own_rows, :]
    for step in range(1, nz):
        far_copy(step).wait()
        total = total + decode(far_recv[step])
    block = precise(total, inverse_ref[...], ((1,), (1,))) - lean * (1.0 / docs_total)

    me = c * nz + z
    pack_gram(
        precise(block, block, ((0,), (0,))) * (1.0 / docs_total), [], right_gram[0]
    )
    right_steps = gram_steps(*right_gram)
    next(right_steps)
    right_parts[me] = encode(block)
    for k in range(m // 4):
        finish_left(k)
    next(right_steps)
    for k in range(m // 4, 3 * m // 4):
        finish_left(k)
    next(right_steps)
    far_copies = []
    for step in range(1, nz):
        copy = remote(
            right_parts.at[me],
            right_parts.at[me],
            sems[12].at[step],
            sems[13].at[step],
            "term",
            2 * lax.rem(z + step, nz) + c,
        )
        copy.start()
        far_copies.append(copy)
    copy = remote(
        right_parts.at[me], right_parts.at[me], sems[14].at[0], sems[15].at[0], "term", sibling
    )
    copy.start()
    near_copies = [copy]
    for k in range(3 * m // 4, m):
        finish_left(k)
    for _ in right_steps:
        pass
    unpack_gram(right_gram[1], gram)
    inverse_kernel(gram, inverse_ref, work)
    split_inverse()

    def finish_right(t):
        at = pl.ds(pl.multiple_of(t * piece, piece), piece)
        right_out[at, :] = whitened(decode(right_parts[t])).astype(jnp.bfloat16)

    for step in range(1, nz):
        far_copies[step - 1].wait()
        t = c * nz + lax.rem(z - step + nz, nz)
        copy = remote(
            right_parts.at[t], right_parts.at[t], sems[14].at[step], sems[15].at[step], "term", sibling
        )
        copy.start()
        near_copies.append(copy)
    for step in range(nz):
        finish_right(c * nz + lax.rem(z - step + nz, nz))
    for step, copy in enumerate(near_copies):
        copy.wait()
        finish_right((1 - c) * nz + lax.rem(z - step + nz, nz))


def emit_kernel(row_ref, col_ref, left_ref, right_ref, *rest):
    outs, sems = rest[:4], rest[4]
    copies = [
        pltpu.make_async_copy(source, target, sems.at[k])
        for k, (source, target) in enumerate(zip((row_ref, col_ref, left_ref, right_ref), outs))
    ]
    for copy in copies:
        copy.start()
    for copy in copies:
        copy.wait()


def emit(arrays):
    return pl.pallas_call(
        emit_kernel,
        out_shape=[jax.ShapeDtypeStruct(x.shape, x.dtype) for x in arrays],
        in_specs=[VMEM] * 4,
        out_specs=[pl.BlockSpec(memory_space=pl.ANY)] * 4,
        scratch_shapes=[pltpu.SemaphoreType.DMA((4,))],
        compiler_params=pltpu.CompilerParams(vmem_limit_bytes=4 << 20),
        name="emit",
    )(*arrays)


def per_device(tile_values, tile_rows, tile_cols, tile_count, start_block):
    n, m = lax.axis_size("term"), lax.axis_size("doc")
    nz = n // 2
    terms, (docs, width) = RB * TILE, start_block.shape
    share, piece = terms // m, docs // n
    wide = max(grid_of(m))
    int16, f32, bf16 = jnp.int16, jnp.float32, jnp.bfloat16
    coded = pltpu.VMEM((2, m, share + 16, TILE), int16)
    coded_b = pltpu.VMEM((2, wide, share + 16, TILE), int16)
    far = pltpu.VMEM((nz, piece + 16, width), int16)
    near = pltpu.VMEM((nz // 2, 2 * piece, width), f32)
    pairs = [pltpu.SemaphoreType.DMA((2, size)) for size in (m, m, wide, wide, wide, wide, m, m)]
    vector = jax.ShapeDtypeStruct((RB, TILE), f32)
    hbm = pl.BlockSpec(memory_space=pltpu.HBM)
    outs = pl.pallas_call(
        whole_kernel,
        out_shape=[
            vector,
            vector,
            jax.ShapeDtypeStruct((terms, width), bf16),
            jax.ShapeDtypeStruct((docs, width), bf16),
        ],
        in_specs=[SMEM] + [hbm] * 4,
        out_specs=[VMEM] * 4,
        scratch_shapes=[
            pltpu.VMEM((terms, TILE), f32),
            pltpu.VMEM((docs, TILE), f32),
            pltpu.VMEM((docs, width), bf16),
            pltpu.VMEM((m, share, width), f32),
            coded,
            coded,
            coded_b,
            coded_b,
            coded,
            pltpu.VMEM((terms, width), bf16),
            pltpu.VMEM((docs, width), f32),
            near,
            near,
            far,
            far,
            pltpu.VMEM((n, piece + 16, width), int16),
            pltpu.VMEM((width, width), f32),
            pltpu.VMEM((2, width, width), bf16),
            pltpu.VMEM((width, width), f32),
            pltpu.VMEM((width, 2 * width), f32),
        ]
        + gram_scratch()
        + gram_scratch()
        + scale_scratch(terms, docs, width, tile_values.shape[0], tile_values.dtype)
        + pairs
        + semaphores(*[nz] * 8),
        compiler_params=pltpu.CompilerParams(
            collective_id=0, has_side_effects=True, vmem_limit_bytes=44 << 20
        ),
        name="whole",
    )(
        tile_count,
        *(
            pltpu.with_memory_space_constraint(x, pltpu.HBM)
            for x in (tile_rows, tile_cols, tile_values, start_block)
        ),
    )
    row, col, left_basis, right_basis = emit(outs)
    return (row.reshape(-1), col.reshape(-1), left_basis, right_basis)


def solution(mesh):
    placed = (
        P("term", "doc", None),
        P("term", "doc"),
        P("term", "doc"),
        P("term", "doc"),
        P("doc", None),
    )
    return jax.shard_map(
        per_device,
        mesh=mesh,
        in_specs=placed,
        out_specs=(P("term"), P("doc"), P("term", None), P("doc", None)),
        check_vma=False,
    )
```

```python
import math

import jax
import jax.numpy as jnp
from jax import lax
from jax.experimental import pallas as pl
from jax.experimental.pallas import tpu as pltpu
from jax.sharding import PartitionSpec as P

TILE = 128
RB = 16
CB = 16


PRECISE = lax.Precision.HIGHEST
MESH = pl.DeviceIdType.MESH
VMEM = pl.BlockSpec(memory_space=pltpu.VMEM)
SMEM = pl.BlockSpec(memory_space=pltpu.SMEM)


BLOCK = 64
GROUP = 16


def block_inverse(block, low, high):
    finished = []
    lanes = lax.broadcasted_iota(jnp.int32, (GROUP, block.shape[1]), 1)
    inside = (lanes >= high) & (lanes < high + BLOCK)
    for base in range(0, BLOCK, GROUP):
        rows = lax.broadcasted_iota(jnp.int32, block.shape, 0)
        pivots = jnp.ones((GROUP, block.shape[1]), block.dtype)
        factors = []
        for at in range(GROUP):
            lane = low + base + at
            column = jnp.broadcast_to(block[:, lane : lane + 1], block.shape)
            for past, factor in enumerate(factors):
                column = column - factor * column[past : past + 1, :]
            pivots = jnp.where(rows[:GROUP] == at, column[:GROUP], pivots)
            ratio = column * (1.0 / column[at : at + 1, :])
            factors.append(jnp.where(rows > at, ratio, 0.0))
        for at, factor in enumerate(factors):
            block = block - factor * block[at : at + 1, :]
        finished.append(jnp.where(inside, block[:GROUP] * lax.rsqrt(pivots), 0.0))
        block = block[GROUP:]
    return jnp.concatenate(finished, axis=0)


def inverse_kernel(gram_ref, o_ref, work):
    width = gram_ref.shape[0]
    work[:, :width] = gram_ref[...]
    rows = lax.broadcasted_iota(jnp.int32, (width, width), 0)
    lanes = lax.broadcasted_iota(jnp.int32, (width, width), 1)
    work[:, width:] = jnp.where(rows == lanes, 1.0, 0.0)
    rows = lax.broadcasted_iota(jnp.int32, (BLOCK, TILE), 0)
    lanes = lax.broadcasted_iota(jnp.int32, (BLOCK, TILE), 1)
    block = gram_ref[:BLOCK, :TILE]
    for index in range(width // BLOCK):
        start = index * BLOCK
        after = start + BLOCK
        near = start // TILE * TILE
        low = start - near
        high = TILE - BLOCK - low
        inside = (lanes >= low) & (lanes < low + BLOCK)
        block = jnp.where(inside, block, jnp.where(lanes - high == rows, 1.0, 0.0))
        inverse = block_inverse(block, low, high)
        inverse = inverse[:, high : high + BLOCK]
        if after < width:
            near = after // TILE * TILE
            low = after - near
            window = precise(inverse, work[start:after, near : near + TILE], ((1,), (0,)))
            block = work[after : after + BLOCK, near : near + TILE] - precise(
                window[:, low : low + BLOCK], window, ((0,), (0,))
            )
        solved = precise(inverse, work[start:after, :], ((1,), (0,)))
        o_ref[start:after, :] = solved[:, width:]
        if after < width:
            update = precise(solved[:, after:width], solved, ((0,), (0,)))
            work[after:, :] = work[after:, :] - update


def greet():
    barrier = pltpu.get_barrier_semaphore()
    n, m = lax.axis_size("term"), lax.axis_size("doc")
    me, doc = lax.axis_index("term"), lax.axis_index("doc")
    peers = [{"term": lax.rem(me + step, n)} for step in range(1, n)]
    for step in range(1, m):
        there = lax.rem(doc + step, m)
        peers += [{"doc": there}, {"doc": there, "term": me + 1 - 2 * lax.rem(me, 2)}]
    for peer in peers:
        pl.semaphore_signal(barrier, inc=1, device_id=peer, device_id_type=MESH)
    pl.semaphore_wait(barrier, len(peers))


def remote(source, target, send_sem, recv_sem, axis, peer):
    return pltpu.make_async_remote_copy(
        src_ref=source,
        dst_ref=target,
        send_sem=send_sem,
        recv_sem=recv_sem,
        device_id=axis if peer is None else {axis: peer},
        device_id_type=MESH,
    )


def paired():
    n, me = lax.axis_size("term"), lax.axis_index("term")
    return n // 2, me // 2, lax.rem(me, 2)


def semaphores(*sizes):
    return [pltpu.SemaphoreType.DMA((size,)) for size in sizes]


def split3(value):
    high = value.astype(jnp.bfloat16)
    rest = value - high.astype(jnp.float32)
    middle = rest.astype(jnp.bfloat16)
    return high, middle, (rest - middle.astype(jnp.float32)).astype(jnp.bfloat16)


def spread(value, parts):
    high, middle, low = (part.astype(jnp.float32) for part in split3(value))
    blocks, depth, lanes = parts.shape
    rows = lax.broadcasted_iota(jnp.int32, (depth, lanes), 0)
    for block in range(blocks):
        at = slice(block, block + 1)
        picked = jnp.where(rows == 0, high[at], jnp.where(rows == 1, middle[at], low[at]))
        parts[block] = jnp.where(rows < 3, picked, 0.0).astype(jnp.bfloat16)


def tile_sums(tiles, source_ids, parts, sums, target, forward):
    slots = sums.shape[0]
    for slot in range(slots):
        product = lax.dot_general(
            parts[source_ids[0, slot]],
            tiles[slot],
            (((1,), (1 if forward else 0,)), ((), ())),
            preferred_element_type=jnp.float32,
        )
        sums[slot : slot + 1, :] = product[0:1] + product[1:2] + product[2:3]
    stacked = jnp.concatenate(split3(sums[...]), axis=0)
    return jnp.dot(target, stacked, preferred_element_type=jnp.float32)


def start_exchange(held, axis, send_sem, recv_sem):
    n, me = lax.axis_size(axis), lax.axis_index(axis)
    copies = []
    for step in range(1, n):
        copy = remote(
            held.at[0], held.at[step], send_sem.at[step], recv_sem.at[step], axis, lax.rem(me + step, n)
        )
        copy.start()
        copies.append(copy)
    return copies


def finish_exchange(copies, held, axis):
    n, me = lax.axis_size(axis), lax.axis_index(axis)
    for copy in copies:
        copy.wait()
    total = held[me]
    for source in range(1, n):
        total = total + held[lax.rem(me - source + n, n)]
    return total


def scale_phase(
    meanwhile,
    count,
    rows_hbm,
    cols_hbm,
    tiles_hbm,
    start_hbm,
    row_ref,
    col_ref,
    weight_ref,
    mean_ref,
    start_ref,
    dense_ref,
    turned_ref,
    row_ids,
    col_ids,
    lanes,
    places,
    lookup,
    tiles,
    flipped,
    parts,
    sums,
    held_a,
    held_b,
    held_c,
    held_d,
    held_e,
    load_sem,
    *sems,
):
    slots = tiles_hbm.shape[0]
    sources = [rows_hbm, cols_hbm, rows_hbm, cols_hbm, start_hbm, tiles_hbm]
    targets = [row_ids, col_ids, lanes.at[0], lanes.at[1], start_ref, tiles.at[pl.ds(0, slots)]]
    loads = [
        pltpu.make_async_copy(source, target, load_sem.at[k])
        for k, (source, target) in enumerate(zip(sources, targets))
    ]
    for load in loads:
        load.start()
    tiles[slots] = jnp.zeros(tiles.shape[1:], tiles.dtype)
    flipped[slots] = jnp.zeros(tiles.shape[1:], tiles.dtype)
    blocks = row_ref.shape[0]
    spread(jnp.ones(row_ref.shape, jnp.float32), parts)
    for load in loads[:4]:
        load.wait()
    used = count[0, 0]
    place = lax.broadcasted_iota(jnp.int32, (blocks, slots), 0)
    live = lax.broadcasted_iota(jnp.int32, (blocks, slots), 1) < used
    to_rows, to_cols = (
        jnp.concatenate([jnp.where(live & (place == lanes[k]), 1.0, 0.0)] * 3, axis=1).astype(jnp.bfloat16)
        for k in range(2)
    )
    row = lax.broadcasted_iota(jnp.int32, places.shape, 0)
    col = lax.broadcasted_iota(jnp.int32, places.shape, 1)
    table = jnp.full(places.shape, slots, jnp.int32)
    for slot in range(slots):
        found = (row == row_ids[0, slot]) & (col == jnp.where(slot < used, col_ids[0, slot], -1))
        table = jnp.where(found, slot, table)
    places[...] = table
    keep = pltpu.make_async_copy(places, lookup, load_sem.at[7])
    keep.start()
    greet()

    def build(out_ref, source, turn):
        def place_row(outer, carry):
            at = pl.multiple_of(outer * TILE, TILE)
            for inner in range(blocks):
                slot = lookup[inner, outer] if turn else lookup[outer, inner]
                tile = source[slot]
                out_ref[pl.ds(at, TILE), inner * TILE : (inner + 1) * TILE] = tile
            return carry

        lax.fori_loop(0, blocks, place_row, 0)

    def flip(slot, carry):
        flipped[slot] = tiles[slot].T
        return carry

    loads[4].wait()
    mean = jnp.sum(start_ref[...].astype(jnp.float32), axis=0, keepdims=True)
    keep.wait()
    loads[5].wait()
    held_a[0, :blocks, :] = tile_sums(tiles, col_ids, parts, sums, to_rows, True)
    extra = held_a.shape[1] - blocks
    pieces = [mean[:, at : at + TILE] for at in range(0, mean.shape[1], TILE)]
    pieces.append(jnp.zeros((extra - len(pieces), TILE), jnp.float32))
    held_a[0, blocks:, :] = jnp.concatenate(pieces, axis=0)
    copies = start_exchange(held_a, "doc", *sems[0:2])
    build(dense_ref, tiles, False)
    joined = finish_exchange(copies, held_a, "doc")
    mean_ref[...] = joined[blocks:, :]
    spread(1.0 / joined[:blocks], parts)

    held_b[0] = tile_sums(tiles, row_ids, parts, sums, to_cols, False)
    copies = start_exchange(held_b, "term", *sems[2:4])
    lax.fori_loop(0, slots, flip, 0)
    total = finish_exchange(copies, held_b, "term")
    spread(1.0 / total, parts)

    held_c[0] = tile_sums(flipped, col_ids, parts, sums, to_rows, False)
    copies = start_exchange(held_c, "doc", *sems[4:6])
    build(turned_ref, flipped, True)
    row_scale = 1.0 / finish_exchange(copies, held_c, "doc")
    row_ref[...] = row_scale
    spread(row_scale, parts)

    held_d[0] = tile_sums(tiles, row_ids, parts, sums, to_cols, False)
    copies = start_exchange(held_d, "term", *sems[6:8])
    meanwhile()
    col_ref[...] = 1.0 / finish_exchange(copies, held_d, "term")

    def weigh():
        spread(col_ref[...], parts)
        held_e[0] = tile_sums(flipped, col_ids, parts, sums, to_rows, False)
        return start_exchange(held_e, "doc", *sems[8:10])

    return weigh


def scale_scratch(terms, docs, width, slots, kind):
    m, n = lax.axis_size("doc"), lax.axis_size("term")
    vector = pltpu.VMEM((RB, TILE), jnp.float32)
    extra = -(-width // (8 * TILE)) * 8
    stack = pltpu.VMEM((slots + 1, TILE, TILE), kind)

    def held(count, more=0):
        return pltpu.VMEM((count, RB + more, TILE), jnp.float32)

    return [
        vector,
        pltpu.VMEM((extra, TILE), jnp.float32),
        pltpu.VMEM((docs, width), kind),
        pltpu.VMEM((terms, docs), kind),
        pltpu.VMEM((docs, terms), kind),
        pltpu.SMEM((1, slots), jnp.int32),
        pltpu.SMEM((1, slots), jnp.int32),
        pltpu.VMEM((2, 1, slots), jnp.int32),
        pltpu.VMEM((RB, TILE), jnp.int32),
        pltpu.SMEM((RB, TILE), jnp.int32),
        stack,
        stack,
        pltpu.VMEM((RB, 16, TILE), jnp.bfloat16),
        pltpu.VMEM((slots, TILE), jnp.float32),
        held(m, extra),
        held(n),
        held(m),
        held(n),
        held(m),
        pltpu.SemaphoreType.DMA((8,)),
    ] + semaphores(m, m, n, n, m, m, n, n, m, m)


SCALE_REFS = 30


CODES = 32760.0
OCTAVE = 256.0 / math.log(2.0)


def encode(value):
    rows, lanes = value.shape
    groups = value.reshape(rows // 8, 8, lanes)
    top = jnp.maximum(jnp.max(jnp.abs(groups), axis=0), 1e-30)
    level = jnp.ceil(jnp.log(top) * OCTAVE)
    codes = jnp.round(groups * (jnp.exp(level * (-1.0 / OCTAVE)) * CODES))
    whole = jnp.concatenate([codes.reshape(rows, lanes), level, level], axis=0)
    return whole.astype(jnp.int32).astype(jnp.int16)


def decode(block):
    rows, lanes = block.shape[0] - 16, block.shape[1]
    value = block.astype(jnp.int32).astype(jnp.float32)
    scale = jnp.exp(value[rows : rows + 8] * (1.0 / OCTAVE)) * (1.0 / CODES)
    return (value[:rows].reshape(rows // 8, 8, lanes) * scale[None]).reshape(rows, lanes)


def grid_of(n):
    nx = int(math.isqrt(n))
    while n % nx:
        nx -= 1
    return nx, n // nx


def turn_out(vector_ref, block, lanes):
    row = jnp.broadcast_to(vector_ref[pl.ds(block, 1), :], (TILE, TILE))
    column = row.T
    return jnp.concatenate([column] * (lanes // TILE), axis=1)


def precise(a, b, dims):
    return lax.dot_general(
        a, b, (dims, ((), ())), precision=PRECISE, preferred_element_type=jnp.float32
    )


def pack_gram(gram, extras, packed):
    groups, rows = packed.shape[0], packed.shape[1] - 8
    row = lax.broadcasted_iota(jnp.int32, (TILE, TILE), 0)
    lane = lax.broadcasted_iota(jnp.int32, (TILE, TILE), 1)
    last = gram[TILE:, TILE:]
    packed_rows = [jnp.where(row <= lane, gram[:TILE, :TILE], last), gram[:TILE, TILE:]]
    packed_rows = jnp.concatenate(packed_rows, axis=0)
    diagonal = jnp.sum(jnp.where(row == lane, last, 0.0), axis=0, keepdims=True)
    extras = [diagonal] + extras
    extras.append(jnp.zeros((8 - len(extras), TILE), jnp.float32))
    for group in range(groups):
        packed[group, :rows, :] = packed_rows[group * rows : (group + 1) * rows]
        packed[group, rows:, :] = (
            jnp.concatenate(extras, axis=0) if group == 0 else jnp.zeros((8, TILE), jnp.float32)
        )


def unpack_gram(packed, gram):
    rows = packed.shape[1] - 8
    row = lax.broadcasted_iota(jnp.int32, (TILE, TILE), 0)
    lane = lax.broadcasted_iota(jnp.int32, (TILE, TILE), 1)
    half = packed.shape[0] // 2
    both = jnp.concatenate([packed[g, :rows, :] for g in range(half)], axis=0)
    cross = jnp.concatenate([packed[half + g, :rows, :] for g in range(half)], axis=0)
    other = both.T
    gram[:TILE, :TILE] = jnp.where(row <= lane, both, other)
    gram[:TILE, TILE:] = cross
    gram[TILE:, :TILE] = jnp.zeros((TILE, TILE), jnp.float32)
    diagonal = jnp.broadcast_to(packed[0, rows : rows + 1, :], (TILE, TILE))
    last = jnp.where(row > lane, both, jnp.where(row == lane, diagonal, other))
    gram[TILE:, TILE:] = last


def gram_steps(x_ref, o_ref, landing, held, *sems):
    nz, z, c = paired()
    m, my = lax.axis_size("doc"), lax.axis_index("doc")
    steps = [(step, flip) for step in range(m) for flip in range(2) if step or flip]

    def peer(step, flip):
        there = lax.rem(my + step, m)
        core = 1 - c if flip else c
        return 2 * there + core, {"doc": there, "term": 2 * z + core}

    def exchange(source, target, send_sem, recv_sem):
        copies = []
        for step, flip in steps:
            group, place = peer(step, flip)
            slot = 2 * step + flip
            copy = remote(
                source(group), target(slot), send_sem.at[slot], recv_sem.at[slot], place, None
            )
            copy.start()
            copies.append(copy)
        return copies

    mine = 2 * my + c
    copies = exchange(lambda g: x_ref.at[g], lambda k: landing.at[k], *sems[0:2])
    yield
    total = x_ref[mine]
    for (step, flip), copy in zip(steps, copies):
        copy.wait()
        total = total + landing[2 * step + flip]
    held[0] = total
    copies = []
    for step in range(1, nz):
        copy = remote(
            held.at[0], held.at[step], sems[2].at[step], sems[3].at[step], "term", 2 * lax.rem(z + step, nz) + c
        )
        copy.start()
        copies.append(copy)
    yield
    for copy in copies:
        copy.wait()
    total = held[z]
    for source in range(1, nz):
        total = total + held[lax.rem(z - source + nz, nz)]
    o_ref[mine] = total
    copies = exchange(lambda g: o_ref.at[mine], lambda k: o_ref.at[mine], *sems[4:6])
    yield
    for copy in copies:
        copy.wait()


def gram_scratch():
    nz, m = lax.axis_size("term") // 2, lax.axis_size("doc")
    rows = TILE // m + 8
    packed = pltpu.VMEM((2 * m, rows, TILE), jnp.float32)
    return [packed, packed, packed, pltpu.VMEM((nz, rows, TILE), jnp.float32)] + semaphores(
        2 * m, 2 * m, nz, nz, 2 * m, 2 * m
    )


GRAM_REFS = 10


def whole_kernel(
    count,
    rows_hbm,
    cols_hbm,
    tiles_hbm,
    start_hbm,
    row_ref,
    col_ref,
    left_out,
    right_out,
    row_turn,
    col_turn,
    scaled,
    partial,
    send_a,
    recv_a,
    send_b,
    recv_b,
    gathered,
    factor,
    right_sum,
    near_send,
    near_recv,
    far_send,
    far_recv,
    right_parts,
    inverse_ref,
    halves,
    gram,
    work,
    *rest,
):
    left_gram, right_gram = rest[:GRAM_REFS], rest[GRAM_REFS : 2 * GRAM_REFS]
    scale_refs = rest[2 * GRAM_REFS : 2 * GRAM_REFS + SCALE_REFS]
    weight_ref, mean_ref, start_ref, matrix, turned = scale_refs[:5]
    held_e = scale_refs[18]
    sems = rest[2 * GRAM_REFS + SCALE_REFS :]
    n, m = lax.axis_size("term"), lax.axis_size("doc")
    nz, z, c = paired()
    doc = lax.axis_index("doc")
    nx, ny = grid_of(m)
    x, y = lax.rem(doc, nx), doc // nx
    terms, width = left_out.shape
    docs = right_out.shape[0]
    share, piece = terms // m, docs // n
    docs_total = docs * m

    def turn_rows():
        def turn(block, carry):
            at = pl.ds(pl.multiple_of(block * TILE, TILE), TILE)
            row_turn[at, :] = turn_out(row_ref, block, TILE)
            return carry

        lax.fori_loop(0, terms // TILE, turn, 0)

    weigh = scale_phase(
        turn_rows,
        count,
        rows_hbm,
        cols_hbm,
        tiles_hbm,
        start_hbm,
        row_ref,
        col_ref,
        *scale_refs,
    )

    halves_of = [(0, 1), (2, 3)]
    part_rows = share // 2

    def axes(flow):
        return (x, nx, y, ny) if flow % 2 == 0 else (y, ny, x, nx)

    def device(flow, first, second):
        return second * nx + first if flow % 2 == 0 else first * nx + second

    def step_of(flow, dx, dy):
        return (dx, dy) if flow % 2 == 0 else (dy, dx)

    def lanes(flow):
        return slice(flow // 2 * TILE, (flow // 2 + 1) * TILE)

    def part(flow):
        return slice(flow % 2 * part_rows, (flow % 2 + 1) * part_rows)

    def prepare(block, carry):
        at = pl.ds(pl.multiple_of(block * TILE, TILE), TILE)
        column = turn_out(col_ref, block, width)
        col_turn[at, :] = column[:, :TILE]
        scaled[at, :] = (column * start_ref[at, :].astype(jnp.float32)).astype(jnp.bfloat16)
        return carry

    lax.fori_loop(0, docs // TILE, prepare, 0)

    steps = [(dx, dy) for dx in range(nx) for dy in range(ny)]
    steps.sort(key=lambda s: -((s[0] > 0) + (s[1] > 0)))
    copies_a, copies_b = {}, {}

    def send_first(half, dx, dy):
        for flow in halves_of[half]:
            a, n1, b, n2 = axes(flow)
            s1, s2 = step_of(flow, dx, dy)
            if s1 == 0:
                continue
            slot = s1 * n2 + s2
            send_a[flow, slot] = encode(partial[dy * nx + dx, part(flow), lanes(flow)])
            copies_a[flow, s1, s2] = remote(
                send_a.at[flow, slot],
                recv_a.at[flow, slot],
                sems[0].at[flow, slot],
                sems[1].at[flow, slot],
                "doc",
                device(flow, lax.rem(a + s1, n1), b),
            )
            copies_a[flow, s1, s2].start()

    for dx, dy in steps:
        target = lax.rem(y + dy, ny) * nx + lax.rem(x + dx, nx)
        at = pl.ds(pl.multiple_of(target * share, share), share)
        product = jnp.dot(matrix[at, :], scaled[...], preferred_element_type=jnp.float32)
        column = row_turn[at, :]
        product = product * jnp.concatenate([column] * (width // TILE), axis=1)
        partial[dy * nx + dx] = product
        send_first(0, dx, dy)
    for dx, dy in steps:
        send_first(1, dx, dy)

    weight_copies = weigh()

    def own(flow, s2):
        dx, dy = step_of(flow, 0, s2)
        return partial[dy * nx + dx, part(flow), lanes(flow)]

    def landed(flow, s2):
        a, n1, b, n2 = axes(flow)
        total = own(flow, s2)
        for s1 in range(1, n1):
            copies_a[flow, s1, s2].wait()
            total = total + decode(recv_a[flow, s1 * n2 + s2])
        return total

    for flow in range(4):
        a, n1, b, n2 = axes(flow)
        for s2 in range(1, n2):
            send_b[flow, s2] = encode(landed(flow, s2))
            copies_b[flow, s2] = remote(
                send_b.at[flow, s2],
                recv_b.at[flow, s2],
                sems[2].at[flow, s2],
                sems[3].at[flow, s2],
                "doc",
                device(flow, a, lax.rem(b + s2, n2)),
            )
            copies_b[flow, s2].start()

    weight_ref[...] = row_ref[...] * finish_exchange(weight_copies, held_e, "doc")
    blocks_of_share = share // TILE
    weight = jnp.concatenate(
        [turn_out(weight_ref, doc * blocks_of_share + k, TILE) for k in range(blocks_of_share)], axis=0
    )
    copies_c, copies_d = {}, {}
    left = []
    for flow in range(4):
        a, n1, b, n2 = axes(flow)
        total = landed(flow, 0)
        for s2 in range(1, n2):
            copies_b[flow, s2].wait()
            total = total + decode(recv_b[flow, s2])
        mean = mean_ref[flow // 2 : flow // 2 + 1, :]
        total = total - weight[part(flow)] * (mean * (1.0 / docs_total))
        left.append(total)
        gathered[flow, doc] = encode(total)
        for s1 in range(1, n1):
            copies_c[flow, s1] = remote(
                gathered.at[flow, doc],
                gathered.at[flow, doc],
                sems[4].at[flow, s1],
                sems[5].at[flow, s1],
                "doc",
                device(flow, lax.rem(a + s1, n1), b),
            )
            copies_c[flow, s1].start()

    left = [jnp.concatenate(left[2 * half : 2 * half + 2], axis=0) for half in range(2)]
    left_share = jnp.concatenate(left, axis=1)
    pack_gram(
        precise(left_share, left_share, ((0,), (0,))) * (1.0 / (terms * n)),
        [jnp.sum(weight * half, axis=0, keepdims=True) for half in left],
        left_gram[0],
    )
    left_steps = gram_steps(*left_gram)
    next(left_steps)

    def unpack(flow, block):
        at = pl.ds(pl.multiple_of(block * share + part(flow).start, part_rows), part_rows)
        value = decode(gathered[flow, block]) * row_turn[at, :]
        factor[at, lanes(flow)] = value.astype(jnp.bfloat16)

    def multiply(block, first_flow, flows, fresh):
        at = pl.ds(pl.multiple_of(block * share, share), share)
        cols = slice(first_flow * TILE, (first_flow + flows) * TILE)
        tall = docs // 2

        def rows_of(k, carry):
            rows = pl.ds(pl.multiple_of(k * tall, tall), tall)
            product = jnp.dot(
                turned[rows, at], factor[at, cols], preferred_element_type=jnp.float32
            )
            right_sum[rows, cols] = product if fresh else right_sum[rows, cols] + product
            return carry

        lax.fori_loop(0, 2, rows_of, 0)

    def source_of(flow, s1, s2):
        a, n1, b, n2 = axes(flow)
        return device(flow, lax.rem(a - s1 + n1, n1), lax.rem(b - s2 + n2, n2))

    for flow in range(4):
        unpack(flow, doc)
    multiply(doc, 0, 2, True)

    def landed_from(dx, dy, half):
        block = source_of(0, dx, dy)
        for flow in halves_of[half]:
            s1, s2 = step_of(flow, dx, dy)
            if s2:
                copies_d[flow, s1, s2].wait()
            unpack(flow, block)
        return block

    for flow in range(4):
        a, n1, b, n2 = axes(flow)
        for s1 in range(n1):
            if s1:
                copies_c[flow, s1].wait()
            source = source_of(flow, s1, 0)
            for s2 in range(1, n2):
                copies_d[flow, s1, s2] = remote(
                    gathered.at[flow, source],
                    gathered.at[flow, source],
                    sems[6].at[flow, s1 * n2 + s2],
                    sems[7].at[flow, s1 * n2 + s2],
                    "doc",
                    device(flow, a, lax.rem(b + s2, n2)),
                )
                copies_d[flow, s1, s2].start()
    next(left_steps)
    others = [step for step in reversed(steps) if step != (0, 0)]

    wide = 2 * piece
    sibling = 2 * z + 1 - c
    chunks = [lax.rem(z // 2 + 1 + j, nz // 2) for j in range(nz // 2)]

    def far_copy(half, step):
        there = lax.rem(z + step, nz)
        return remote(
            far_send.at[half, step],
            far_recv.at[half, step],
            sems[10].at[half, step],
            sems[11].at[half, step],
            "term",
            2 * there + c,
        )

    for half in range(2):
        for dx, dy in others:
            block = landed_from(dx, dy, half)
            if (dx, dy) != others[-1]:
                multiply(block, half, 1, False)
        cols = slice(half * TILE, (half + 1) * TILE)
        last_terms = pl.ds(pl.multiple_of(block * share, share), share)

        def right_product(chunk, core):
            at = pl.ds(pl.multiple_of(core * (docs // 2) + chunk * wide, wide), wide)
            product = jnp.dot(
                turned[at, last_terms], factor[last_terms, cols], preferred_element_type=jnp.float32
            )
            return (right_sum[at, cols] + product) * col_turn[at, :]

        near_copies = []
        for j, chunk in enumerate(chunks):
            near_send[half, j] = right_product(chunk, 1 - c)
            copy = remote(
                near_send.at[half, j],
                near_recv.at[half, j],
                sems[8].at[half, j],
                sems[9].at[half, j],
                "term",
                sibling,
            )
            copy.start()
            near_copies.append(copy)
        if half == 0:
            next(left_steps)
        for j, chunk in enumerate(chunks):
            product = right_product(chunk, c)
            near_copies[j].wait()
            near_recv[half, j] = near_recv[half, j] + product
            last = j + 1 == len(chunks)
            for k in range(2):
                if last and k:
                    continue
                inner = 1 - lax.rem(z, 2) if last else k
                step = lax.rem(2 * chunk + inner - z + nz, nz)
                at = pl.ds(pl.multiple_of(inner * piece, piece), piece)
                far_send[half, step] = encode(near_recv[half, j, at, :])
                far_copy(half, step).start()
    for _ in left_steps:
        pass
    unpack_gram(left_gram[1], gram)
    inverse_kernel(gram, inverse_ref, work)

    def split_inverse():
        whiten = inverse_ref[...].T
        high = whiten.astype(jnp.bfloat16)
        halves[0] = high
        halves[1] = (whiten - high.astype(jnp.float32)).astype(jnp.bfloat16)

    def whitened(value):
        high = value.astype(jnp.bfloat16)
        low = (value - high.astype(jnp.float32)).astype(jnp.bfloat16)
        parts = [(high, 0), (low, 0), (high, 1)]
        total = [jnp.dot(v, halves[k], preferred_element_type=jnp.float32) for v, k in parts]
        return total[0] + (total[1] + total[2])

    def finish_left(block):
        at = pl.ds(pl.multiple_of(block * share, share), share)
        value = jnp.concatenate(
            [
                jnp.concatenate([decode(gathered[flow, block]) for flow in flows], axis=0)
                for flows in halves_of
            ],
            axis=1,
        )
        left_out[at, :] = whitened(value).astype(jnp.bfloat16)

    extra = left_gram[1].shape[1] - 8
    weighted = jnp.concatenate(
        [left_gram[1][0, extra + 1 + k : extra + 2 + k, :] for k in range(width // TILE)], axis=1
    )
    lean = precise(jnp.broadcast_to(weighted, (8, width)), inverse_ref[...], ((1,), (1,)))[0:1]
    split_inverse()
    own_rows = pl.ds(pl.multiple_of(lax.rem(z, 2) * piece, piece), piece)
    totals = []
    for half in range(2):
        total = near_recv[half, len(chunks) - 1, own_rows, :]
        for step in range(1, nz):
            far_copy(half, step).wait()
            total = total + decode(far_recv[half, step])
        totals.append(total)
    total = jnp.concatenate(totals, axis=1)
    block = precise(total, inverse_ref[...], ((1,), (1,))) - lean * (1.0 / docs_total)

    me = c * nz + z
    pack_gram(
        precise(block, block, ((0,), (0,))) * (1.0 / docs_total), [], right_gram[0]
    )
    right_steps = gram_steps(*right_gram)
    next(right_steps)
    right_parts[me] = encode(block)
    for k in range(m // 4):
        finish_left(k)
    next(right_steps)
    for k in range(m // 4, 3 * m // 4):
        finish_left(k)
    next(right_steps)
    far_copies = []
    for step in range(1, nz):
        copy = remote(
            right_parts.at[me],
            right_parts.at[me],
            sems[12].at[step],
            sems[13].at[step],
            "term",
            2 * lax.rem(z + step, nz) + c,
        )
        copy.start()
        far_copies.append(copy)
    copy = remote(
        right_parts.at[me], right_parts.at[me], sems[14].at[0], sems[15].at[0], "term", sibling
    )
    copy.start()
    near_copies = [copy]
    for k in range(3 * m // 4, m):
        finish_left(k)
    for _ in right_steps:
        pass
    unpack_gram(right_gram[1], gram)
    inverse_kernel(gram, inverse_ref, work)
    split_inverse()

    def finish_right(t):
        at = pl.ds(pl.multiple_of(t * piece, piece), piece)
        right_out[at, :] = whitened(decode(right_parts[t])).astype(jnp.bfloat16)

    for step in range(1, nz):
        far_copies[step - 1].wait()
        t = c * nz + lax.rem(z - step + nz, nz)
        copy = remote(
            right_parts.at[t], right_parts.at[t], sems[14].at[step], sems[15].at[step], "term", sibling
        )
        copy.start()
        near_copies.append(copy)
    for step in range(nz):
        finish_right(c * nz + lax.rem(z - step + nz, nz))
    for step, copy in enumerate(near_copies):
        copy.wait()
        finish_right((1 - c) * nz + lax.rem(z - step + nz, nz))


def emit_kernel(row_ref, col_ref, left_ref, right_ref, *rest):
    outs, sems = rest[:4], rest[4]
    copies = [
        pltpu.make_async_copy(source, target, sems.at[k])
        for k, (source, target) in enumerate(zip((row_ref, col_ref, left_ref, right_ref), outs))
    ]
    for copy in copies:
        copy.start()
    for copy in copies:
        copy.wait()


def emit(arrays):
    return pl.pallas_call(
        emit_kernel,
        out_shape=[jax.ShapeDtypeStruct(x.shape, x.dtype) for x in arrays],
        in_specs=[VMEM] * 4,
        out_specs=[pl.BlockSpec(memory_space=pl.ANY)] * 4,
        scratch_shapes=[pltpu.SemaphoreType.DMA((4,))],
        compiler_params=pltpu.CompilerParams(vmem_limit_bytes=4 << 20),
        name="emit",
    )(*arrays)


def per_device(tile_values, tile_rows, tile_cols, tile_count, start_block):
    n, m = lax.axis_size("term"), lax.axis_size("doc")
    nz = n // 2
    terms, (docs, width) = RB * TILE, start_block.shape
    share, piece = terms // m, docs // n
    wide = max(grid_of(m))
    int16, f32, bf16 = jnp.int16, jnp.float32, jnp.bfloat16
    coded = pltpu.VMEM((4, m, share // 2 + 16, TILE), int16)
    coded_b = pltpu.VMEM((4, wide, share // 2 + 16, TILE), int16)
    far = pltpu.VMEM((2, nz, piece + 16, TILE), int16)
    near = pltpu.VMEM((2, nz // 2, 2 * piece, TILE), f32)
    pairs = [pltpu.SemaphoreType.DMA((4, size)) for size in (m, m, wide, wide, wide, wide, m, m)]
    pairs += [pltpu.SemaphoreType.DMA((2, nz))] * 4
    vector = jax.ShapeDtypeStruct((RB, TILE), f32)
    hbm = pl.BlockSpec(memory_space=pltpu.HBM)
    outs = pl.pallas_call(
        whole_kernel,
        out_shape=[
            vector,
            vector,
            jax.ShapeDtypeStruct((terms, width), bf16),
            jax.ShapeDtypeStruct((docs, width), bf16),
        ],
        in_specs=[SMEM] + [hbm] * 4,
        out_specs=[VMEM] * 4,
        scratch_shapes=[
            pltpu.VMEM((terms, TILE), f32),
            pltpu.VMEM((docs, TILE), f32),
            pltpu.VMEM((docs, width), bf16),
            pltpu.VMEM((m, share, width), f32),
            coded,
            coded,
            coded_b,
            coded_b,
            coded,
            pltpu.VMEM((terms, width), bf16),
            pltpu.VMEM((docs, width), f32),
            near,
            near,
            far,
            far,
            pltpu.VMEM((n, piece + 16, width), int16),
            pltpu.VMEM((width, width), f32),
            pltpu.VMEM((2, width, width), bf16),
            pltpu.VMEM((width, width), f32),
            pltpu.VMEM((width, 2 * width), f32),
        ]
        + gram_scratch()
        + gram_scratch()
        + scale_scratch(terms, docs, width, tile_values.shape[0], tile_values.dtype)
        + pairs
        + semaphores(*[nz] * 4),
        compiler_params=pltpu.CompilerParams(
            collective_id=0, has_side_effects=True, vmem_limit_bytes=44 << 20
        ),
        name="whole",
    )(
        tile_count,
        *(
            pltpu.with_memory_space_constraint(x, pltpu.HBM)
            for x in (tile_rows, tile_cols, tile_values, start_block)
        ),
    )
    row, col, left_basis, right_basis = emit(outs)
    return (row.reshape(-1), col.reshape(-1), left_basis, right_basis)


def solution(mesh):
    placed = (
        P("term", "doc", None),
        P("term", "doc"),
        P("term", "doc"),
        P("term", "doc"),
        P("doc", None),
    )
    return jax.shard_map(
        per_device,
        mesh=mesh,
        in_specs=placed,
        out_specs=(P("term"), P("doc"), P("term", None), P("doc", None)),
        check_vma=False,
    )
```

```python
import math

import jax
import jax.numpy as jnp
from jax import lax
from jax.experimental import pallas as pl
from jax.experimental.pallas import tpu as pltpu
from jax.sharding import PartitionSpec as P

TILE = 128
RB = 16
CB = 16


PRECISE = lax.Precision.HIGHEST
MESH = pl.DeviceIdType.MESH
VMEM = pl.BlockSpec(memory_space=pltpu.VMEM)
SMEM = pl.BlockSpec(memory_space=pltpu.SMEM)


BLOCK = 64
GROUP = 16


def block_inverse(block, low, high):
    finished = []
    lanes = lax.broadcasted_iota(jnp.int32, (GROUP, block.shape[1]), 1)
    inside = (lanes >= high) & (lanes < high + BLOCK)
    for base in range(0, BLOCK, GROUP):
        rows = lax.broadcasted_iota(jnp.int32, block.shape, 0)
        pivots = jnp.ones((GROUP, block.shape[1]), block.dtype)
        factors = []
        for at in range(GROUP):
            lane = low + base + at
            column = jnp.broadcast_to(block[:, lane : lane + 1], block.shape)
            for past, factor in enumerate(factors):
                column = column - factor * column[past : past + 1, :]
            pivots = jnp.where(rows[:GROUP] == at, column[:GROUP], pivots)
            ratio = column * (1.0 / column[at : at + 1, :])
            factors.append(jnp.where(rows > at, ratio, 0.0))
        for at, factor in enumerate(factors):
            block = block - factor * block[at : at + 1, :]
        finished.append(jnp.where(inside, block[:GROUP] * lax.rsqrt(pivots), 0.0))
        block = block[GROUP:]
    return jnp.concatenate(finished, axis=0)


def inverse_kernel(gram_ref, o_ref, work, meanwhile=None):
    width = gram_ref.shape[0]
    work[:, :width] = gram_ref[...]
    rows = lax.broadcasted_iota(jnp.int32, (width, width), 0)
    lanes = lax.broadcasted_iota(jnp.int32, (width, width), 1)
    work[:, width:] = jnp.where(rows == lanes, 1.0, 0.0)
    rows = lax.broadcasted_iota(jnp.int32, (BLOCK, TILE), 0)
    lanes = lax.broadcasted_iota(jnp.int32, (BLOCK, TILE), 1)
    block = gram_ref[:BLOCK, :TILE]
    for index in range(width // BLOCK):
        start = index * BLOCK
        after = start + BLOCK
        near = start // TILE * TILE
        low = start - near
        high = TILE - BLOCK - low
        if meanwhile is not None:
            meanwhile(width // BLOCK - 1 - index)
        inside = (lanes >= low) & (lanes < low + BLOCK)
        block = jnp.where(inside, block, jnp.where(lanes - high == rows, 1.0, 0.0))
        inverse = block_inverse(block, low, high)
        inverse = inverse[:, high : high + BLOCK]
        if after < width:
            near = after // TILE * TILE
            low = after - near
            window = precise(inverse, work[start:after, near : near + TILE], ((1,), (0,)))
            block = work[after : after + BLOCK, near : near + TILE] - precise(
                window[:, low : low + BLOCK], window, ((0,), (0,))
            )
        solved = precise(inverse, work[start:after, :], ((1,), (0,)))
        o_ref[start:after, :] = solved[:, width:]
        if after < width:
            update = precise(solved[:, after:width], solved, ((0,), (0,)))
            work[after:, :] = work[after:, :] - update


def greet():
    barrier = pltpu.get_barrier_semaphore()
    n, m = lax.axis_size("term"), lax.axis_size("doc")
    me, doc = lax.axis_index("term"), lax.axis_index("doc")
    peers = [{"term": lax.rem(me + step, n)} for step in range(1, n)]
    for step in range(1, m):
        there = lax.rem(doc + step, m)
        peers += [{"doc": there}, {"doc": there, "term": me + 1 - 2 * lax.rem(me, 2)}]
    for peer in peers:
        pl.semaphore_signal(barrier, inc=1, device_id=peer, device_id_type=MESH)
    pl.semaphore_wait(barrier, len(peers))


def remote(source, target, send_sem, recv_sem, axis, peer):
    return pltpu.make_async_remote_copy(
        src_ref=source,
        dst_ref=target,
        send_sem=send_sem,
        recv_sem=recv_sem,
        device_id=axis if peer is None else {axis: peer},
        device_id_type=MESH,
    )


def paired():
    n, me = lax.axis_size("term"), lax.axis_index("term")
    return n // 2, me // 2, lax.rem(me, 2)


def semaphores(*sizes):
    return [pltpu.SemaphoreType.DMA((size,)) for size in sizes]


def split3(value):
    high = value.astype(jnp.bfloat16)
    rest = value - high.astype(jnp.float32)
    middle = rest.astype(jnp.bfloat16)
    return high, middle, (rest - middle.astype(jnp.float32)).astype(jnp.bfloat16)


def spread(value, parts):
    high, middle, low = (part.astype(jnp.float32) for part in split3(value))
    blocks, depth, lanes = parts.shape
    rows = lax.broadcasted_iota(jnp.int32, (depth, lanes), 0)
    for block in range(blocks):
        at = slice(block, block + 1)
        picked = jnp.where(rows == 0, high[at], jnp.where(rows == 1, middle[at], low[at]))
        parts[block] = jnp.where(rows < 3, picked, 0.0).astype(jnp.bfloat16)


def tile_sums(tiles, source_ids, parts, sums, target, forward):
    slots = sums.shape[0]
    for slot in range(slots):
        product = lax.dot_general(
            parts[source_ids[0, slot]],
            tiles[slot],
            (((1,), (1 if forward else 0,)), ((), ())),
            preferred_element_type=jnp.float32,
        )
        sums[slot : slot + 1, :] = product[0:1] + product[1:2] + product[2:3]
    stacked = jnp.concatenate(split3(sums[...]), axis=0)
    return jnp.dot(target, stacked, preferred_element_type=jnp.float32)


def start_exchange(held, axis, send_sem, recv_sem):
    n, me = lax.axis_size(axis), lax.axis_index(axis)
    copies = []
    for step in range(1, n):
        copy = remote(
            held.at[0], held.at[step], send_sem.at[step], recv_sem.at[step], axis, lax.rem(me + step, n)
        )
        copy.start()
        copies.append(copy)
    return copies


def finish_exchange(copies, held, axis):
    n, me = lax.axis_size(axis), lax.axis_index(axis)
    for copy in copies:
        copy.wait()
    total = held[me]
    for source in range(1, n):
        total = total + held[lax.rem(me - source + n, n)]
    return total


def scale_phase(
    meanwhile,
    count,
    rows_hbm,
    cols_hbm,
    tiles_hbm,
    start_hbm,
    row_ref,
    col_ref,
    weight_ref,
    mean_ref,
    start_ref,
    dense_ref,
    turned_ref,
    row_ids,
    col_ids,
    lanes,
    places,
    lookup,
    tiles,
    flipped,
    parts,
    sums,
    held_a,
    held_b,
    held_c,
    held_d,
    held_e,
    load_sem,
    *sems,
):
    slots = tiles_hbm.shape[0]
    sources = [rows_hbm, cols_hbm, rows_hbm, cols_hbm, start_hbm, tiles_hbm]
    targets = [row_ids, col_ids, lanes.at[0], lanes.at[1], start_ref, tiles.at[pl.ds(0, slots)]]
    loads = [
        pltpu.make_async_copy(source, target, load_sem.at[k])
        for k, (source, target) in enumerate(zip(sources, targets))
    ]
    for load in loads:
        load.start()
    tiles[slots] = jnp.zeros(tiles.shape[1:], tiles.dtype)
    flipped[slots] = jnp.zeros(tiles.shape[1:], tiles.dtype)
    blocks = row_ref.shape[0]
    spread(jnp.ones(row_ref.shape, jnp.float32), parts)
    for load in loads[:4]:
        load.wait()
    used = count[0, 0]
    place = lax.broadcasted_iota(jnp.int32, (blocks, slots), 0)
    live = lax.broadcasted_iota(jnp.int32, (blocks, slots), 1) < used
    to_rows, to_cols = (
        jnp.concatenate([jnp.where(live & (place == lanes[k]), 1.0, 0.0)] * 3, axis=1).astype(jnp.bfloat16)
        for k in range(2)
    )
    row = lax.broadcasted_iota(jnp.int32, places.shape, 0)
    col = lax.broadcasted_iota(jnp.int32, places.shape, 1)
    table = jnp.full(places.shape, slots, jnp.int32)
    for slot in range(slots):
        found = (row == row_ids[0, slot]) & (col == jnp.where(slot < used, col_ids[0, slot], -1))
        table = jnp.where(found, slot, table)
    places[...] = table
    keep = pltpu.make_async_copy(places, lookup, load_sem.at[7])
    keep.start()
    greet()

    def build(out_ref, source, turn):
        def place_row(outer, carry):
            at = pl.multiple_of(outer * TILE, TILE)
            for inner in range(blocks):
                slot = lookup[inner, outer] if turn else lookup[outer, inner]
                tile = source[slot]
                out_ref[pl.ds(at, TILE), inner * TILE : (inner + 1) * TILE] = tile
            return carry

        lax.fori_loop(0, blocks, place_row, 0)

    def flip(slot, carry):
        flipped[slot] = tiles[slot].T
        return carry

    loads[4].wait()
    mean = jnp.sum(start_ref[...].astype(jnp.float32), axis=0, keepdims=True)
    keep.wait()
    loads[5].wait()
    held_a[0, :blocks, :] = tile_sums(tiles, col_ids, parts, sums, to_rows, True)
    extra = held_a.shape[1] - blocks
    pieces = [mean[:, at : at + TILE] for at in range(0, mean.shape[1], TILE)]
    pieces.append(jnp.zeros((extra - len(pieces), TILE), jnp.float32))
    held_a[0, blocks:, :] = jnp.concatenate(pieces, axis=0)
    copies = start_exchange(held_a, "doc", *sems[0:2])
    build(dense_ref, tiles, False)
    joined = finish_exchange(copies, held_a, "doc")
    mean_ref[...] = joined[blocks:, :]
    spread(1.0 / joined[:blocks], parts)

    held_b[0] = tile_sums(tiles, row_ids, parts, sums, to_cols, False)
    copies = start_exchange(held_b, "term", *sems[2:4])
    lax.fori_loop(0, slots, flip, 0)
    total = finish_exchange(copies, held_b, "term")
    spread(1.0 / total, parts)

    held_c[0] = tile_sums(flipped, col_ids, parts, sums, to_rows, False)
    copies = start_exchange(held_c, "doc", *sems[4:6])
    build(turned_ref, flipped, True)
    row_scale = 1.0 / finish_exchange(copies, held_c, "doc")
    row_ref[...] = row_scale
    spread(row_scale, parts)

    held_d[0] = tile_sums(tiles, row_ids, parts, sums, to_cols, False)
    copies = start_exchange(held_d, "term", *sems[6:8])
    meanwhile()
    col_ref[...] = 1.0 / finish_exchange(copies, held_d, "term")

    def weigh():
        spread(col_ref[...], parts)
        held_e[0] = tile_sums(flipped, col_ids, parts, sums, to_rows, False)
        return start_exchange(held_e, "doc", *sems[8:10])

    return weigh


def scale_scratch(terms, docs, width, slots, kind):
    m, n = lax.axis_size("doc"), lax.axis_size("term")
    vector = pltpu.VMEM((RB, TILE), jnp.float32)
    extra = -(-width // (8 * TILE)) * 8
    stack = pltpu.VMEM((slots + 1, TILE, TILE), kind)

    def held(count, more=0):
        return pltpu.VMEM((count, RB + more, TILE), jnp.float32)

    return [
        vector,
        pltpu.VMEM((extra, TILE), jnp.float32),
        pltpu.VMEM((docs, width), kind),
        pltpu.VMEM((terms, docs), kind),
        pltpu.VMEM((docs, terms), kind),
        pltpu.SMEM((1, slots), jnp.int32),
        pltpu.SMEM((1, slots), jnp.int32),
        pltpu.VMEM((2, 1, slots), jnp.int32),
        pltpu.VMEM((RB, TILE), jnp.int32),
        pltpu.SMEM((RB, TILE), jnp.int32),
        stack,
        stack,
        pltpu.VMEM((RB, 16, TILE), jnp.bfloat16),
        pltpu.VMEM((slots, TILE), jnp.float32),
        held(m, extra),
        held(n),
        held(m),
        held(n),
        held(m),
        pltpu.SemaphoreType.DMA((8,)),
    ] + semaphores(m, m, n, n, m, m, n, n, m, m)


SCALE_REFS = 30


CODES = 32760.0
OCTAVE = 256.0 / math.log(2.0)


def encode(value):
    rows, lanes = value.shape
    groups = value.reshape(rows // 8, 8, lanes)
    top = jnp.maximum(jnp.max(jnp.abs(groups), axis=0), 1e-30)
    level = jnp.ceil(jnp.log(top) * OCTAVE)
    codes = jnp.round(groups * (jnp.exp(level * (-1.0 / OCTAVE)) * CODES))
    whole = jnp.concatenate([codes.reshape(rows, lanes), level, level], axis=0)
    return whole.astype(jnp.int32).astype(jnp.int16)


def decode(block):
    rows, lanes = block.shape[0] - 16, block.shape[1]
    value = block.astype(jnp.int32).astype(jnp.float32)
    scale = jnp.exp(value[rows : rows + 8] * (1.0 / OCTAVE)) * (1.0 / CODES)
    return (value[:rows].reshape(rows // 8, 8, lanes) * scale[None]).reshape(rows, lanes)


def grid_of(n):
    nx = int(math.isqrt(n))
    while n % nx:
        nx -= 1
    return nx, n // nx


def turn_out(vector_ref, block, lanes):
    row = jnp.broadcast_to(vector_ref[pl.ds(block, 1), :], (TILE, TILE))
    column = row.T
    return jnp.concatenate([column] * (lanes // TILE), axis=1)


def precise(a, b, dims):
    return lax.dot_general(
        a, b, (dims, ((), ())), precision=PRECISE, preferred_element_type=jnp.float32
    )


def whitened(value, halves):
    high = value.astype(jnp.bfloat16)
    low = (value - high.astype(jnp.float32)).astype(jnp.bfloat16)
    parts = [(high, 0), (low, 0), (high, 1)]
    total = [jnp.dot(v, halves[k], preferred_element_type=jnp.float32) for v, k in parts]
    return total[0] + (total[1] + total[2])


def pack_gram(gram, extras, packed):
    groups, rows = packed.shape[0], packed.shape[1] - 1
    row = lax.broadcasted_iota(jnp.int32, (TILE, TILE), 0)
    lane = lax.broadcasted_iota(jnp.int32, (TILE, TILE), 1)
    last = gram[TILE:, TILE:]
    packed_rows = [jnp.where(row <= lane, gram[:TILE, :TILE], last), gram[:TILE, TILE:]]
    packed_rows = jnp.concatenate(packed_rows, axis=0)
    diagonal = jnp.sum(jnp.where(row == lane, last, 0.0), axis=0, keepdims=True)
    extras = [diagonal] + extras
    zero = jnp.zeros((1, TILE), jnp.float32)
    for group in range(groups):
        packed[group, :rows, :] = packed_rows[group * rows : (group + 1) * rows]
        packed[group, rows:, :] = extras[group] if group < len(extras) else zero


def unpack_gram(packed, gram):
    rows = packed.shape[1] - 1
    row = lax.broadcasted_iota(jnp.int32, (TILE, TILE), 0)
    lane = lax.broadcasted_iota(jnp.int32, (TILE, TILE), 1)
    half = packed.shape[0] // 2
    both = jnp.concatenate([packed[g, :rows, :] for g in range(half)], axis=0)
    cross = jnp.concatenate([packed[half + g, :rows, :] for g in range(half)], axis=0)
    other = both.T
    gram[:TILE, :TILE] = jnp.where(row <= lane, both, other)
    gram[:TILE, TILE:] = cross
    gram[TILE:, :TILE] = jnp.zeros((TILE, TILE), jnp.float32)
    diagonal = jnp.broadcast_to(packed[0, rows : rows + 1, :], (TILE, TILE))
    last = jnp.where(row > lane, both, jnp.where(row == lane, diagonal, other))
    gram[TILE:, TILE:] = last


def gram_steps(x_ref, o_ref, landing, held, *sems):
    nz, z, c = paired()
    m, my = lax.axis_size("doc"), lax.axis_index("doc")
    steps = [(step, flip) for step in range(m) for flip in range(2) if step or flip]

    def peer(step, flip):
        there = lax.rem(my + step, m)
        core = 1 - c if flip else c
        return 2 * there + core, {"doc": there, "term": 2 * z + core}

    def exchange(source, target, send_sem, recv_sem):
        copies = []
        for step, flip in steps:
            group, place = peer(step, flip)
            slot = 2 * step + flip
            copy = remote(
                source(group), target(slot), send_sem.at[slot], recv_sem.at[slot], place, None
            )
            copy.start()
            copies.append(copy)
        return copies

    mine = 2 * my + c
    copies = exchange(lambda g: x_ref.at[g], lambda k: landing.at[k], *sems[0:2])
    yield
    total = x_ref[mine]
    for (step, flip), copy in zip(steps, copies):
        copy.wait()
        total = total + landing[2 * step + flip]
    held[0] = total
    copies = []
    for step in range(1, nz):
        copy = remote(
            held.at[0], held.at[step], sems[2].at[step], sems[3].at[step], "term", 2 * lax.rem(z + step, nz) + c
        )
        copy.start()
        copies.append(copy)
    yield
    for copy in copies:
        copy.wait()
    total = held[z]
    for source in range(1, nz):
        total = total + held[lax.rem(z - source + nz, nz)]
    o_ref[mine] = total
    copies = exchange(lambda g: o_ref.at[mine], lambda k: o_ref.at[mine], *sems[4:6])
    yield
    for copy in copies:
        copy.wait()


def gram_scratch():
    nz, m = lax.axis_size("term") // 2, lax.axis_size("doc")
    rows = TILE // m + 1
    packed = pltpu.VMEM((2 * m, rows, TILE), jnp.float32)
    return [packed, packed, packed, pltpu.VMEM((nz, rows, TILE), jnp.float32)] + semaphores(
        2 * m, 2 * m, nz, nz, 2 * m, 2 * m
    )


GRAM_REFS = 10


def whole_kernel(
    count,
    rows_hbm,
    cols_hbm,
    tiles_hbm,
    start_hbm,
    row_ref,
    col_ref,
    left_out,
    right_parts,
    halves,
    row_turn,
    col_turn,
    scaled,
    partial,
    send_a,
    recv_a,
    send_b,
    recv_b,
    gathered,
    factor,
    right_sum,
    near_send,
    near_recv,
    far_send,
    far_recv,
    inverse_ref,
    gram,
    work,
    *rest,
):
    left_gram, right_gram = rest[:GRAM_REFS], rest[GRAM_REFS : 2 * GRAM_REFS]
    scale_refs = rest[2 * GRAM_REFS : 2 * GRAM_REFS + SCALE_REFS]
    weight_ref, mean_ref, start_ref, matrix, turned = scale_refs[:5]
    held_e = scale_refs[18]
    sems = rest[2 * GRAM_REFS + SCALE_REFS :]
    n, m = lax.axis_size("term"), lax.axis_size("doc")
    nz, z, c = paired()
    doc = lax.axis_index("doc")
    nx, ny = grid_of(m)
    x, y = lax.rem(doc, nx), doc // nx
    terms, width = left_out.shape
    docs = start_hbm.shape[0]
    share, piece = terms // m, docs // n
    docs_total = docs * m

    def turn_rows():
        def turn(block, carry):
            at = pl.ds(pl.multiple_of(block * TILE, TILE), TILE)
            row_turn[at, :] = turn_out(row_ref, block, TILE)
            return carry

        lax.fori_loop(0, terms // TILE, turn, 0)

    weigh = scale_phase(
        turn_rows,
        count,
        rows_hbm,
        cols_hbm,
        tiles_hbm,
        start_hbm,
        row_ref,
        col_ref,
        *scale_refs,
    )

    halves_of = [(0, 1), (2, 3)]
    part_rows = share // 2

    def axes(flow):
        return (x, nx, y, ny) if flow % 2 == 0 else (y, ny, x, nx)

    def device(flow, first, second):
        return second * nx + first if flow % 2 == 0 else first * nx + second

    def step_of(flow, dx, dy):
        return (dx, dy) if flow % 2 == 0 else (dy, dx)

    def lanes(flow):
        return slice(flow // 2 * TILE, (flow // 2 + 1) * TILE)

    def part(flow):
        return slice(flow % 2 * part_rows, (flow % 2 + 1) * part_rows)

    def prepare(block, carry):
        at = pl.ds(pl.multiple_of(block * TILE, TILE), TILE)
        column = turn_out(col_ref, block, width)
        col_turn[at, :] = column[:, :TILE]
        scaled[at, :] = (column * start_ref[at, :].astype(jnp.float32)).astype(jnp.bfloat16)
        return carry

    lax.fori_loop(0, docs // TILE, prepare, 0, unroll=4)

    steps = [(dx, dy) for dx in range(nx) for dy in range(ny)]
    steps.sort(key=lambda s: -((s[0] > 0) + (s[1] > 0)))
    copies_a, copies_b = {}, {}

    def send_first(half, dx, dy):
        for flow in halves_of[half]:
            a, n1, b, n2 = axes(flow)
            s1, s2 = step_of(flow, dx, dy)
            if s1 == 0:
                continue
            slot = s1 * n2 + s2
            send_a[flow, slot] = encode(partial[dy * nx + dx, part(flow), lanes(flow)])
            copies_a[flow, s1, s2] = remote(
                send_a.at[flow, slot],
                recv_a.at[flow, slot],
                sems[0].at[flow, slot],
                sems[1].at[flow, slot],
                "doc",
                device(flow, lax.rem(a + s1, n1), b),
            )
            copies_a[flow, s1, s2].start()

    for dx, dy in steps:
        target = lax.rem(y + dy, ny) * nx + lax.rem(x + dx, nx)
        at = pl.ds(pl.multiple_of(target * share, share), share)
        product = jnp.dot(matrix[at, :], scaled[...], preferred_element_type=jnp.float32)
        column = row_turn[at, :]
        product = product * jnp.concatenate([column] * (width // TILE), axis=1)
        partial[dy * nx + dx] = product
        send_first(0, dx, dy)
    for dx, dy in steps:
        send_first(1, dx, dy)

    weight_copies = weigh()

    def own(flow, s2):
        dx, dy = step_of(flow, 0, s2)
        return partial[dy * nx + dx, part(flow), lanes(flow)]

    def landed(flow, s2):
        a, n1, b, n2 = axes(flow)
        total = own(flow, s2)
        for s1 in range(1, n1):
            copies_a[flow, s1, s2].wait()
            total = total + decode(recv_a[flow, s1 * n2 + s2])
        return total

    for flow in range(4):
        a, n1, b, n2 = axes(flow)
        for s2 in range(1, n2):
            send_b[flow, s2] = encode(landed(flow, s2))
            copies_b[flow, s2] = remote(
                send_b.at[flow, s2],
                recv_b.at[flow, s2],
                sems[2].at[flow, s2],
                sems[3].at[flow, s2],
                "doc",
                device(flow, a, lax.rem(b + s2, n2)),
            )
            copies_b[flow, s2].start()

    weight_ref[...] = row_ref[...] * finish_exchange(weight_copies, held_e, "doc")
    blocks_of_share = share // TILE
    weight = jnp.concatenate(
        [turn_out(weight_ref, doc * blocks_of_share + k, TILE) for k in range(blocks_of_share)], axis=0
    )
    copies_c, copies_d = {}, {}
    left = []
    for flow in range(4):
        a, n1, b, n2 = axes(flow)
        total = landed(flow, 0)
        for s2 in range(1, n2):
            copies_b[flow, s2].wait()
            total = total + decode(recv_b[flow, s2])
        mean = mean_ref[flow // 2 : flow // 2 + 1, :]
        total = total - weight[part(flow)] * (mean * (1.0 / docs_total))
        left.append(total)
        gathered[flow, doc] = encode(total)
        for s1 in range(1, n1):
            copies_c[flow, s1] = remote(
                gathered.at[flow, doc],
                gathered.at[flow, doc],
                sems[4].at[flow, s1],
                sems[5].at[flow, s1],
                "doc",
                device(flow, lax.rem(a + s1, n1), b),
            )
            copies_c[flow, s1].start()

    left = [jnp.concatenate(left[2 * half : 2 * half + 2], axis=0) for half in range(2)]
    left_share = jnp.concatenate(left, axis=1)
    pack_gram(
        precise(left_share, left_share, ((0,), (0,))) * (1.0 / (terms * n)),
        [jnp.sum(weight * half, axis=0, keepdims=True) for half in left],
        left_gram[0],
    )
    left_steps = gram_steps(*left_gram)
    next(left_steps)

    def unpack(flow, block):
        at = pl.ds(pl.multiple_of(block * share + part(flow).start, part_rows), part_rows)
        value = decode(gathered[flow, block]) * row_turn[at, :]
        factor[at, lanes(flow)] = value.astype(jnp.bfloat16)

    def multiply(block, first_flow, flows, fresh):
        at = pl.ds(pl.multiple_of(block * share, share), share)
        cols = slice(first_flow * TILE, (first_flow + flows) * TILE)
        tall = docs // 2

        def rows_of(k, carry):
            rows = pl.ds(pl.multiple_of(k * tall, tall), tall)
            product = jnp.dot(
                turned[rows, at], factor[at, cols], preferred_element_type=jnp.float32
            )
            right_sum[rows, cols] = product if fresh else right_sum[rows, cols] + product
            return carry

        lax.fori_loop(0, 2, rows_of, 0)

    def source_of(flow, s1, s2):
        a, n1, b, n2 = axes(flow)
        return device(flow, lax.rem(a - s1 + n1, n1), lax.rem(b - s2 + n2, n2))

    for flow in range(4):
        unpack(flow, doc)
    multiply(doc, 0, 2, True)

    def landed_from(dx, dy, half):
        block = source_of(0, dx, dy)
        for flow in halves_of[half]:
            s1, s2 = step_of(flow, dx, dy)
            if s2:
                copies_d[flow, s1, s2].wait()
            unpack(flow, block)
        return block

    for flow in range(4):
        a, n1, b, n2 = axes(flow)
        for s1 in range(n1):
            if s1:
                copies_c[flow, s1].wait()
            source = source_of(flow, s1, 0)
            for s2 in range(1, n2):
                copies_d[flow, s1, s2] = remote(
                    gathered.at[flow, source],
                    gathered.at[flow, source],
                    sems[6].at[flow, s1 * n2 + s2],
                    sems[7].at[flow, s1 * n2 + s2],
                    "doc",
                    device(flow, a, lax.rem(b + s2, n2)),
                )
                copies_d[flow, s1, s2].start()
    next(left_steps)
    others = [step for step in reversed(steps) if step != (0, 0)]

    wide = 2 * piece
    sibling = 2 * z + 1 - c
    chunks = [lax.rem(z // 2 + 1 + j, nz // 2) for j in range(nz // 2)]

    def far_copy(half, step):
        there = lax.rem(z + step, nz)
        return remote(
            far_send.at[half, step],
            far_recv.at[half, step],
            sems[10].at[half, step],
            sems[11].at[half, step],
            "term",
            2 * there + c,
        )

    for half in range(2):
        for dx, dy in others:
            block = landed_from(dx, dy, half)
            if (dx, dy) != others[-1]:
                multiply(block, half, 1, False)
        cols = slice(half * TILE, (half + 1) * TILE)
        last_terms = pl.ds(pl.multiple_of(block * share, share), share)

        def right_product(chunk, core):
            at = pl.ds(pl.multiple_of(core * (docs // 2) + chunk * wide, wide), wide)
            product = jnp.dot(
                turned[at, last_terms], factor[last_terms, cols], preferred_element_type=jnp.float32
            )
            return (right_sum[at, cols] + product) * col_turn[at, :]

        near_copies = []
        for j, chunk in enumerate(chunks):
            near_send[half, j] = right_product(chunk, 1 - c)
            copy = remote(
                near_send.at[half, j],
                near_recv.at[half, j],
                sems[8].at[half, j],
                sems[9].at[half, j],
                "term",
                sibling,
            )
            copy.start()
            near_copies.append(copy)
        if half == 0:
            next(left_steps)
        for j, chunk in enumerate(chunks):
            product = right_product(chunk, c)
            near_copies[j].wait()
            near_recv[half, j] = near_recv[half, j] + product
            last = j + 1 == len(chunks)
            for k in range(2):
                if last and k:
                    continue
                inner = 1 - lax.rem(z, 2) if last else k
                step = lax.rem(2 * chunk + inner - z + nz, nz)
                at = pl.ds(pl.multiple_of(inner * piece, piece), piece)
                far_send[half, step] = encode(near_recv[half, j, at, :])
                far_copy(half, step).start()
    for _ in left_steps:
        pass
    unpack_gram(left_gram[1], gram)
    inverse_kernel(gram, inverse_ref, work)

    def split_inverse():
        whiten = inverse_ref[...].T
        high = whiten.astype(jnp.bfloat16)
        halves[0] = high
        halves[1] = (whiten - high.astype(jnp.float32)).astype(jnp.bfloat16)

    def finish_left(block):
        at = pl.ds(pl.multiple_of(block * share, share), share)
        value = jnp.concatenate(
            [
                jnp.concatenate([decode(gathered[flow, block]) for flow in flows], axis=0)
                for flows in halves_of
            ],
            axis=1,
        )
        left_out[at, :] = whitened(value, halves).astype(jnp.bfloat16)

    extra = left_gram[1].shape[1] - 1
    weighted = jnp.concatenate(
        [left_gram[1][1 + k, extra:, :] for k in range(width // TILE)], axis=1
    )
    lean = precise(jnp.broadcast_to(weighted, (8, width)), inverse_ref[...], ((1,), (1,)))[0:1]
    split_inverse()
    own_rows = pl.ds(pl.multiple_of(lax.rem(z, 2) * piece, piece), piece)
    totals = []
    for half in range(2):
        total = near_recv[half, len(chunks) - 1, own_rows, :]
        for step in range(1, nz):
            far_copy(half, step).wait()
            total = total + decode(far_recv[half, step])
        totals.append(total)
    total = jnp.concatenate(totals, axis=1)
    block = precise(total, inverse_ref[...], ((1,), (1,))) - lean * (1.0 / docs_total)

    me = c * nz + z
    pack_gram(
        precise(block, block, ((0,), (0,))) * (1.0 / docs_total), [], right_gram[0]
    )
    right_steps = gram_steps(*right_gram)
    next(right_steps)
    right_parts[me] = encode(block)
    far_copies = []

    def send_part(step):
        copy = remote(
            right_parts.at[me],
            right_parts.at[me],
            sems[12].at[step],
            sems[13].at[step],
            "term",
            2 * lax.rem(z + step, nz) + c,
        )
        copy.start()
        far_copies.append(copy)

    send_part(1)
    copy = remote(
        right_parts.at[me], right_parts.at[me], sems[14].at[0], sems[15].at[0], "term", sibling
    )
    copy.start()
    near_copies = [copy]
    for k in range(m // 4):
        finish_left(k)
    next(right_steps)
    for k in range(m // 4, 3 * m // 4):
        finish_left(k)
    next(right_steps)
    for step in range(2, nz):
        send_part(step)
    for k in range(3 * m // 4, m):
        finish_left(k)
    for _ in right_steps:
        pass
    unpack_gram(right_gram[1], gram)
    def pass_on(left):
        if left:
            return
        for step in range(1, nz):
            far_copies[step - 1].wait()
            t = c * nz + lax.rem(z - step + nz, nz)
            copy = remote(
                right_parts.at[t],
                right_parts.at[t],
                sems[14].at[step],
                sems[15].at[step],
                "term",
                sibling,
            )
            copy.start()
            near_copies.append(copy)

    inverse_kernel(gram, inverse_ref, work, pass_on)
    split_inverse()

    for copy in near_copies:
        copy.wait()


def emit_kernel(row_ref, col_ref, left_ref, parts_ref, halves, *rest):
    outs, right, sems = rest[:4], rest[4], rest[5]
    right_out = outs[3]
    copies = [
        pltpu.make_async_copy(source, target, sems.at[k])
        for k, (source, target) in enumerate(zip((left_ref, row_ref, col_ref), (outs[2], *outs[:2])))
    ]
    for copy in copies:
        copy.start()
    shares, piece = parts_ref.shape[0], right.shape[0] // parts_ref.shape[0]

    def copy_of(t):
        at = pl.ds(pl.multiple_of(t * piece, piece), piece)
        return pltpu.make_async_copy(right.at[at], right_out.at[at], sems.at[3 + t])

    for t in range(shares):
        right[t * piece : (t + 1) * piece, :] = whitened(decode(parts_ref[t]), halves).astype(
            jnp.bfloat16
        )
        copy_of(t).start()
        copies.append(copy_of(t))
    for copy in copies:
        copy.wait()


def emit(row, col, left, parts, halves, docs):
    width = left.shape[1]
    hbm = pl.BlockSpec(memory_space=pl.ANY)
    right = jax.ShapeDtypeStruct((docs, width), left.dtype)
    return pl.pallas_call(
        emit_kernel,
        out_shape=[jax.ShapeDtypeStruct(x.shape, x.dtype) for x in (row, col, left)] + [right],
        in_specs=[VMEM] * 5,
        out_specs=[hbm] * 4,
        scratch_shapes=[
            pltpu.VMEM(right.shape, right.dtype),
            pltpu.SemaphoreType.DMA((3 + parts.shape[0],)),
        ],
        compiler_params=pltpu.CompilerParams(vmem_limit_bytes=6 << 20),
        name="emit",
    )(row, col, left, parts, halves)


def per_device(tile_values, tile_rows, tile_cols, tile_count, start_block):
    n, m = lax.axis_size("term"), lax.axis_size("doc")
    nz = n // 2
    terms, (docs, width) = RB * TILE, start_block.shape
    share, piece = terms // m, docs // n
    wide = max(grid_of(m))
    int16, f32, bf16 = jnp.int16, jnp.float32, jnp.bfloat16
    coded = pltpu.VMEM((4, m, share // 2 + 16, TILE), int16)
    coded_b = pltpu.VMEM((4, wide, share // 2 + 16, TILE), int16)
    far = pltpu.VMEM((2, nz, piece + 16, TILE), int16)
    near = pltpu.VMEM((2, nz // 2, 2 * piece, TILE), f32)
    pairs = [pltpu.SemaphoreType.DMA((4, size)) for size in (m, m, wide, wide, wide, wide, m, m)]
    pairs += [pltpu.SemaphoreType.DMA((2, nz))] * 4
    vector = jax.ShapeDtypeStruct((RB, TILE), f32)
    hbm = pl.BlockSpec(memory_space=pltpu.HBM)
    outs = pl.pallas_call(
        whole_kernel,
        out_shape=[
            vector,
            vector,
            jax.ShapeDtypeStruct((terms, width), bf16),
            jax.ShapeDtypeStruct((n, piece + 16, width), int16),
            jax.ShapeDtypeStruct((2, width, width), bf16),
        ],
        in_specs=[SMEM] + [hbm] * 4,
        out_specs=[VMEM] * 5,
        scratch_shapes=[
            pltpu.VMEM((terms, TILE), f32),
            pltpu.VMEM((docs, TILE), f32),
            pltpu.VMEM((docs, width), bf16),
            pltpu.VMEM((m, share, width), f32),
            coded,
            coded,
            coded_b,
            coded_b,
            coded,
            pltpu.VMEM((terms, width), bf16),
            pltpu.VMEM((docs, width), f32),
            near,
            near,
            far,
            far,
            pltpu.VMEM((width, width), f32),
            pltpu.VMEM((width, width), f32),
            pltpu.VMEM((width, 2 * width), f32),
        ]
        + gram_scratch()
        + gram_scratch()
        + scale_scratch(terms, docs, width, tile_values.shape[0], tile_values.dtype)
        + pairs
        + semaphores(*[nz] * 4),
        compiler_params=pltpu.CompilerParams(
            collective_id=0, has_side_effects=True, vmem_limit_bytes=44 << 20
        ),
        name="whole",
    )(
        tile_count,
        *(
            pltpu.with_memory_space_constraint(x, pltpu.HBM)
            for x in (tile_rows, tile_cols, tile_values, start_block)
        ),
    )
    row, col, left_basis, right_basis = emit(*outs, docs)
    return (row.reshape(-1), col.reshape(-1), left_basis, right_basis)


def solution(mesh):
    placed = (
        P("term", "doc", None),
        P("term", "doc"),
        P("term", "doc"),
        P("term", "doc"),
        P("doc", None),
    )
    return jax.shard_map(
        per_device,
        mesh=mesh,
        in_specs=placed,
        out_specs=(P("term"), P("doc"), P("term", None), P("doc", None)),
        check_vma=False,
    )
```

```python
import math

import jax
import jax.numpy as jnp
from jax import lax
from jax.experimental import pallas as pl
from jax.experimental.pallas import tpu as pltpu
from jax.sharding import PartitionSpec as P

TILE = 128
RB = 16
CB = 16


PRECISE = lax.Precision.HIGHEST
MESH = pl.DeviceIdType.MESH
VMEM = pl.BlockSpec(memory_space=pltpu.VMEM)
SMEM = pl.BlockSpec(memory_space=pltpu.SMEM)


BLOCK = 64
GROUP = 16


def block_inverse(block, low, high):
    finished = []
    lanes = lax.broadcasted_iota(jnp.int32, (GROUP, block.shape[1]), 1)
    inside = (lanes >= high) & (lanes < high + BLOCK)
    for base in range(0, BLOCK, GROUP):
        rows = lax.broadcasted_iota(jnp.int32, block.shape, 0)
        pivots = jnp.ones((GROUP, block.shape[1]), block.dtype)
        factors = []
        for at in range(GROUP):
            lane = low + base + at
            column = jnp.broadcast_to(block[:, lane : lane + 1], block.shape)
            for past, factor in enumerate(factors):
                column = column - factor * column[past : past + 1, :]
            pivots = jnp.where(rows[:GROUP] == at, column[:GROUP], pivots)
            ratio = column * (1.0 / column[at : at + 1, :])
            factors.append(jnp.where(rows > at, ratio, 0.0))
        for at, factor in enumerate(factors):
            block = block - factor * block[at : at + 1, :]
        finished.append(jnp.where(inside, block[:GROUP] * lax.rsqrt(pivots), 0.0))
        block = block[GROUP:]
    return jnp.concatenate(finished, axis=0)


def inverse_kernel(gram_ref, o_ref, work, meanwhile=None):
    width = gram_ref.shape[0]
    work[:, :width] = gram_ref[...]
    rows = lax.broadcasted_iota(jnp.int32, (width, width), 0)
    lanes = lax.broadcasted_iota(jnp.int32, (width, width), 1)
    work[:, width:] = jnp.where(rows == lanes, 1.0, 0.0)
    rows = lax.broadcasted_iota(jnp.int32, (BLOCK, TILE), 0)
    lanes = lax.broadcasted_iota(jnp.int32, (BLOCK, TILE), 1)
    block = gram_ref[:BLOCK, :TILE]
    for index in range(width // BLOCK):
        start = index * BLOCK
        after = start + BLOCK
        near = start // TILE * TILE
        low = start - near
        high = TILE - BLOCK - low
        if meanwhile is not None:
            meanwhile(width // BLOCK - 1 - index)
        inside = (lanes >= low) & (lanes < low + BLOCK)
        block = jnp.where(inside, block, jnp.where(lanes - high == rows, 1.0, 0.0))
        inverse = block_inverse(block, low, high)
        inverse = inverse[:, high : high + BLOCK]
        if after < width:
            near = after // TILE * TILE
            low = after - near
            window = precise(inverse, work[start:after, near : near + TILE], ((1,), (0,)))
            block = work[after : after + BLOCK, near : near + TILE] - precise(
                window[:, low : low + BLOCK], window, ((0,), (0,))
            )
        solved = precise(inverse, work[start:after, :], ((1,), (0,)))
        o_ref[start:after, :] = solved[:, width:]
        if after < width:
            update = precise(solved[:, after:width], solved, ((0,), (0,)))
            work[after:, :] = work[after:, :] - update


def announce():
    barrier = pltpu.get_barrier_semaphore()
    n, m = lax.axis_size("term"), lax.axis_size("doc")
    me, doc = lax.axis_index("term"), lax.axis_index("doc")
    peers = [{"term": lax.rem(me + step, n)} for step in range(1, n)]
    for step in range(1, m):
        there = lax.rem(doc + step, m)
        peers += [{"doc": there}, {"doc": there, "term": me + 1 - 2 * lax.rem(me, 2)}]
    for peer in peers:
        pl.semaphore_signal(barrier, inc=1, device_id=peer, device_id_type=MESH)
    return len(peers)


def remote(source, target, send_sem, recv_sem, axis, peer):
    return pltpu.make_async_remote_copy(
        src_ref=source,
        dst_ref=target,
        send_sem=send_sem,
        recv_sem=recv_sem,
        device_id=axis if peer is None else {axis: peer},
        device_id_type=MESH,
    )


def paired():
    n, me = lax.axis_size("term"), lax.axis_index("term")
    return n // 2, me // 2, lax.rem(me, 2)


def semaphores(*sizes):
    return [pltpu.SemaphoreType.DMA((size,)) for size in sizes]


def split3(value):
    high = value.astype(jnp.bfloat16)
    rest = value - high.astype(jnp.float32)
    middle = rest.astype(jnp.bfloat16)
    return high, middle, (rest - middle.astype(jnp.float32)).astype(jnp.bfloat16)


def spread(value, parts):
    high, middle, low = (part.astype(jnp.float32) for part in split3(value))
    blocks, depth, lanes = parts.shape
    rows = lax.broadcasted_iota(jnp.int32, (depth, lanes), 0)
    for block in range(blocks):
        at = slice(block, block + 1)
        picked = jnp.where(rows == 0, high[at], jnp.where(rows == 1, middle[at], low[at]))
        parts[block] = jnp.where(rows < 3, picked, 0.0).astype(jnp.bfloat16)


def tile_sums(tiles, source_ids, parts, sums, target, forward):
    slots = sums.shape[0]
    for slot in range(slots):
        product = lax.dot_general(
            parts[source_ids[0, slot]],
            tiles[slot],
            (((1,), (1 if forward else 0,)), ((), ())),
            preferred_element_type=jnp.float32,
        )
        sums[slot : slot + 1, :] = product[0:1] + product[1:2] + product[2:3]
    stacked = jnp.concatenate(split3(sums[...]), axis=0)
    return jnp.dot(target, stacked, preferred_element_type=jnp.float32)


def start_exchange(held, axis, send_sem, recv_sem):
    n, me = lax.axis_size(axis), lax.axis_index(axis)

    def copy_of(step):
        return remote(
            held.at[0], held.at[step], send_sem.at[step], recv_sem.at[step], axis, lax.rem(me + step, n)
        )

    steps = list(range(1, n))
    if axis == "term":
        nz, z, c = paired()
        places = []
        for k in range(nz - 1):
            down, up = nz - 1 - k, k
            down = jnp.where(down <= z, down - 1, down)
            up = jnp.where(up >= z, up + 1, up)
            there = jnp.where(2 * z < nz, down, up)
            places += [2 * there + c, 2 * there + 1 - c]
        places.append(2 * z + 1 - c)
        steps = [lax.rem(place - me + n, n) for place in places]
    for step in steps:
        copy_of(step).start()
    return [copy_of(step) for step in range(1, n)]


def finish_exchange(copies, held, axis):
    n, me = lax.axis_size(axis), lax.axis_index(axis)
    for copy in copies:
        copy.wait()
    total = held[me]
    for source in range(1, n):
        total = total + held[lax.rem(me - source + n, n)]
    return total


def scale_phase(
    meanwhile,
    count,
    rows_hbm,
    cols_hbm,
    tiles_hbm,
    start_hbm,
    row_ref,
    col_ref,
    weight_ref,
    mean_ref,
    start_ref,
    dense_ref,
    turned_ref,
    row_ids,
    col_ids,
    lanes,
    places,
    lookup,
    tiles,
    flipped,
    parts,
    sums,
    held_a,
    held_b,
    held_c,
    held_d,
    held_e,
    load_sem,
    *sems,
):
    expected = announce()
    slots = tiles_hbm.shape[0]
    sources = [rows_hbm, cols_hbm, rows_hbm, cols_hbm]
    targets = [row_ids, col_ids, lanes.at[0], lanes.at[1]]
    quarter = -(-slots // 4)
    for at in range(0, slots, quarter):
        stretch = pl.ds(at, min(quarter, slots - at))
        sources.append(tiles_hbm.at[stretch])
        targets.append(tiles.at[stretch])
    sources.append(start_hbm)
    targets.append(start_ref)
    loads = [
        pltpu.make_async_copy(source, target, load_sem.at[k])
        for k, (source, target) in enumerate(zip(sources, targets))
    ]
    for load in loads:
        load.start()
    tiles[slots] = jnp.zeros(tiles.shape[1:], tiles.dtype)
    flipped[slots] = jnp.zeros(tiles.shape[1:], tiles.dtype)
    blocks = row_ref.shape[0]
    spread(jnp.ones(row_ref.shape, jnp.float32), parts)
    for load in loads[:4]:
        load.wait()
    used = count[0, 0]
    place = lax.broadcasted_iota(jnp.int32, (blocks, slots), 0)
    live = lax.broadcasted_iota(jnp.int32, (blocks, slots), 1) < used
    to_rows, to_cols = (
        jnp.concatenate([jnp.where(live & (place == lanes[k]), 1.0, 0.0)] * 3, axis=1).astype(jnp.bfloat16)
        for k in range(2)
    )
    def build(out_ref, source, turn):
        def place_row(outer, carry):
            at = pl.multiple_of(outer * TILE, TILE)
            for inner in range(blocks):
                slot = lookup[inner, outer] if turn else lookup[outer, inner]
                tile = source[slot]
                out_ref[pl.ds(at, TILE), inner * TILE : (inner + 1) * TILE] = tile
            return carry

        lax.fori_loop(0, blocks, place_row, 0)

    def flip(slot, carry):
        flipped[slot] = tiles[slot].T
        return carry

    for load in loads[4:-1]:
        load.wait()
    held_a[0] = tile_sums(tiles, col_ids, parts, sums, to_rows, True)
    pl.semaphore_wait(pltpu.get_barrier_semaphore(), expected)
    copies = start_exchange(held_a, "doc", *sems[0:2])
    row = lax.broadcasted_iota(jnp.int32, places.shape, 0)
    col = lax.broadcasted_iota(jnp.int32, places.shape, 1)
    table = jnp.full(places.shape, slots, jnp.int32)
    for slot in range(slots):
        found = (row == row_ids[0, slot]) & (col == jnp.where(slot < used, col_ids[0, slot], -1))
        table = jnp.where(found, slot, table)
    places[...] = table
    keep = pltpu.make_async_copy(places, lookup, load_sem.at[9])
    keep.start()
    loads[-1].wait()
    mean = jnp.sum(start_ref[...].astype(jnp.float32), axis=0, keepdims=True)
    extra = held_c.shape[1] - blocks
    pieces = [mean[:, at : at + TILE] for at in range(0, mean.shape[1], TILE)]
    pieces.append(jnp.zeros((extra - len(pieces), TILE), jnp.float32))
    held_c[0, blocks:, :] = jnp.concatenate(pieces, axis=0)
    keep.wait()
    total = finish_exchange(copies, held_a, "doc")
    spread(1.0 / total, parts)

    held_b[0] = tile_sums(tiles, row_ids, parts, sums, to_cols, False)
    copies = start_exchange(held_b, "term", *sems[2:4])
    lax.fori_loop(0, slots, flip, 0)
    total = finish_exchange(copies, held_b, "term")
    spread(1.0 / total, parts)

    held_c[0, :blocks, :] = tile_sums(flipped, col_ids, parts, sums, to_rows, False)
    copies = start_exchange(held_c, "doc", *sems[4:6])
    build(dense_ref, tiles, False)
    joined = finish_exchange(copies, held_c, "doc")
    mean_ref[...] = joined[blocks:, :]
    row_scale = 1.0 / joined[:blocks]
    row_ref[...] = row_scale
    spread(row_scale, parts)

    held_d[0] = tile_sums(tiles, row_ids, parts, sums, to_cols, False)
    copies = start_exchange(held_d, "term", *sems[6:8])
    meanwhile()
    col_ref[...] = 1.0 / finish_exchange(copies, held_d, "term")

    def weigh():
        spread(col_ref[...], parts)
        held_e[0] = tile_sums(flipped, col_ids, parts, sums, to_rows, False)
        copies = start_exchange(held_e, "doc", *sems[8:10])
        build(turned_ref, flipped, True)
        return copies

    return weigh


def scale_scratch(terms, docs, width, slots, kind):
    m, n = lax.axis_size("doc"), lax.axis_size("term")
    vector = pltpu.VMEM((RB, TILE), jnp.float32)
    extra = -(-width // (8 * TILE)) * 8
    stack = pltpu.VMEM((slots + 1, TILE, TILE), kind)

    def held(count, more=0):
        return pltpu.VMEM((count, RB + more, TILE), jnp.float32)

    return [
        vector,
        pltpu.VMEM((extra, TILE), jnp.float32),
        pltpu.VMEM((docs, width), kind),
        pltpu.VMEM((terms, docs), kind),
        pltpu.VMEM((docs, terms), kind),
        pltpu.SMEM((1, slots), jnp.int32),
        pltpu.SMEM((1, slots), jnp.int32),
        pltpu.VMEM((2, 1, slots), jnp.int32),
        pltpu.VMEM((RB, TILE), jnp.int32),
        pltpu.SMEM((RB, TILE), jnp.int32),
        stack,
        stack,
        pltpu.VMEM((RB, 16, TILE), jnp.bfloat16),
        pltpu.VMEM((slots, TILE), jnp.float32),
        held(m),
        held(n),
        held(m, extra),
        held(n),
        held(m),
        pltpu.SemaphoreType.DMA((10,)),
    ] + semaphores(m, m, n, n, m, m, n, n, m, m)


SCALE_REFS = 30


CODES = 32760.0
OCTAVE = 256.0 / math.log(2.0)


def encode(value):
    rows, lanes = value.shape
    groups = value.reshape(rows // 8, 8, lanes)
    top = jnp.maximum(jnp.max(jnp.abs(groups), axis=0), 1e-30)
    level = jnp.ceil(jnp.log(top) * OCTAVE)
    codes = jnp.round(groups * (jnp.exp(level * (-1.0 / OCTAVE)) * CODES))
    whole = jnp.concatenate([codes.reshape(rows, lanes), level, level], axis=0)
    return whole.astype(jnp.int32).astype(jnp.int16)


def decode(block):
    rows, lanes = block.shape[0] - 16, block.shape[1]
    value = block.astype(jnp.int32).astype(jnp.float32)
    scale = jnp.exp(value[rows : rows + 8] * (1.0 / OCTAVE)) * (1.0 / CODES)
    return (value[:rows].reshape(rows // 8, 8, lanes) * scale[None]).reshape(rows, lanes)


def grid_of(n):
    nx = int(math.isqrt(n))
    while n % nx:
        nx -= 1
    return nx, n // nx


def turn_out(vector_ref, block, lanes):
    row = jnp.broadcast_to(vector_ref[pl.ds(block, 1), :], (TILE, TILE))
    column = row.T
    return jnp.concatenate([column] * (lanes // TILE), axis=1)


def precise(a, b, dims):
    return lax.dot_general(
        a, b, (dims, ((), ())), precision=PRECISE, preferred_element_type=jnp.float32
    )


def whitened(value, halves):
    high = value.astype(jnp.bfloat16)
    low = (value - high.astype(jnp.float32)).astype(jnp.bfloat16)
    parts = [(high, 0), (low, 0), (high, 1)]
    total = [jnp.dot(v, halves[k], preferred_element_type=jnp.float32) for v, k in parts]
    return total[0] + (total[1] + total[2])


def pack_gram(gram, extras, packed):
    groups, rows = packed.shape[0], packed.shape[1] - 1
    row = lax.broadcasted_iota(jnp.int32, (TILE, TILE), 0)
    lane = lax.broadcasted_iota(jnp.int32, (TILE, TILE), 1)
    last = gram[TILE:, TILE:]
    packed_rows = [jnp.where(row <= lane, gram[:TILE, :TILE], last), gram[:TILE, TILE:]]
    packed_rows = jnp.concatenate(packed_rows, axis=0)
    diagonal = jnp.sum(jnp.where(row == lane, last, 0.0), axis=0, keepdims=True)
    extras = [diagonal] + extras
    zero = jnp.zeros((1, TILE), jnp.float32)
    for group in range(groups):
        packed[group, :rows, :] = packed_rows[group * rows : (group + 1) * rows]
        packed[group, rows:, :] = extras[group] if group < len(extras) else zero


def unpack_gram(packed, gram):
    rows = packed.shape[1] - 1
    row = lax.broadcasted_iota(jnp.int32, (TILE, TILE), 0)
    lane = lax.broadcasted_iota(jnp.int32, (TILE, TILE), 1)
    half = packed.shape[0] // 2
    both = jnp.concatenate([packed[g, :rows, :] for g in range(half)], axis=0)
    cross = jnp.concatenate([packed[half + g, :rows, :] for g in range(half)], axis=0)
    other = both.T
    gram[:TILE, :TILE] = jnp.where(row <= lane, both, other)
    gram[:TILE, TILE:] = cross
    gram[TILE:, :TILE] = jnp.zeros((TILE, TILE), jnp.float32)
    diagonal = jnp.broadcast_to(packed[0, rows : rows + 1, :], (TILE, TILE))
    last = jnp.where(row > lane, both, jnp.where(row == lane, diagonal, other))
    gram[TILE:, TILE:] = last


def gram_steps(x_ref, o_ref, landing, held, *sems):
    nz, z, c = paired()
    m, my = lax.axis_size("doc"), lax.axis_index("doc")
    steps = [(step, flip) for step in range(m) for flip in range(2) if step or flip]

    def peer(step, flip):
        there = lax.rem(my + step, m)
        core = 1 - c if flip else c
        return 2 * there + core, {"doc": there, "term": 2 * z + core}

    def exchange(source, target, send_sem, recv_sem):
        copies = []
        for step, flip in steps:
            group, place = peer(step, flip)
            slot = 2 * step + flip
            copy = remote(
                source(group), target(slot), send_sem.at[slot], recv_sem.at[slot], place, None
            )
            copy.start()
            copies.append(copy)
        return copies

    mine = 2 * my + c
    copies = exchange(lambda g: x_ref.at[g], lambda k: landing.at[k], *sems[0:2])
    yield
    total = x_ref[mine]
    for (step, flip), copy in zip(steps, copies):
        copy.wait()
        total = total + landing[2 * step + flip]
    held[0] = total
    copies = []
    for step in range(1, nz):
        copy = remote(
            held.at[0], held.at[step], sems[2].at[step], sems[3].at[step], "term", 2 * lax.rem(z + step, nz) + c
        )
        copy.start()
        copies.append(copy)
    yield
    for copy in copies:
        copy.wait()
    total = held[z]
    for source in range(1, nz):
        total = total + held[lax.rem(z - source + nz, nz)]
    o_ref[mine] = total
    copies = exchange(lambda g: o_ref.at[mine], lambda k: o_ref.at[mine], *sems[4:6])
    yield
    for copy in copies:
        copy.wait()


def gram_scratch():
    nz, m = lax.axis_size("term") // 2, lax.axis_size("doc")
    rows = TILE // m + 1
    packed = pltpu.VMEM((2 * m, rows, TILE), jnp.float32)
    return [packed, packed, packed, pltpu.VMEM((nz, rows, TILE), jnp.float32)] + semaphores(
        2 * m, 2 * m, nz, nz, 2 * m, 2 * m
    )


GRAM_REFS = 10


def whole_kernel(
    count,
    rows_hbm,
    cols_hbm,
    tiles_hbm,
    start_hbm,
    row_ref,
    col_ref,
    left_out,
    right_parts,
    halves,
    row_turn,
    col_turn,
    scaled,
    partial,
    send_a,
    recv_a,
    send_b,
    recv_b,
    gathered,
    factor,
    right_sum,
    near_send,
    near_recv,
    far_send,
    far_recv,
    inverse_ref,
    gram,
    work,
    *rest,
):
    left_gram, right_gram = rest[:GRAM_REFS], rest[GRAM_REFS : 2 * GRAM_REFS]
    scale_refs = rest[2 * GRAM_REFS : 2 * GRAM_REFS + SCALE_REFS]
    weight_ref, mean_ref, start_ref, matrix, turned = scale_refs[:5]
    held_e = scale_refs[18]
    sems = rest[2 * GRAM_REFS + SCALE_REFS :]
    n, m = lax.axis_size("term"), lax.axis_size("doc")
    nz, z, c = paired()
    doc = lax.axis_index("doc")
    nx, ny = grid_of(m)
    x, y = lax.rem(doc, nx), doc // nx
    terms, width = left_out.shape
    docs = start_hbm.shape[0]
    share, piece = terms // m, docs // n
    docs_total = docs * m

    def turn_rows():
        def turn(block, carry):
            at = pl.ds(pl.multiple_of(block * TILE, TILE), TILE)
            row_turn[at, :] = turn_out(row_ref, block, TILE)
            return carry

        lax.fori_loop(0, terms // TILE, turn, 0)

    weigh = scale_phase(
        turn_rows,
        count,
        rows_hbm,
        cols_hbm,
        tiles_hbm,
        start_hbm,
        row_ref,
        col_ref,
        *scale_refs,
    )

    halves_of = [(0, 1), (2, 3)]
    part_rows = share // 2

    def axes(flow):
        return (x, nx, y, ny) if flow % 2 == 0 else (y, ny, x, nx)

    def device(flow, first, second):
        return second * nx + first if flow % 2 == 0 else first * nx + second

    def step_of(flow, dx, dy):
        return (dx, dy) if flow % 2 == 0 else (dy, dx)

    def lanes(flow):
        return slice(flow // 2 * TILE, (flow // 2 + 1) * TILE)

    def part(flow):
        return slice(flow % 2 * part_rows, (flow % 2 + 1) * part_rows)

    def prepare(block, carry):
        at = pl.ds(pl.multiple_of(block * TILE, TILE), TILE)
        column = turn_out(col_ref, block, width)
        col_turn[at, :] = column[:, :TILE]
        scaled[at, :] = (column * start_ref[at, :].astype(jnp.float32)).astype(jnp.bfloat16)
        return carry

    lax.fori_loop(0, docs // TILE, prepare, 0, unroll=4)

    steps = [(dx, dy) for dx in range(nx) for dy in range(ny)]
    steps.sort(key=lambda s: -((s[0] > 0) + (s[1] > 0)))
    copies_a, copies_b = {}, {}

    def send_first(half, dx, dy):
        for flow in halves_of[half]:
            a, n1, b, n2 = axes(flow)
            s1, s2 = step_of(flow, dx, dy)
            if s1 == 0:
                continue
            slot = s1 * n2 + s2
            send_a[flow, slot] = encode(partial[dy * nx + dx, part(flow), lanes(flow)])
            copies_a[flow, s1, s2] = remote(
                send_a.at[flow, slot],
                recv_a.at[flow, slot],
                sems[0].at[flow, slot],
                sems[1].at[flow, slot],
                "doc",
                device(flow, lax.rem(a + s1, n1), b),
            )
            copies_a[flow, s1, s2].start()

    for dx, dy in steps:
        target = lax.rem(y + dy, ny) * nx + lax.rem(x + dx, nx)
        at = pl.ds(pl.multiple_of(target * share, share), share)
        product = jnp.dot(matrix[at, :], scaled[...], preferred_element_type=jnp.float32)
        column = row_turn[at, :]
        product = product * jnp.concatenate([column] * (width // TILE), axis=1)
        partial[dy * nx + dx] = product
        send_first(0, dx, dy)
    for dx, dy in steps:
        send_first(1, dx, dy)

    weight_copies = weigh()

    def own(flow, s2):
        dx, dy = step_of(flow, 0, s2)
        return partial[dy * nx + dx, part(flow), lanes(flow)]

    def landed(flow, s2):
        a, n1, b, n2 = axes(flow)
        total = own(flow, s2)
        for s1 in range(1, n1):
            copies_a[flow, s1, s2].wait()
            total = total + decode(recv_a[flow, s1 * n2 + s2])
        return total

    for flow in range(4):
        a, n1, b, n2 = axes(flow)
        for s2 in range(1, n2):
            send_b[flow, s2] = encode(landed(flow, s2))
            copies_b[flow, s2] = remote(
                send_b.at[flow, s2],
                recv_b.at[flow, s2],
                sems[2].at[flow, s2],
                sems[3].at[flow, s2],
                "doc",
                device(flow, a, lax.rem(b + s2, n2)),
            )
            copies_b[flow, s2].start()

    weight_ref[...] = row_ref[...] * finish_exchange(weight_copies, held_e, "doc")
    blocks_of_share = share // TILE
    weight = jnp.concatenate(
        [turn_out(weight_ref, doc * blocks_of_share + k, TILE) for k in range(blocks_of_share)], axis=0
    )
    copies_c, copies_d = {}, {}
    left = []
    for flow in range(4):
        a, n1, b, n2 = axes(flow)
        total = landed(flow, 0)
        for s2 in range(1, n2):
            copies_b[flow, s2].wait()
            total = total + decode(recv_b[flow, s2])
        mean = mean_ref[flow // 2 : flow // 2 + 1, :]
        total = total - weight[part(flow)] * (mean * (1.0 / docs_total))
        left.append(total)
        gathered[flow, doc] = encode(total)
        for s1 in range(1, n1):
            copies_c[flow, s1] = remote(
                gathered.at[flow, doc],
                gathered.at[flow, doc],
                sems[4].at[flow, s1],
                sems[5].at[flow, s1],
                "doc",
                device(flow, lax.rem(a + s1, n1), b),
            )
            copies_c[flow, s1].start()

    left = [jnp.concatenate(left[2 * half : 2 * half + 2], axis=0) for half in range(2)]
    left_share = jnp.concatenate(left, axis=1)
    pack_gram(
        precise(left_share, left_share, ((0,), (0,))) * (1.0 / (terms * n)),
        [jnp.sum(weight * half, axis=0, keepdims=True) for half in left],
        left_gram[0],
    )
    left_steps = gram_steps(*left_gram)
    next(left_steps)

    def unpack(flow, block):
        at = pl.ds(pl.multiple_of(block * share + part(flow).start, part_rows), part_rows)
        value = decode(gathered[flow, block]) * row_turn[at, :]
        factor[at, lanes(flow)] = value.astype(jnp.bfloat16)

    def multiply(block, first_flow, flows, fresh):
        at = pl.ds(pl.multiple_of(block * share, share), share)
        cols = slice(first_flow * TILE, (first_flow + flows) * TILE)
        tall = docs // 2

        def rows_of(k, carry):
            rows = pl.ds(pl.multiple_of(k * tall, tall), tall)
            product = jnp.dot(
                turned[rows, at], factor[at, cols], preferred_element_type=jnp.float32
            )
            right_sum[rows, cols] = product if fresh else right_sum[rows, cols] + product
            return carry

        lax.fori_loop(0, 2, rows_of, 0)

    def source_of(flow, s1, s2):
        a, n1, b, n2 = axes(flow)
        return device(flow, lax.rem(a - s1 + n1, n1), lax.rem(b - s2 + n2, n2))

    for flow in range(4):
        unpack(flow, doc)
    multiply(doc, 0, 2, True)

    def landed_from(dx, dy, half):
        block = source_of(0, dx, dy)
        for flow in halves_of[half]:
            s1, s2 = step_of(flow, dx, dy)
            if s2:
                copies_d[flow, s1, s2].wait()
            unpack(flow, block)
        return block

    for flow in range(4):
        a, n1, b, n2 = axes(flow)
        for s1 in range(n1):
            if s1:
                copies_c[flow, s1].wait()
            source = source_of(flow, s1, 0)
            for s2 in range(1, n2):
                copies_d[flow, s1, s2] = remote(
                    gathered.at[flow, source],
                    gathered.at[flow, source],
                    sems[6].at[flow, s1 * n2 + s2],
                    sems[7].at[flow, s1 * n2 + s2],
                    "doc",
                    device(flow, a, lax.rem(b + s2, n2)),
                )
                copies_d[flow, s1, s2].start()
    next(left_steps)
    others = [step for step in reversed(steps) if step != (0, 0)]

    wide = 2 * piece
    sibling = 2 * z + 1 - c
    chunks = [lax.rem(z // 2 + 1 + j, nz // 2) for j in range(nz // 2)]

    def far_copy(half, step):
        there = lax.rem(z + step, nz)
        return remote(
            far_send.at[half, step],
            far_recv.at[half, step],
            sems[10].at[half, step],
            sems[11].at[half, step],
            "term",
            2 * there + c,
        )

    for half in range(2):
        for dx, dy in others:
            block = landed_from(dx, dy, half)
            if (dx, dy) != others[-1]:
                multiply(block, half, 1, False)
        cols = slice(half * TILE, (half + 1) * TILE)
        last_terms = pl.ds(pl.multiple_of(block * share, share), share)

        def right_product(chunk, core):
            at = pl.ds(pl.multiple_of(core * (docs // 2) + chunk * wide, wide), wide)
            product = jnp.dot(
                turned[at, last_terms], factor[last_terms, cols], preferred_element_type=jnp.float32
            )
            return (right_sum[at, cols] + product) * col_turn[at, :]

        near_copies = []
        for j, chunk in enumerate(chunks):
            near_send[half, j] = right_product(chunk, 1 - c)
            copy = remote(
                near_send.at[half, j],
                near_recv.at[half, j],
                sems[8].at[half, j],
                sems[9].at[half, j],
                "term",
                sibling,
            )
            copy.start()
            near_copies.append(copy)
        if half == 0:
            next(left_steps)
        for j, chunk in enumerate(chunks):
            product = right_product(chunk, c)
            near_copies[j].wait()
            near_recv[half, j] = near_recv[half, j] + product
            last = j + 1 == len(chunks)
            for k in range(2):
                if last and k:
                    continue
                inner = 1 - lax.rem(z, 2) if last else k
                step = lax.rem(2 * chunk + inner - z + nz, nz)
                at = pl.ds(pl.multiple_of(inner * piece, piece), piece)
                far_send[half, step] = encode(near_recv[half, j, at, :])
                far_copy(half, step).start()
    for _ in left_steps:
        pass
    unpack_gram(left_gram[1], gram)
    inverse_kernel(gram, inverse_ref, work)

    def split_inverse():
        whiten = inverse_ref[...].T
        high = whiten.astype(jnp.bfloat16)
        halves[0] = high
        halves[1] = (whiten - high.astype(jnp.float32)).astype(jnp.bfloat16)

    def finish_left(block):
        at = pl.ds(pl.multiple_of(block * share, share), share)
        value = jnp.concatenate(
            [
                jnp.concatenate([decode(gathered[flow, block]) for flow in flows], axis=0)
                for flows in halves_of
            ],
            axis=1,
        )
        left_out[at, :] = whitened(value, halves).astype(jnp.bfloat16)

    extra = left_gram[1].shape[1] - 1
    weighted = jnp.concatenate(
        [left_gram[1][1 + k, extra:, :] for k in range(width // TILE)], axis=1
    )
    lean = precise(jnp.broadcast_to(weighted, (8, width)), inverse_ref[...], ((1,), (1,)))[0:1]
    split_inverse()
    own_rows = pl.ds(pl.multiple_of(lax.rem(z, 2) * piece, piece), piece)
    totals = []
    for half in range(2):
        total = near_recv[half, len(chunks) - 1, own_rows, :]
        for step in range(1, nz):
            far_copy(half, step).wait()
            total = total + decode(far_recv[half, step])
        totals.append(total)
    total = jnp.concatenate(totals, axis=1)
    block = whitened(total, halves) - lean * (1.0 / docs_total)

    me = c * nz + z
    pack_gram(
        precise(block, block, ((0,), (0,))) * (1.0 / docs_total), [], right_gram[0]
    )
    right_steps = gram_steps(*right_gram)
    next(right_steps)
    right_parts[me] = encode(block)
    far_copies = []

    def send_part(step):
        copy = remote(
            right_parts.at[me],
            right_parts.at[me],
            sems[12].at[step],
            sems[13].at[step],
            "term",
            2 * lax.rem(z + step, nz) + c,
        )
        copy.start()
        far_copies.append(copy)

    send_part(1)
    copy = remote(
        right_parts.at[me], right_parts.at[me], sems[14].at[0], sems[15].at[0], "term", sibling
    )
    copy.start()
    near_copies = [copy]
    for k in range(m // 4):
        finish_left(k)
    next(right_steps)
    for k in range(m // 4, 3 * m // 4):
        finish_left(k)
    next(right_steps)
    for step in range(2, nz):
        send_part(step)
    for k in range(3 * m // 4, m):
        finish_left(k)
    for _ in right_steps:
        pass
    unpack_gram(right_gram[1], gram)
    def pass_on(left):
        if left:
            return
        for step in range(1, nz):
            far_copies[step - 1].wait()
            t = c * nz + lax.rem(z - step + nz, nz)
            copy = remote(
                right_parts.at[t],
                right_parts.at[t],
                sems[14].at[step],
                sems[15].at[step],
                "term",
                sibling,
            )
            copy.start()
            near_copies.append(copy)

    inverse_kernel(gram, inverse_ref, work, pass_on)
    split_inverse()

    for copy in near_copies:
        copy.wait()


def emit_kernel(row_ref, col_ref, left_ref, parts_ref, halves, *rest):
    outs, right, sems = rest[:4], rest[4], rest[5]
    right_out = outs[3]
    copies = [
        pltpu.make_async_copy(source, target, sems.at[k])
        for k, (source, target) in enumerate(zip((left_ref, row_ref, col_ref), (outs[2], *outs[:2])))
    ]
    for copy in copies:
        copy.start()
    shares, piece = parts_ref.shape[0], right.shape[0] // parts_ref.shape[0]

    def copy_of(t):
        at = pl.ds(pl.multiple_of(t * piece, piece), piece)
        return pltpu.make_async_copy(right.at[at], right_out.at[at], sems.at[3 + t])

    for t in range(shares):
        right[t * piece : (t + 1) * piece, :] = whitened(decode(parts_ref[t]), halves).astype(
            jnp.bfloat16
        )
        copy_of(t).start()
        copies.append(copy_of(t))
    for copy in copies:
        copy.wait()


def emit(row, col, left, parts, halves, docs):
    width = left.shape[1]
    hbm = pl.BlockSpec(memory_space=pl.ANY)
    right = jax.ShapeDtypeStruct((docs, width), left.dtype)
    return pl.pallas_call(
        emit_kernel,
        out_shape=[jax.ShapeDtypeStruct(x.shape, x.dtype) for x in (row, col, left)] + [right],
        in_specs=[VMEM] * 5,
        out_specs=[hbm] * 4,
        scratch_shapes=[
            pltpu.VMEM(right.shape, right.dtype),
            pltpu.SemaphoreType.DMA((3 + parts.shape[0],)),
        ],
        compiler_params=pltpu.CompilerParams(vmem_limit_bytes=6 << 20),
        name="emit",
    )(row, col, left, parts, halves)


def per_device(tile_values, tile_rows, tile_cols, tile_count, start_block):
    n, m = lax.axis_size("term"), lax.axis_size("doc")
    nz = n // 2
    terms, (docs, width) = RB * TILE, start_block.shape
    share, piece = terms // m, docs // n
    wide = max(grid_of(m))
    int16, f32, bf16 = jnp.int16, jnp.float32, jnp.bfloat16
    coded = pltpu.VMEM((4, m, share // 2 + 16, TILE), int16)
    coded_b = pltpu.VMEM((4, wide, share // 2 + 16, TILE), int16)
    far = pltpu.VMEM((2, nz, piece + 16, TILE), int16)
    near = pltpu.VMEM((2, nz // 2, 2 * piece, TILE), f32)
    pairs = [pltpu.SemaphoreType.DMA((4, size)) for size in (m, m, wide, wide, wide, wide, m, m)]
    pairs += [pltpu.SemaphoreType.DMA((2, nz))] * 4
    vector = jax.ShapeDtypeStruct((RB, TILE), f32)
    hbm = pl.BlockSpec(memory_space=pltpu.HBM)
    outs = pl.pallas_call(
        whole_kernel,
        out_shape=[
            vector,
            vector,
            jax.ShapeDtypeStruct((terms, width), bf16),
            jax.ShapeDtypeStruct((n, piece + 16, width), int16),
            jax.ShapeDtypeStruct((2, width, width), bf16),
        ],
        in_specs=[SMEM] + [hbm] * 4,
        out_specs=[VMEM] * 5,
        scratch_shapes=[
            pltpu.VMEM((terms, TILE), f32),
            pltpu.VMEM((docs, TILE), f32),
            pltpu.VMEM((docs, width), bf16),
            pltpu.VMEM((m, share, width), f32),
            coded,
            coded,
            coded_b,
            coded_b,
            coded,
            pltpu.VMEM((terms, width), bf16),
            pltpu.VMEM((docs, width), f32),
            near,
            near,
            far,
            far,
            pltpu.VMEM((width, width), f32),
            pltpu.VMEM((width, width), f32),
            pltpu.VMEM((width, 2 * width), f32),
        ]
        + gram_scratch()
        + gram_scratch()
        + scale_scratch(terms, docs, width, tile_values.shape[0], tile_values.dtype)
        + pairs
        + semaphores(*[nz] * 4),
        compiler_params=pltpu.CompilerParams(
            collective_id=0, has_side_effects=True, vmem_limit_bytes=44 << 20
        ),
        name="whole",
    )(
        tile_count,
        *(
            pltpu.with_memory_space_constraint(x, pltpu.HBM)
            for x in (tile_rows, tile_cols, tile_values, start_block)
        ),
    )
    row, col, left_basis, right_basis = emit(*outs, docs)
    return (row.reshape(-1), col.reshape(-1), left_basis, right_basis)


def solution(mesh):
    placed = (
        P("term", "doc", None),
        P("term", "doc"),
        P("term", "doc"),
        P("term", "doc"),
        P("doc", None),
    )
    return jax.shard_map(
        per_device,
        mesh=mesh,
        in_specs=placed,
        out_specs=(P("term"), P("doc"), P("term", None), P("doc", None)),
        check_vma=False,
    )
```

```python
import math

import jax
import jax.numpy as jnp
from jax import lax
from jax.experimental import pallas as pl
from jax.experimental.pallas import tpu as pltpu
from jax.sharding import PartitionSpec as P

TILE = 128
RB = 16
CB = 16


PRECISE = lax.Precision.HIGHEST
MESH = pl.DeviceIdType.MESH
VMEM = pl.BlockSpec(memory_space=pltpu.VMEM)
SMEM = pl.BlockSpec(memory_space=pltpu.SMEM)


BLOCK = 64
GROUP = 16


def block_inverse(block, low, high):
    finished = []
    lanes = lax.broadcasted_iota(jnp.int32, (GROUP, block.shape[1]), 1)
    inside = (lanes >= high) & (lanes < high + BLOCK)
    for base in range(0, BLOCK, GROUP):
        rows = lax.broadcasted_iota(jnp.int32, block.shape, 0)
        pivots = jnp.ones((GROUP, block.shape[1]), block.dtype)
        factors = []
        for at in range(GROUP):
            lane = low + base + at
            column = jnp.broadcast_to(block[:, lane : lane + 1], block.shape)
            for past, factor in enumerate(factors):
                column = column - factor * column[past : past + 1, :]
            pivots = jnp.where(rows[:GROUP] == at, column[:GROUP], pivots)
            ratio = column * (1.0 / column[at : at + 1, :])
            factors.append(jnp.where(rows > at, ratio, 0.0))
        for at, factor in enumerate(factors):
            block = block - factor * block[at : at + 1, :]
        finished.append(jnp.where(inside, block[:GROUP] * lax.rsqrt(pivots), 0.0))
        block = block[GROUP:]
    return jnp.concatenate(finished, axis=0)


def inverse_kernel(gram_ref, o_ref, work, meanwhile=None):
    width = gram_ref.shape[0]
    work[:, :width] = gram_ref[...]
    rows = lax.broadcasted_iota(jnp.int32, (width, width), 0)
    lanes = lax.broadcasted_iota(jnp.int32, (width, width), 1)
    work[:, width:] = jnp.where(rows == lanes, 1.0, 0.0)
    rows = lax.broadcasted_iota(jnp.int32, (BLOCK, TILE), 0)
    lanes = lax.broadcasted_iota(jnp.int32, (BLOCK, TILE), 1)
    block = gram_ref[:BLOCK, :TILE]
    for index in range(width // BLOCK):
        start = index * BLOCK
        after = start + BLOCK
        near = start // TILE * TILE
        low = start - near
        high = TILE - BLOCK - low
        if meanwhile is not None:
            meanwhile(width // BLOCK - 1 - index)
        inside = (lanes >= low) & (lanes < low + BLOCK)
        block = jnp.where(inside, block, jnp.where(lanes - high == rows, 1.0, 0.0))
        inverse = block_inverse(block, low, high)
        inverse = inverse[:, high : high + BLOCK]
        if after < width:
            near = after // TILE * TILE
            low = after - near
            window = precise(inverse, work[start:after, near : near + TILE], ((1,), (0,)))
            block = work[after : after + BLOCK, near : near + TILE] - precise(
                window[:, low : low + BLOCK], window, ((0,), (0,))
            )
        solved = precise(inverse, work[start:after, :], ((1,), (0,)))
        o_ref[start:after, :] = solved[:, width:]
        if after < width:
            update = precise(solved[:, after:width], solved, ((0,), (0,)))
            work[after:, :] = work[after:, :] - update


def announce():
    barrier = pltpu.get_barrier_semaphore()
    n, m = lax.axis_size("term"), lax.axis_size("doc")
    me, doc = lax.axis_index("term"), lax.axis_index("doc")
    peers = [{"term": lax.rem(me + step, n)} for step in range(1, n)]
    for step in range(1, m):
        there = lax.rem(doc + step, m)
        peers += [{"doc": there}, {"doc": there, "term": me + 1 - 2 * lax.rem(me, 2)}]
    for peer in peers:
        pl.semaphore_signal(barrier, inc=1, device_id=peer, device_id_type=MESH)
    return len(peers)


def remote(source, target, send_sem, recv_sem, axis, peer):
    return pltpu.make_async_remote_copy(
        src_ref=source,
        dst_ref=target,
        send_sem=send_sem,
        recv_sem=recv_sem,
        device_id=axis if peer is None else {axis: peer},
        device_id_type=MESH,
    )


def paired():
    n, me = lax.axis_size("term"), lax.axis_index("term")
    return n // 2, me // 2, lax.rem(me, 2)


def semaphores(*sizes):
    return [pltpu.SemaphoreType.DMA((size,)) for size in sizes]


def split3(value):
    high = value.astype(jnp.bfloat16)
    rest = value - high.astype(jnp.float32)
    middle = rest.astype(jnp.bfloat16)
    return high, middle, (rest - middle.astype(jnp.float32)).astype(jnp.bfloat16)


def spread(value, parts):
    high, middle, low = (part.astype(jnp.float32) for part in split3(value))
    blocks, depth, lanes = parts.shape
    rows = lax.broadcasted_iota(jnp.int32, (depth, lanes), 0)
    for block in range(blocks):
        at = slice(block, block + 1)
        picked = jnp.where(rows == 0, high[at], jnp.where(rows == 1, middle[at], low[at]))
        parts[block] = jnp.where(rows < 3, picked, 0.0).astype(jnp.bfloat16)


def tile_sums(tiles, source_ids, parts, sums, target, forward):
    slots = sums.shape[0]
    for slot in range(slots):
        product = lax.dot_general(
            parts[source_ids[0, slot]],
            tiles[slot],
            (((1,), (1 if forward else 0,)), ((), ())),
            preferred_element_type=jnp.float32,
        )
        sums[slot : slot + 1, :] = product[0:1] + product[1:2] + product[2:3]
    stacked = jnp.concatenate(split3(sums[...]), axis=0)
    return jnp.dot(target, stacked, preferred_element_type=jnp.float32)


def start_exchange(held, axis, send_sem, recv_sem):
    n, me = lax.axis_size(axis), lax.axis_index(axis)

    def copy_of(step):
        return remote(
            held.at[0], held.at[step], send_sem.at[step], recv_sem.at[step], axis, lax.rem(me + step, n)
        )

    steps = list(range(1, n))
    if axis == "term":
        nz, z, c = paired()
        places = []
        for k in range(nz - 1):
            down, up = nz - 1 - k, k
            down = jnp.where(down <= z, down - 1, down)
            up = jnp.where(up >= z, up + 1, up)
            there = jnp.where(2 * z < nz, down, up)
            places += [2 * there + c, 2 * there + 1 - c]
        places.append(2 * z + 1 - c)
        steps = [lax.rem(place - me + n, n) for place in places]
    for step in steps:
        copy_of(step).start()
    return [copy_of(step) for step in range(1, n)]


def finish_exchange(copies, held, axis):
    n, me = lax.axis_size(axis), lax.axis_index(axis)
    for copy in copies:
        copy.wait()
    total = held[me]
    for source in range(1, n):
        total = total + held[lax.rem(me - source + n, n)]
    return total


def scale_phase(
    meanwhile,
    count,
    rows_hbm,
    cols_hbm,
    tiles_hbm,
    start_hbm,
    row_ref,
    col_ref,
    weight_ref,
    mean_ref,
    start_ref,
    dense_ref,
    turned_ref,
    row_ids,
    col_ids,
    lanes,
    places,
    lookup,
    tiles,
    flipped,
    parts,
    sums,
    held_a,
    held_b,
    held_c,
    held_d,
    held_e,
    load_sem,
    *sems,
):
    expected = announce()
    slots = tiles_hbm.shape[0]
    sources = [rows_hbm, cols_hbm, rows_hbm, cols_hbm]
    targets = [row_ids, col_ids, lanes.at[0], lanes.at[1]]
    quarter = -(-slots // 4)
    for at in range(0, slots, quarter):
        stretch = pl.ds(at, min(quarter, slots - at))
        sources.append(tiles_hbm.at[stretch])
        targets.append(tiles.at[stretch])
    sources.append(start_hbm)
    targets.append(start_ref)
    loads = [
        pltpu.make_async_copy(source, target, load_sem.at[k])
        for k, (source, target) in enumerate(zip(sources, targets))
    ]
    for load in loads:
        load.start()
    tiles[slots] = jnp.zeros(tiles.shape[1:], tiles.dtype)
    flipped[slots] = jnp.zeros(tiles.shape[1:], tiles.dtype)
    blocks = row_ref.shape[0]
    spread(jnp.ones(row_ref.shape, jnp.float32), parts)
    for load in loads[:4]:
        load.wait()
    used = count[0, 0]
    place = lax.broadcasted_iota(jnp.int32, (blocks, slots), 0)
    live = lax.broadcasted_iota(jnp.int32, (blocks, slots), 1) < used
    to_rows, to_cols = (
        jnp.concatenate([jnp.where(live & (place == lanes[k]), 1.0, 0.0)] * 3, axis=1).astype(jnp.bfloat16)
        for k in range(2)
    )
    def build(out_ref, source, turn):
        def place_row(outer, carry):
            at = pl.multiple_of(outer * TILE, TILE)
            for inner in range(blocks):
                slot = lookup[inner, outer] if turn else lookup[outer, inner]
                tile = source[slot]
                out_ref[pl.ds(at, TILE), inner * TILE : (inner + 1) * TILE] = tile
            return carry

        lax.fori_loop(0, blocks, place_row, 0)

    def flip(slot, carry):
        flipped[slot] = tiles[slot].T
        return carry

    for load in loads[4:-1]:
        load.wait()
    held_a[0] = tile_sums(tiles, col_ids, parts, sums, to_rows, True)
    pl.semaphore_wait(pltpu.get_barrier_semaphore(), expected)
    copies = start_exchange(held_a, "doc", *sems[0:2])
    row = lax.broadcasted_iota(jnp.int32, places.shape, 0)
    col = lax.broadcasted_iota(jnp.int32, places.shape, 1)
    table = jnp.full(places.shape, slots, jnp.int32)
    for slot in range(slots):
        found = (row == row_ids[0, slot]) & (col == jnp.where(slot < used, col_ids[0, slot], -1))
        table = jnp.where(found, slot, table)
    places[...] = table
    keep = pltpu.make_async_copy(places, lookup, load_sem.at[9])
    keep.start()
    loads[-1].wait()
    mean = jnp.sum(start_ref[...].astype(jnp.float32), axis=0, keepdims=True)
    extra = held_c.shape[1] - blocks
    pieces = [mean[:, at : at + TILE] for at in range(0, mean.shape[1], TILE)]
    pieces.append(jnp.zeros((extra - len(pieces), TILE), jnp.float32))
    held_c[0, blocks:, :] = jnp.concatenate(pieces, axis=0)
    keep.wait()
    total = finish_exchange(copies, held_a, "doc")
    spread(1.0 / total, parts)

    held_b[0] = tile_sums(tiles, row_ids, parts, sums, to_cols, False)
    copies = start_exchange(held_b, "term", *sems[2:4])
    lax.fori_loop(0, slots, flip, 0)
    total = finish_exchange(copies, held_b, "term")
    spread(1.0 / total, parts)

    held_c[0, :blocks, :] = tile_sums(flipped, col_ids, parts, sums, to_rows, False)
    copies = start_exchange(held_c, "doc", *sems[4:6])
    build(dense_ref, tiles, False)
    joined = finish_exchange(copies, held_c, "doc")
    mean_ref[...] = joined[blocks:, :]
    row_scale = 1.0 / joined[:blocks]
    row_ref[...] = row_scale
    spread(row_scale, parts)

    held_d[0] = tile_sums(tiles, row_ids, parts, sums, to_cols, False)
    copies = start_exchange(held_d, "term", *sems[6:8])
    meanwhile()
    col_ref[...] = 1.0 / finish_exchange(copies, held_d, "term")

    def weigh():
        spread(col_ref[...], parts)
        held_e[0] = tile_sums(flipped, col_ids, parts, sums, to_rows, False)
        copies = start_exchange(held_e, "doc", *sems[8:10])
        build(turned_ref, flipped, True)
        return copies

    return weigh


def scale_scratch(terms, docs, width, slots, kind):
    m, n = lax.axis_size("doc"), lax.axis_size("term")
    vector = pltpu.VMEM((RB, TILE), jnp.float32)
    extra = -(-width // (8 * TILE)) * 8
    stack = pltpu.VMEM((slots + 1, TILE, TILE), kind)

    def held(count, more=0):
        return pltpu.VMEM((count, RB + more, TILE), jnp.float32)

    return [
        vector,
        pltpu.VMEM((extra, TILE), jnp.float32),
        pltpu.VMEM((docs, width), kind),
        pltpu.VMEM((terms, docs), kind),
        pltpu.VMEM((docs, terms), kind),
        pltpu.SMEM((1, slots), jnp.int32),
        pltpu.SMEM((1, slots), jnp.int32),
        pltpu.VMEM((2, 1, slots), jnp.int32),
        pltpu.VMEM((RB, TILE), jnp.int32),
        pltpu.SMEM((RB, TILE), jnp.int32),
        stack,
        stack,
        pltpu.VMEM((RB, 16, TILE), jnp.bfloat16),
        pltpu.VMEM((slots, TILE), jnp.float32),
        held(m),
        held(n),
        held(m, extra),
        held(n),
        held(m),
        pltpu.SemaphoreType.DMA((10,)),
    ] + semaphores(m, m, n, n, m, m, n, n, m, m)


SCALE_REFS = 30


CODES = 32760.0
OCTAVE = 256.0 / math.log(2.0)


def encode(value):
    rows, lanes = value.shape
    groups = value.reshape(rows // 8, 8, lanes)
    top = jnp.maximum(jnp.max(jnp.abs(groups), axis=0), 1e-30)
    level = jnp.ceil(jnp.log(top) * OCTAVE)
    codes = jnp.round(groups * (jnp.exp(level * (-1.0 / OCTAVE)) * CODES))
    whole = jnp.concatenate([codes.reshape(rows, lanes), level, level], axis=0)
    return whole.astype(jnp.int32).astype(jnp.int16)


def decode(block):
    rows, lanes = block.shape[0] - 16, block.shape[1]
    value = block.astype(jnp.int32).astype(jnp.float32)
    scale = jnp.exp(value[rows : rows + 8] * (1.0 / OCTAVE)) * (1.0 / CODES)
    return (value[:rows].reshape(rows // 8, 8, lanes) * scale[None]).reshape(rows, lanes)


def grid_of(n):
    nx = int(math.isqrt(n))
    while n % nx:
        nx -= 1
    return nx, n // nx


def turn_out(vector_ref, block, lanes):
    row = jnp.broadcast_to(vector_ref[pl.ds(block, 1), :], (TILE, TILE))
    column = row.T
    return jnp.concatenate([column] * (lanes // TILE), axis=1)


def precise(a, b, dims):
    return lax.dot_general(
        a, b, (dims, ((), ())), precision=PRECISE, preferred_element_type=jnp.float32
    )


def whitened(value, halves):
    high = value.astype(jnp.bfloat16)
    low = (value - high.astype(jnp.float32)).astype(jnp.bfloat16)
    parts = [(high, 0), (low, 0), (high, 1)]
    total = [jnp.dot(v, halves[k], preferred_element_type=jnp.float32) for v, k in parts]
    return total[0] + (total[1] + total[2])


def pack_gram(gram, extras, packed):
    groups, rows = packed.shape[0], packed.shape[1] - 1
    row = lax.broadcasted_iota(jnp.int32, (TILE, TILE), 0)
    lane = lax.broadcasted_iota(jnp.int32, (TILE, TILE), 1)
    last = gram[TILE:, TILE:]
    packed_rows = [jnp.where(row <= lane, gram[:TILE, :TILE], last), gram[:TILE, TILE:]]
    packed_rows = jnp.concatenate(packed_rows, axis=0)
    diagonal = jnp.sum(jnp.where(row == lane, last, 0.0), axis=0, keepdims=True)
    extras = [diagonal] + extras
    zero = jnp.zeros((1, TILE), jnp.float32)
    for group in range(groups):
        packed[group, :rows, :] = packed_rows[group * rows : (group + 1) * rows]
        packed[group, rows:, :] = extras[group] if group < len(extras) else zero


def unpack_gram(packed, gram):
    rows = packed.shape[1] - 1
    row = lax.broadcasted_iota(jnp.int32, (TILE, TILE), 0)
    lane = lax.broadcasted_iota(jnp.int32, (TILE, TILE), 1)
    half = packed.shape[0] // 2
    both = jnp.concatenate([packed[g, :rows, :] for g in range(half)], axis=0)
    cross = jnp.concatenate([packed[half + g, :rows, :] for g in range(half)], axis=0)
    other = both.T
    gram[:TILE, :TILE] = jnp.where(row <= lane, both, other)
    gram[:TILE, TILE:] = cross
    gram[TILE:, :TILE] = jnp.zeros((TILE, TILE), jnp.float32)
    diagonal = jnp.broadcast_to(packed[0, rows : rows + 1, :], (TILE, TILE))
    last = jnp.where(row > lane, both, jnp.where(row == lane, diagonal, other))
    gram[TILE:, TILE:] = last


def gram_steps(x_ref, o_ref, landing, held, *sems):
    nz, z, c = paired()
    m, my = lax.axis_size("doc"), lax.axis_index("doc")
    steps = [(step, flip) for step in range(m) for flip in range(2) if step or flip]

    def peer(step, flip):
        there = lax.rem(my + step, m)
        core = 1 - c if flip else c
        return 2 * there + core, {"doc": there, "term": 2 * z + core}

    def exchange(source, target, send_sem, recv_sem):
        copies = []
        for step, flip in steps:
            group, place = peer(step, flip)
            slot = 2 * step + flip
            copy = remote(
                source(group), target(slot), send_sem.at[slot], recv_sem.at[slot], place, None
            )
            copy.start()
            copies.append(copy)
        return copies

    mine = 2 * my + c
    copies = exchange(lambda g: x_ref.at[g], lambda k: landing.at[k], *sems[0:2])
    yield
    total = x_ref[mine]
    for (step, flip), copy in zip(steps, copies):
        copy.wait()
        total = total + landing[2 * step + flip]
    held[0] = total
    copies = []
    for step in range(1, nz):
        copy = remote(
            held.at[0], held.at[step], sems[2].at[step], sems[3].at[step], "term", 2 * lax.rem(z + step, nz) + c
        )
        copy.start()
        copies.append(copy)
    yield
    for copy in copies:
        copy.wait()
    total = held[z]
    for source in range(1, nz):
        total = total + held[lax.rem(z - source + nz, nz)]
    o_ref[mine] = total
    copies = exchange(lambda g: o_ref.at[mine], lambda k: o_ref.at[mine], *sems[4:6])
    yield
    for copy in copies:
        copy.wait()


def gram_scratch():
    nz, m = lax.axis_size("term") // 2, lax.axis_size("doc")
    rows = TILE // m + 1
    packed = pltpu.VMEM((2 * m, rows, TILE), jnp.float32)
    return [packed, packed, packed, pltpu.VMEM((nz, rows, TILE), jnp.float32)] + semaphores(
        2 * m, 2 * m, nz, nz, 2 * m, 2 * m
    )


GRAM_REFS = 10


def whole_kernel(
    count,
    rows_hbm,
    cols_hbm,
    tiles_hbm,
    start_hbm,
    row_ref,
    col_ref,
    left_out,
    right_parts,
    halves,
    row_turn,
    col_turn,
    scaled,
    partial,
    send_a,
    recv_a,
    send_b,
    recv_b,
    gathered,
    factor,
    right_sum,
    near_send,
    near_recv,
    far_send,
    far_recv,
    inverse_ref,
    gram,
    work,
    *rest,
):
    left_gram, right_gram = rest[:GRAM_REFS], rest[GRAM_REFS : 2 * GRAM_REFS]
    scale_refs = rest[2 * GRAM_REFS : 2 * GRAM_REFS + SCALE_REFS]
    weight_ref, mean_ref, start_ref, matrix, turned = scale_refs[:5]
    held_e = scale_refs[18]
    sems = rest[2 * GRAM_REFS + SCALE_REFS :]
    n, m = lax.axis_size("term"), lax.axis_size("doc")
    nz, z, c = paired()
    doc = lax.axis_index("doc")
    nx, ny = grid_of(m)
    x, y = lax.rem(doc, nx), doc // nx
    terms, width = left_out.shape
    docs = start_hbm.shape[0]
    share, piece = terms // m, docs // n
    docs_total = docs * m

    def turn_rows():
        def turn(block, carry):
            at = pl.ds(pl.multiple_of(block * TILE, TILE), TILE)
            row_turn[at, :] = turn_out(row_ref, block, TILE)
            return carry

        lax.fori_loop(0, terms // TILE, turn, 0)

    weigh = scale_phase(
        turn_rows,
        count,
        rows_hbm,
        cols_hbm,
        tiles_hbm,
        start_hbm,
        row_ref,
        col_ref,
        *scale_refs,
    )

    halves_of = [(0, 1), (2, 3)]
    part_rows = share // 2

    def axes(flow):
        return (x, nx, y, ny) if flow % 2 == 0 else (y, ny, x, nx)

    def device(flow, first, second):
        return second * nx + first if flow % 2 == 0 else first * nx + second

    def step_of(flow, dx, dy):
        return (dx, dy) if flow % 2 == 0 else (dy, dx)

    def lanes(flow):
        return slice(flow // 2 * TILE, (flow // 2 + 1) * TILE)

    def part(flow):
        return slice(flow % 2 * part_rows, (flow % 2 + 1) * part_rows)

    def prepare(block, carry):
        at = pl.ds(pl.multiple_of(block * TILE, TILE), TILE)
        column = turn_out(col_ref, block, width)
        col_turn[at, :] = column[:, :TILE]
        scaled[at, :] = (column * start_ref[at, :].astype(jnp.float32)).astype(jnp.bfloat16)
        return carry

    lax.fori_loop(0, docs // TILE, prepare, 0, unroll=4)

    steps = [(dx, dy) for dx in range(nx) for dy in range(ny)]
    steps.sort(key=lambda s: -((s[0] > 0) + (s[1] > 0)))
    copies_a, copies_b = {}, {}

    def send_first(half, dx, dy):
        for flow in halves_of[half]:
            a, n1, b, n2 = axes(flow)
            s1, s2 = step_of(flow, dx, dy)
            if s1 == 0:
                continue
            slot = s1 * n2 + s2
            send_a[flow, slot] = encode(partial[dy * nx + dx, part(flow), lanes(flow)])
            copies_a[flow, s1, s2] = remote(
                send_a.at[flow, slot],
                recv_a.at[flow, slot],
                sems[0].at[flow, slot],
                sems[1].at[flow, slot],
                "doc",
                device(flow, lax.rem(a + s1, n1), b),
            )
            copies_a[flow, s1, s2].start()

    for dx, dy in steps:
        target = lax.rem(y + dy, ny) * nx + lax.rem(x + dx, nx)
        at = pl.ds(pl.multiple_of(target * share, share), share)
        product = jnp.dot(matrix[at, :], scaled[...], preferred_element_type=jnp.float32)
        column = row_turn[at, :]
        product = product * jnp.concatenate([column] * (width // TILE), axis=1)
        partial[dy * nx + dx] = product
        send_first(0, dx, dy)
    for dx, dy in steps:
        send_first(1, dx, dy)

    weight_copies = weigh()

    def own(flow, s2):
        dx, dy = step_of(flow, 0, s2)
        return partial[dy * nx + dx, part(flow), lanes(flow)]

    def landed(flow, s2):
        a, n1, b, n2 = axes(flow)
        total = own(flow, s2)
        for s1 in range(1, n1):
            copies_a[flow, s1, s2].wait()
            total = total + decode(recv_a[flow, s1 * n2 + s2])
        return total

    for flow in range(4):
        a, n1, b, n2 = axes(flow)
        for s2 in range(1, n2):
            send_b[flow, s2] = encode(landed(flow, s2))
            copies_b[flow, s2] = remote(
                send_b.at[flow, s2],
                recv_b.at[flow, s2],
                sems[2].at[flow, s2],
                sems[3].at[flow, s2],
                "doc",
                device(flow, a, lax.rem(b + s2, n2)),
            )
            copies_b[flow, s2].start()

    weight_ref[...] = row_ref[...] * finish_exchange(weight_copies, held_e, "doc")
    blocks_of_share = share // TILE
    weight = jnp.concatenate(
        [turn_out(weight_ref, doc * blocks_of_share + k, TILE) for k in range(blocks_of_share)], axis=0
    )
    copies_c, copies_d = {}, {}
    left = []
    for flow in range(4):
        a, n1, b, n2 = axes(flow)
        total = landed(flow, 0)
        for s2 in range(1, n2):
            copies_b[flow, s2].wait()
            total = total + decode(recv_b[flow, s2])
        mean = mean_ref[flow // 2 : flow // 2 + 1, :]
        total = total - weight[part(flow)] * (mean * (1.0 / docs_total))
        left.append(total)
        gathered[flow, doc] = encode(total)
        for s1 in range(1, n1):
            copies_c[flow, s1] = remote(
                gathered.at[flow, doc],
                gathered.at[flow, doc],
                sems[4].at[flow, s1],
                sems[5].at[flow, s1],
                "doc",
                device(flow, lax.rem(a + s1, n1), b),
            )
            copies_c[flow, s1].start()

    left = [jnp.concatenate(left[2 * half : 2 * half + 2], axis=0) for half in range(2)]
    left_share = jnp.concatenate(left, axis=1)
    pack_gram(
        precise(left_share, left_share, ((0,), (0,))) * (1.0 / (terms * n)),
        [jnp.sum(weight * half, axis=0, keepdims=True) for half in left],
        left_gram[0],
    )
    left_steps = gram_steps(*left_gram)
    next(left_steps)

    def unpack(flow, block):
        at = pl.ds(pl.multiple_of(block * share + part(flow).start, part_rows), part_rows)
        value = decode(gathered[flow, block]) * row_turn[at, :]
        factor[at, lanes(flow)] = value.astype(jnp.bfloat16)

    def multiply(block, first_flow, flows, fresh):
        at = pl.ds(pl.multiple_of(block * share, share), share)
        cols = slice(first_flow * TILE, (first_flow + flows) * TILE)
        tall = docs // 2

        def rows_of(k, carry):
            rows = pl.ds(pl.multiple_of(k * tall, tall), tall)
            product = jnp.dot(
                turned[rows, at], factor[at, cols], preferred_element_type=jnp.float32
            )
            right_sum[rows, cols] = product if fresh else right_sum[rows, cols] + product
            return carry

        lax.fori_loop(0, 2, rows_of, 0)

    def source_of(flow, s1, s2):
        a, n1, b, n2 = axes(flow)
        return device(flow, lax.rem(a - s1 + n1, n1), lax.rem(b - s2 + n2, n2))

    for flow in range(4):
        unpack(flow, doc)
    multiply(doc, 0, 2, True)

    def landed_from(dx, dy, half):
        block = source_of(0, dx, dy)
        for flow in halves_of[half]:
            s1, s2 = step_of(flow, dx, dy)
            if s2:
                copies_d[flow, s1, s2].wait()
            unpack(flow, block)
        return block

    for flow in range(4):
        a, n1, b, n2 = axes(flow)
        for s1 in range(n1):
            if s1:
                copies_c[flow, s1].wait()
            source = source_of(flow, s1, 0)
            for s2 in range(1, n2):
                copies_d[flow, s1, s2] = remote(
                    gathered.at[flow, source],
                    gathered.at[flow, source],
                    sems[6].at[flow, s1 * n2 + s2],
                    sems[7].at[flow, s1 * n2 + s2],
                    "doc",
                    device(flow, a, lax.rem(b + s2, n2)),
                )
                copies_d[flow, s1, s2].start()
    next(left_steps)
    others = [step for step in reversed(steps) if step != (0, 0)]

    wide = 2 * piece
    sibling = 2 * z + 1 - c
    chunks = [lax.rem(z // 2 + 1 + j, nz // 2) for j in range(nz // 2)]

    def far_copy(half, step):
        there = lax.rem(z + step, nz)
        return remote(
            far_send.at[half, step],
            far_recv.at[half, step],
            sems[10].at[half, step],
            sems[11].at[half, step],
            "term",
            2 * there + c,
        )

    for half in range(2):
        for dx, dy in others:
            block = landed_from(dx, dy, half)
            if (dx, dy) != others[-1]:
                multiply(block, half, 1, False)
        cols = slice(half * TILE, (half + 1) * TILE)
        last_terms = pl.ds(pl.multiple_of(block * share, share), share)

        def right_product(chunk, core):
            at = pl.ds(pl.multiple_of(core * (docs // 2) + chunk * wide, wide), wide)
            product = jnp.dot(
                turned[at, last_terms], factor[last_terms, cols], preferred_element_type=jnp.float32
            )
            return (right_sum[at, cols] + product) * col_turn[at, :]

        near_copies = []
        for j, chunk in enumerate(chunks):
            near_send[half, j] = right_product(chunk, 1 - c)
            copy = remote(
                near_send.at[half, j],
                near_recv.at[half, j],
                sems[8].at[half, j],
                sems[9].at[half, j],
                "term",
                sibling,
            )
            copy.start()
            near_copies.append(copy)
        if half == 0:
            next(left_steps)
        for j, chunk in enumerate(chunks):
            product = right_product(chunk, c)
            near_copies[j].wait()
            near_recv[half, j] = near_recv[half, j] + product
            last = j + 1 == len(chunks)
            for k in range(2):
                if last and k:
                    continue
                inner = 1 - lax.rem(z, 2) if last else k
                step = lax.rem(2 * chunk + inner - z + nz, nz)
                at = pl.ds(pl.multiple_of(inner * piece, piece), piece)
                far_send[half, step] = encode(near_recv[half, j, at, :])
                far_copy(half, step).start()
    for _ in left_steps:
        pass
    unpack_gram(left_gram[1], gram)
    inverse_kernel(gram, inverse_ref, work)

    def split_inverse():
        whiten = inverse_ref[...].T
        high = whiten.astype(jnp.bfloat16)
        halves[0] = high
        halves[1] = (whiten - high.astype(jnp.float32)).astype(jnp.bfloat16)

    def finish_left(block):
        at = pl.ds(pl.multiple_of(block * share, share), share)
        value = jnp.concatenate(
            [
                jnp.concatenate([decode(gathered[flow, block]) for flow in flows], axis=0)
                for flows in halves_of
            ],
            axis=1,
        )
        left_out[at, :] = whitened(value, halves).astype(jnp.bfloat16)

    extra = left_gram[1].shape[1] - 1
    weighted = jnp.concatenate(
        [left_gram[1][1 + k, extra:, :] for k in range(width // TILE)], axis=1
    )
    lean = precise(jnp.broadcast_to(weighted, (8, width)), inverse_ref[...], ((1,), (1,)))[0:1]
    split_inverse()
    own_rows = pl.ds(pl.multiple_of(lax.rem(z, 2) * piece, piece), piece)
    totals = []
    for half in range(2):
        total = near_recv[half, len(chunks) - 1, own_rows, :]
        for step in range(1, nz):
            far_copy(half, step).wait()
            total = total + decode(far_recv[half, step])
        totals.append(total)
    total = jnp.concatenate(totals, axis=1)
    block = whitened(total, halves) - lean * (1.0 / docs_total)

    me = c * nz + z
    pack_gram(
        precise(block, block, ((0,), (0,))) * (1.0 / docs_total), [], right_gram[0]
    )
    right_steps = gram_steps(*right_gram)
    next(right_steps)
    right_parts[me] = encode(block)
    far_copies = []

    def send_part(step):
        copy = remote(
            right_parts.at[me],
            right_parts.at[me],
            sems[12].at[step],
            sems[13].at[step],
            "term",
            2 * lax.rem(z + step, nz) + c,
        )
        copy.start()
        far_copies.append(copy)

    send_part(1)
    copy = remote(
        right_parts.at[me], right_parts.at[me], sems[14].at[0], sems[15].at[0], "term", sibling
    )
    copy.start()
    near_copies = [copy]
    for k in range(m // 4):
        finish_left(k)
    next(right_steps)
    for k in range(m // 4, 3 * m // 4):
        finish_left(k)
    next(right_steps)
    for step in range(2, nz):
        send_part(step)
    for k in range(3 * m // 4, m):
        finish_left(k)
    for _ in right_steps:
        pass
    unpack_gram(right_gram[1], gram)
    def pass_on(left):
        if left:
            return
        for step in range(1, nz):
            far_copies[step - 1].wait()
            t = c * nz + lax.rem(z - step + nz, nz)
            copy = remote(
                right_parts.at[t],
                right_parts.at[t],
                sems[14].at[step],
                sems[15].at[step],
                "term",
                sibling,
            )
            copy.start()
            near_copies.append(copy)

    inverse_kernel(gram, inverse_ref, work, pass_on)
    split_inverse()

    for copy in near_copies:
        copy.wait()


def emit_kernel(row_ref, col_ref, left_ref, parts_ref, halves, *rest):
    outs, right, sems = rest[:4], rest[4], rest[5]
    right_out = outs[3]
    copies = [
        pltpu.make_async_copy(source, target, sems.at[k])
        for k, (source, target) in enumerate(zip((left_ref, row_ref, col_ref), (outs[2], *outs[:2])))
    ]
    for copy in copies:
        copy.start()
    shares, piece = parts_ref.shape[0], right.shape[0] // parts_ref.shape[0]

    def copy_of(t):
        at = pl.ds(pl.multiple_of(t * piece, piece), piece)
        return pltpu.make_async_copy(right.at[at], right_out.at[at], sems.at[3 + t])

    for t in range(0, shares, 2):
        value = jnp.concatenate([decode(parts_ref[t]), decode(parts_ref[t + 1])], axis=0)
        right[t * piece : (t + 2) * piece, :] = whitened(value, halves).astype(jnp.bfloat16)
        for share in (t, t + 1):
            copy_of(share).start()
            copies.append(copy_of(share))
    for copy in copies:
        copy.wait()


def emit(row, col, left, parts, halves, docs):
    width = left.shape[1]
    hbm = pl.BlockSpec(memory_space=pl.ANY)
    right = jax.ShapeDtypeStruct((docs, width), left.dtype)
    return pl.pallas_call(
        emit_kernel,
        out_shape=[jax.ShapeDtypeStruct(x.shape, x.dtype) for x in (row, col, left)] + [right],
        in_specs=[VMEM] * 5,
        out_specs=[hbm] * 4,
        scratch_shapes=[
            pltpu.VMEM(right.shape, right.dtype),
            pltpu.SemaphoreType.DMA((3 + parts.shape[0],)),
        ],
        compiler_params=pltpu.CompilerParams(vmem_limit_bytes=6 << 20),
        name="emit",
    )(row, col, left, parts, halves)


def per_device(tile_values, tile_rows, tile_cols, tile_count, start_block):
    n, m = lax.axis_size("term"), lax.axis_size("doc")
    nz = n // 2
    terms, (docs, width) = RB * TILE, start_block.shape
    share, piece = terms // m, docs // n
    wide = max(grid_of(m))
    int16, f32, bf16 = jnp.int16, jnp.float32, jnp.bfloat16
    coded = pltpu.VMEM((4, m, share // 2 + 16, TILE), int16)
    coded_b = pltpu.VMEM((4, wide, share // 2 + 16, TILE), int16)
    far = pltpu.VMEM((2, nz, piece + 16, TILE), int16)
    near = pltpu.VMEM((2, nz // 2, 2 * piece, TILE), f32)
    pairs = [pltpu.SemaphoreType.DMA((4, size)) for size in (m, m, wide, wide, wide, wide, m, m)]
    pairs += [pltpu.SemaphoreType.DMA((2, nz))] * 4
    vector = jax.ShapeDtypeStruct((RB, TILE), f32)
    hbm = pl.BlockSpec(memory_space=pltpu.HBM)
    outs = pl.pallas_call(
        whole_kernel,
        out_shape=[
            vector,
            vector,
            jax.ShapeDtypeStruct((terms, width), bf16),
            jax.ShapeDtypeStruct((n, piece + 16, width), int16),
            jax.ShapeDtypeStruct((2, width, width), bf16),
        ],
        in_specs=[SMEM] + [hbm] * 4,
        out_specs=[VMEM] * 5,
        scratch_shapes=[
            pltpu.VMEM((terms, TILE), f32),
            pltpu.VMEM((docs, TILE), f32),
            pltpu.VMEM((docs, width), bf16),
            pltpu.VMEM((m, share, width), f32),
            coded,
            coded,
            coded_b,
            coded_b,
            coded,
            pltpu.VMEM((terms, width), bf16),
            pltpu.VMEM((docs, width), f32),
            near,
            near,
            far,
            far,
            pltpu.VMEM((width, width), f32),
            pltpu.VMEM((width, width), f32),
            pltpu.VMEM((width, 2 * width), f32),
        ]
        + gram_scratch()
        + gram_scratch()
        + scale_scratch(terms, docs, width, tile_values.shape[0], tile_values.dtype)
        + pairs
        + semaphores(*[nz] * 4),
        compiler_params=pltpu.CompilerParams(
            collective_id=0, has_side_effects=True, vmem_limit_bytes=44 << 20
        ),
        name="whole",
    )(
        tile_count,
        *(
            pltpu.with_memory_space_constraint(x, pltpu.HBM)
            for x in (tile_rows, tile_cols, tile_values, start_block)
        ),
    )
    row, col, left_basis, right_basis = emit(*outs, docs)
    return (row.reshape(-1), col.reshape(-1), left_basis, right_basis)


def solution(mesh):
    placed = (
        P("term", "doc", None),
        P("term", "doc"),
        P("term", "doc"),
        P("term", "doc"),
        P("doc", None),
    )
    return jax.shard_map(
        per_device,
        mesh=mesh,
        in_specs=placed,
        out_specs=(P("term"), P("doc"), P("term", None), P("doc", None)),
        check_vma=False,
    )
```
